32 devices in a mesh: row: 8 (over z, core), col: 4 (over y, x).
Axes of the slice: x: 2, y: 2, z: 4, core: 2. Of those that a mesh axis runs over, the one named last changes fastest.
Arguments:
- intensity: float32 [1024, 1024], P('row', 'col'), may hold values from 0 to 1
- start_block: float32 [16, 1024, 1024], P(None, 'row', 'col'), may hold values from -60 to 60
- old_direction: float32 [16, 1024, 1024], P(None, 'row', 'col'), may hold values from -60 to 60
Outputs:
- new_block: float32 [16, 1024, 1024], P(None, 'row', 'col')
- new_direction: float32 [16, 1024, 1024], P(None, 'row', 'col')
- ritz_values: float32 [16], replicated
The draws below stay inside these ranges and needn't reach their ends.
All inputs are finite; a program needn't handle non-finite values.
Results may differ from the reference program's by a relative error of at most 0.0003.
Values sent between devices are 32-bit elements; how exact they have to be, the bound alone decides.
No kernel may reach another device: no remote copies, remote signals or barrier semaphores. Data moves between devices by JAX's collectives and lax.ppermute only.
A program may use at most 128 MiB of HBM per device.

```python
import math
import jax
import jax.numpy as jnp
from jax import lax

K = 16
SWEEPS = 8
NR = 1024
NC = 1024


def start_envelope():
    row_part = jnp.arange(NR, dtype=jnp.float32) / NR
    col_part = jnp.arange(NC, dtype=jnp.float32) / NC
    return jnp.exp(math.log(10.0) * 0.5 * (row_part[:, None] + col_part[None, :]))


def block_draw(key, salt_value):
    subkey = jax.random.fold_in(key, salt_value)
    noise_field = jnp.clip(jax.random.normal(subkey, (K, NR, NC), jnp.float32), -5.0, 5.0)
    envelope = start_envelope()
    return noise_field * envelope[None]


def draw_start_block(key, part):
    return block_draw(key, 11)


def draw_old_direction(key, part):
    return block_draw(key, 23)


def steps_of(stream_key, shape, shards, smallest, top_value):
    def one(position, blocks):
        heights = jax.random.uniform(jax.random.fold_in(jax.random.fold_in(stream_key, 6), position), (blocks,), jnp.float32, smallest / len(shards), top_value / len(shards))
        return jnp.repeat(jnp.exp(heights), shape[position] // blocks).reshape((-1,) + (1,) * (len(shape) - position - 1))

    level = one(*shards[0])
    for cut in shards[1:]:
        level = level * one(*cut)
    return level


def setup_inputs(seed: int = 0) -> dict:
    key_list = jax.random.split(jax.random.key(seed), 4)
    intensity = jnp.clip(1.0 * jax.random.uniform(key_list[0], (NR, NC), jnp.float32) ** steps_of(key_list[0], (NR, NC), ((0, 8), (1, 4)), -0.2, 0.2), 0.0, 1.0)
    start_block = draw_start_block(jax.random.fold_in(key_list[3], 71), 0)
    old_direction = draw_old_direction(jax.random.fold_in(key_list[3], 71), 0)
    return dict(intensity=intensity, start_block=start_block, old_direction=old_direction)


beta_value = 4.0
spatial_rate = 0.25
shift_numerator = 16.0
ritz_offset = 1.5
highest = lax.Precision.HIGHEST

def offset_list():
    return [(row_step, col_step) for row_step in range(-2, 3) for col_step in range(-2, 3)]

def graph_weights(intensity):
    row_count, col_count = intensity.shape
    padded = jnp.pad(intensity, 2)
    inside = jnp.pad(jnp.ones((row_count, col_count), jnp.float32), 2)
    weights = []
    for row_step, col_step in offset_list():
        shifted = padded[2 + row_step:2 + row_step + row_count, 2 + col_step:2 + col_step + col_count]
        inside_part = inside[2 + row_step:2 + row_step + row_count, 2 + col_step:2 + col_step + col_count]
        contrast = intensity - shifted
        weights.append(inside_part * jnp.exp(-beta_value * contrast * contrast - spatial_rate * (row_step * row_step + col_step * col_step)))
    return weights

def apply_graph(weights, fields):
    row_count, col_count = (fields.shape[1], fields.shape[2])
    padded = jnp.pad(fields, ((0, 0), (2, 2), (2, 2)))
    result = jnp.zeros(fields.shape, fields.dtype)
    for weight_map, (row_step, col_step) in zip(weights, offset_list()):
        result = result + weight_map[None] * padded[:, 2 + row_step:2 + row_step + row_count, 2 + col_step:2 + col_step + col_count]
    return result

def cosine_forward(values):
    length = values.shape[-1]
    reordered = jnp.concatenate([values[..., ::2], values[..., 1::2][..., ::-1]], -1)
    spectrum = jnp.fft.fft(reordered, axis=-1)
    freq = jnp.arange(length, dtype=jnp.float32)
    rotation = jnp.exp(-1j * (math.pi / (2 * length)) * freq)
    norming = math.sqrt(2.0 / length) * jnp.where(freq == 0, math.sqrt(0.5), 1.0)
    return jnp.real(spectrum * rotation) * norming

def cosine_inverse(values):
    length = values.shape[-1]
    freq = jnp.arange(length, dtype=jnp.float32)
    norming = math.sqrt(2.0 / length) * jnp.where(freq == 0, math.sqrt(0.5), 1.0)
    scaled = values / norming
    mirrored = jnp.concatenate([jnp.zeros_like(scaled[..., :1]), scaled[..., :0:-1]], -1)
    rotation = jnp.exp(1j * (math.pi / (2 * length)) * freq)
    spectrum = rotation * (scaled - 1j * mirrored)
    reordered = jnp.real(jnp.fft.ifft(spectrum, axis=-1))
    half_len = length // 2
    even_part = reordered[..., :half_len]
    odd_part = reordered[..., half_len:][..., ::-1]
    return jnp.stack([even_part, odd_part], -1).reshape(values.shape)

def laplace_values(index, length):
    sine_part = jnp.sin(math.pi / (2 * length) * index)
    return 4.0 * sine_part * sine_part

def precondition(residual):
    row_count, col_count = (residual.shape[1], residual.shape[2])
    spectral_shift = shift_numerator / (row_count * col_count)
    spectrum = cosine_forward(residual)
    spectrum = cosine_forward(jnp.swapaxes(spectrum, 1, 2))
    divisor = laplace_values(jnp.arange(col_count, dtype=jnp.float32), col_count)[:, None] + laplace_values(jnp.arange(row_count, dtype=jnp.float32), row_count)[None, :] + spectral_shift
    solved = cosine_inverse(spectrum / divisor[None])
    return cosine_inverse(jnp.swapaxes(solved, 1, 2))

def rayleigh_ritz(big_a, big_b, pixel_total):
    basis_size = big_a.shape[0]
    fields = basis_size // 3
    scaling = 1.0 / jnp.sqrt(jnp.diagonal(big_b) + 1e-06)
    norm_a = scaling[:, None] * (0.5 * (big_a + big_a.T)) * scaling[None, :]
    norm_b = scaling[:, None] * (0.5 * (big_b + big_b.T)) * scaling[None, :]
    factor_low = jnp.linalg.cholesky(norm_b)
    left_solve = jax.scipy.linalg.solve_triangular(factor_low, norm_a, lower=True)
    reduced = jax.scipy.linalg.solve_triangular(factor_low, left_solve.T, lower=True).T
    reduced = 0.5 * (reduced + reduced.T) + ritz_offset * jnp.eye(basis_size, dtype=norm_a.dtype)
    basis_q = jnp.eye(basis_size, fields, dtype=norm_a.dtype)
    for sweep in range(SWEEPS):
        images_q = jnp.dot(reduced, basis_q, precision=highest)
        upper_u = jnp.linalg.cholesky(jnp.dot(images_q.T, images_q, precision=highest))
        basis_q = jax.scipy.linalg.solve_triangular(upper_u, images_q.T, lower=True).T
    ritz_values = lax.optimization_barrier(jnp.sum(basis_q * jnp.dot(reduced, basis_q, precision=highest), 0)) - ritz_offset
    coeffs = math.sqrt(pixel_total) * scaling[:, None] * jax.scipy.linalg.solve_triangular(factor_low.T, basis_q, lower=False)
    return (ritz_values, coeffs)

def reference(intensity, start_block, old_direction):
    weights = graph_weights(intensity)
    degree = weights[0]
    for weight_map in weights[1:]:
        degree = degree + weight_map
    graph_x = apply_graph(weights, start_block)
    graph_p = apply_graph(weights, old_direction)
    x_flat = start_block.reshape(K, -1)
    gx_flat = graph_x.reshape(K, -1)
    degree_flat = degree.reshape(1, -1)
    gram_x = jnp.dot(x_flat * degree_flat, x_flat.T, precision=highest)
    affinity_x = jnp.dot(x_flat, gx_flat.T, precision=highest)
    factor = jnp.linalg.cholesky(gram_x)
    rayleigh = jax.scipy.linalg.cho_solve((factor, True), affinity_x)
    residual = gx_flat - jnp.dot(rayleigh.T, x_flat * degree_flat, precision=highest)
    precond = precondition(residual.reshape(K, NR, NC))
    graph_h = apply_graph(weights, precond)
    basis_all = jnp.concatenate([x_flat, precond.reshape(K, -1), old_direction.reshape(K, -1)], 0)
    graph_all = jnp.concatenate([gx_flat, graph_h.reshape(K, -1), graph_p.reshape(K, -1)], 0)
    big_a = jnp.dot(basis_all, graph_all.T, precision=highest)
    big_b = jnp.dot(basis_all * degree_flat, basis_all.T, precision=highest)
    ritz_values, coeffs = rayleigh_ritz(big_a, big_b, NR * NC)
    new_block = jnp.dot(coeffs.T, basis_all, precision=highest).reshape(K, NR, NC)
    new_direction = jnp.dot(coeffs[K:].T, basis_all[K:], precision=highest).reshape(K, NR, NC)
    return (new_block, new_direction, ritz_values)
```

```python
import functools
import math

import jax
import jax.numpy as jnp
import numpy as np
from jax import lax
from jax.experimental import pallas as pl
from jax.experimental.pallas import tpu as pltpu
from jax.sharding import PartitionSpec as P

SWEEPS = 8
beta_value = 4.0
spatial_rate = 0.25
shift_numerator = 16.0
ritz_offset = 1.5
highest = lax.Precision.HIGHEST
f32 = jnp.float32
bf16 = jnp.bfloat16
BOTH = ("row", "col")
LANES = 128
OFFSETS = [(a, b) for a in range(-2, 3) for b in range(-2, 3)]
VMEM_BYTES = 50 * 2**20


def params():
    return pltpu.CompilerParams(vmem_limit_bytes=VMEM_BYTES)


def cost(flops, nbytes):
    return pl.CostEstimate(flops=int(flops), bytes_accessed=int(nbytes), transcendentals=0)


@functools.lru_cache(None)
def cosine_tables(length):
    k = np.arange(length)[:, None]
    n = np.arange(length)[None, :]
    table = np.cos(np.pi * ((2 * n + 1) * k % (4 * length)) / (2 * length)) * np.sqrt(2.0 / length)
    table[0] *= np.sqrt(0.5)
    high = table.astype(jnp.bfloat16)
    low = (table - high.astype(np.float64)).astype(jnp.bfloat16)
    return high, low


def ratio_sinh(a, b):
    return np.exp(a - b) * (1 - np.exp(-2 * a)) / (1 - np.exp(-2 * b))


@functools.lru_cache(None)
def row_tables(strips, depth, cols):
    rows = strips * depth
    lam = 4 * np.sin(np.pi * np.arange(cols) / (2 * cols)) ** 2
    mu = lam + shift_numerator / (rows * cols)
    excess = np.zeros((depth, cols))
    excess[0] = mu
    for r in range(1, depth):
        last = r == depth - 1
        prev = excess[r - 1]
        excess[r] = mu + prev / (1 + prev) - (1.0 if last else 0.0) + (0.0 if last else 0.0)
        if last:
            excess[r] = mu + prev / (1 + prev)
    eps = excess / (1 + excess)
    last_inv = 1.0 / (mu + eps[depth - 2])
    theta = 2 * np.arcsinh(np.sqrt(mu) / 2)
    levels = strips.bit_length() - 1
    gain, cross = [], []
    top = np.zeros((strips, levels, cols))
    bot = np.zeros((strips, levels, cols))
    for level in range(levels):
        m = 1 << level
        n = m * depth
        half = np.sinh(theta / 2)
        b = n * theta
        a = (n - 0.5) * theta
        end_end = np.exp(a - b) * (1 + np.exp(-2 * a)) / (1 - np.exp(-2 * b)) / (2 * half)
        first_last = 2 * np.cosh(theta / 2) * np.exp(-b) / (1 - np.exp(-2 * b)) / (2 * half)
        gain.append(1 / (1 + 2 * end_end))
        cross.append(first_last)
        rho = [ratio_sinh(p * depth * theta, b) for p in range(m + 1)]
        for s in range(strips):
            p = s % m
            if (s >> level) & 1:
                top[s, level], bot[s, level] = rho[m - p], rho[m - 1 - p]
            else:
                top[s, level], bot[s, level] = rho[p], rho[p + 1]
    cast = lambda x: np.asarray(x, np.float32)
    return cast(eps), cast(last_inv[None]), cast(gain), cast(cross), cast(top), cast(bot)


def split(x):
    high = x.astype(bf16)
    return high, (x - high.astype(f32)).astype(bf16)


def weights_kernel(index_ref, image_ref, w_ref, deg_ref):
    depth, cols = deg_ref.shape
    total_rows = index_ref[1]
    center = image_ref[2 : 2 + depth, :]
    row = lax.broadcasted_iota(jnp.int32, (depth, cols), 0) + index_ref[0] * depth
    col = lax.broadcasted_iota(jnp.int32, (depth, cols), 1)
    degree = jnp.zeros((depth, cols), f32)
    for b in range(-2, 3):
        moved = pltpu.roll(center, b % cols, 1) if b else center
        col_ok = (col - b >= 0) & (col - b < cols)
        total = None
        for a in range(-2, 3):
            if a == 0 and b == 0:
                weight = jnp.ones((depth, cols), f32)
            else:
                contrast = moved - image_ref[2 + a : 2 + a + depth, :]
                ok = col_ok & (row + a >= 0) & (row + a < total_rows)
                weight = jnp.where(
                    ok,
                    jnp.exp(-beta_value * contrast * contrast - spatial_rate * (a * a + b * b)),
                    0.0,
                )
            w_ref[OFFSETS.index((a, b))] = weight
            total = weight if total is None else total + weight
        degree = degree + (pltpu.roll(total, (-b) % cols, 1) if b else total)
    deg_ref[...] = degree


def make_weights(strip_index, image, depth, total_rows):
    cols = image.shape[1]
    index = jnp.stack([strip_index, jnp.int32(total_rows)]).astype(jnp.int32)
    return pl.pallas_call(
        weights_kernel,
        out_shape=(
            jax.ShapeDtypeStruct((25, depth, cols), f32),
            jax.ShapeDtypeStruct((depth, cols), f32),
        ),
        in_specs=[
            pl.BlockSpec(memory_space=pltpu.SMEM),
            pl.BlockSpec(memory_space=pltpu.VMEM),
        ],
        out_specs=(pl.BlockSpec(memory_space=pltpu.VMEM),) * 2,
        compiler_params=params(),
        cost_estimate=cost(60 * depth * cols * 25, 25 * depth * cols * 4),
        name="weights",
    )(index, image)


def graph_kernel(order, keep, lane_shift, v_ref, top_ref, bot_ref, w_ref, deg_ref, *rest):
    others, rest = rest[: len(order) - 1], rest[len(order) - 1 :]
    if keep:
        g_ref, gram_ref, pad_ref, acc_ref = rest
    else:
        gram_ref, pad_ref, acc_ref = rest
    chunks, depth, fields, width = v_ref.shape
    cols = chunks * width
    for c in range(chunks):
        lanes = slice(c * width, (c + 1) * width)
        pad_ref[0:2, :, lanes] = top_ref[c]
        pad_ref[2 : 2 + depth, :, lanes] = v_ref[c]
        pad_ref[2 + depth : 4 + depth, :, lanes] = bot_ref[c]
    parts = len(order)

    def one_row(r, acc):
        result = None
        for b in range(-2, 3):
            total = None
            for a in range(-2, 3):
                value = pad_ref[r + 2 + a]
                if a or b:
                    value = w_ref[OFFSETS.index((a, b)), pl.ds(r, 1), :] * value
                total = value if total is None else total + value
            if b:
                total = pltpu.roll(total, (-b) % cols, 1)
            result = total if result is None else result + total
        if keep:
            g_ref[r] = result
        own = pad_ref[r + 2]
        weighted = deg_ref[pl.ds(r, 1), :] * own
        left, position = [], 0
        for which in order:
            if which == "v":
                left.append(split(own))
            else:
                ref = others[position]
                position += 1
                left.append(split(jnp.concatenate([ref[c, r] for c in range(chunks)], 1)))
        left = jnp.concatenate([p[0] for p in left] + [p[1] for p in left], 0)
        graph_pair, degree_pair = split(result), split(weighted)
        right = jnp.concatenate(
            [graph_pair[0], degree_pair[0], graph_pair[1], degree_pair[1]], 0
        )
        return acc + lax.dot_general(
            left, right, (((1,), (1,)), ((), ())), preferred_element_type=f32
        )

    acc = lax.fori_loop(0, depth, one_row, jnp.zeros((2 * parts * fields, 4 * fields), f32))
    half = parts * fields
    acc_ref[...] = jnp.zeros(acc_ref.shape, f32)
    acc_ref[:, 0 : 4 * fields] = acc[:half] + acc[half:]
    both = acc_ref[...]
    both = both + pltpu.roll(both, LANES - 2 * fields, 1)
    lane = lax.broadcasted_iota(jnp.int32, both.shape, 1)
    both = jnp.where(lane < 2 * fields, both, 0.0)
    if lane_shift:
        both = pltpu.roll(both, lane_shift, 1)
    gram_ref[...] = both


def apply_graph(order, keep, lane_shift, v, top, bot, w, deg, *others):
    chunks, depth, fields, width = v.shape
    cols = chunks * width
    parts = len(order)
    out_shape = (jax.ShapeDtypeStruct((parts * fields, LANES), f32),)
    if keep:
        out_shape = (jax.ShapeDtypeStruct((depth, fields, cols), f32),) + out_shape
    return pl.pallas_call(
        functools.partial(graph_kernel, order, keep, lane_shift),
        out_shape=out_shape,
        in_specs=[pl.BlockSpec(memory_space=pltpu.VMEM)] * (5 + len(others)),
        out_specs=(pl.BlockSpec(memory_space=pltpu.VMEM),) * len(out_shape),
        scratch_shapes=[
            pltpu.VMEM((depth + 4, fields, cols), f32),
            pltpu.VMEM((parts * fields, LANES), f32),
        ],
        compiler_params=params(),
        cost_estimate=cost(50 * fields * depth * cols * 4, 4 * cols * depth * (25 + 3 * fields)),
        name="graph_" + "".join(order),
    )(v, top, bot, w, deg, *others)


def forward_kernel(scaled, x_ref, *rest):
    if scaled:
        deg_ref, high_ref, low_ref, out_ref = rest
        chunks, depth, fields, width = x_ref.shape
    else:
        high_ref, low_ref, out_ref = rest
        depth, fields, _ = x_ref.shape
    cols = high_ref.shape[0]
    block = 8
    contract = (((1,), (1,)), ((), ()))

    def one_block(i, _):
        start = i * block
        if scaled:
            value = jnp.concatenate([x_ref[c, pl.ds(start, block)] for c in range(chunks)], 2)
            value = value * deg_ref[pl.ds(start, block), :][:, None, :]
        else:
            value = x_ref[pl.ds(start, block)]
        high, low = split(value.reshape(block * fields, cols))
        result = lax.dot_general(high, high_ref[...], contract, preferred_element_type=f32)
        result += lax.dot_general(high, low_ref[...], contract, preferred_element_type=f32)
        result += lax.dot_general(low, high_ref[...], contract, preferred_element_type=f32)
        out_ref[pl.ds(start, block)] = result.reshape(block, fields, cols)
        return 0

    lax.fori_loop(0, depth // block, one_block, 0)


def cosine_forward(x, deg, high, low, depth, fields):
    cols = high.shape[0]
    args = (x,) + ((deg,) if deg is not None else ()) + (high, low)
    return pl.pallas_call(
        functools.partial(forward_kernel, deg is not None),
        out_shape=jax.ShapeDtypeStruct((depth, fields, cols), f32),
        in_specs=[pl.BlockSpec(memory_space=pltpu.VMEM)] * len(args),
        out_specs=pl.BlockSpec(memory_space=pltpu.VMEM),
        compiler_params=params(),
        cost_estimate=cost(6 * depth * fields * cols * cols, 4 * cols * (2 * depth * fields + cols)),
        name="cosine_forward",
    )(*args)


def solve_kernel(gram_ref, fg_ref, fd_ref, eps_ref, last_ref, f_ref, ends_ref):
    depth, fields, cols = fg_ref.shape
    gram = gram_ref[...]
    affinity = pltpu.roll(gram, LANES - 4 * fields, 1)[:, :fields]
    mass = pltpu.roll(gram, LANES - 5 * fields, 1)[:, :fields]
    row = lax.broadcasted_iota(jnp.int32, (fields, fields), 0)
    for k in range(fields):
        inverse = 1.0 / mass[k : k + 1, k : k + 1]
        column = mass[:, k : k + 1]
        mass_row = mass[k : k + 1, :] * inverse
        affinity_row = affinity[k : k + 1, :] * inverse
        affinity = jnp.where(row == k, affinity_row, affinity - column * affinity_row)
        mass = jnp.where(row == k, mass_row, mass - column * mass_row)
    rayleigh_t = affinity.T

    def one_row(r, carry):
        value = fg_ref[r] - jnp.dot(
            rayleigh_t, fd_ref[r], precision=highest, preferred_element_type=f32
        )
        f_ref[r] = value
        keep = eps_ref[pl.ds(jnp.maximum(r - 1, 0), 1), :]
        return value + (carry - keep * carry)

    down = lax.fori_loop(0, depth, one_row, jnp.zeros((fields, cols), f32))

    def back_row(i, carry):
        r = depth - 1 - i
        keep = eps_ref[pl.ds(jnp.maximum(i - 1, 0), 1), :]
        return f_ref[r] + (carry - keep * carry)

    up = lax.fori_loop(0, depth, back_row, jnp.zeros((fields, cols), f32))
    last = last_ref[...]
    ends_ref[0] = up * last
    ends_ref[1] = down * last


def row_solve(gram, fg, fd, eps, last):
    depth, fields, cols = fg.shape
    return pl.pallas_call(
        solve_kernel,
        out_shape=(
            jax.ShapeDtypeStruct((depth, fields, cols), f32),
            jax.ShapeDtypeStruct((2, fields, cols), f32),
        ),
        in_specs=[pl.BlockSpec(memory_space=pltpu.VMEM)] * 5,
        out_specs=(pl.BlockSpec(memory_space=pltpu.VMEM),) * 2,
        compiler_params=params(),
        cost_estimate=cost(200 * depth * fields * cols, 4 * 3 * depth * fields * cols),
        name="row_solve",
    )(gram, fg, fd, eps, last)


def inverse_kernel(levels, *refs):
    g_refs = refs[:levels]
    f_ref, top_ref, bot_ref, eps_ref, last_ref, high_ref, low_ref, out_ref, u_ref = refs[levels:]
    depth, fields, cols = f_ref.shape
    chunks, _, _, width = out_ref.shape
    flux_top = jnp.zeros((fields, cols), f32)
    flux_bot = jnp.zeros((fields, cols), f32)
    for level in range(levels):
        g = g_refs[level][...]
        flux_top = flux_top + g * top_ref[level : level + 1, :]
        flux_bot = flux_bot - g * bot_ref[level : level + 1, :]

    u_ref[0] = f_ref[0] + flux_top

    def down_row(r, carry):
        keep = eps_ref[pl.ds(r - 1, 1), :]
        value = f_ref[r] + (carry - keep * carry)
        u_ref[r] = value
        return value

    value = lax.fori_loop(1, depth, down_row, u_ref[0])
    value = (value + flux_bot) * last_ref[...]
    u_ref[depth - 1] = value

    def up_row(i, carry):
        r = depth - 2 - i
        keep = eps_ref[pl.ds(r, 1), :]
        total = u_ref[r] + carry
        total = total - keep * total
        u_ref[r] = total
        return total

    lax.fori_loop(0, depth - 1, up_row, value)
    block = 8

    def one_block(i, _):
        start = i * block
        high, low = split(u_ref[pl.ds(start, block)].reshape(block * fields, cols))
        result = jnp.dot(high, high_ref[...], preferred_element_type=f32)
        result += jnp.dot(high, low_ref[...], preferred_element_type=f32)
        result += jnp.dot(low, high_ref[...], preferred_element_type=f32)
        result = result.reshape(block, fields, cols)
        for c in range(chunks):
            out_ref[c, pl.ds(start, block)] = result[:, :, c * width : (c + 1) * width]
        return 0

    lax.fori_loop(0, depth // block, one_block, 0)


def row_inverse(gs, f, top, bot, eps, last, high, low, chunks):
    depth, fields, cols = f.shape
    return pl.pallas_call(
        functools.partial(inverse_kernel, len(gs)),
        out_shape=jax.ShapeDtypeStruct((chunks, depth, fields, cols // chunks), f32),
        in_specs=[pl.BlockSpec(memory_space=pltpu.VMEM)] * (len(gs) + 7),
        out_specs=pl.BlockSpec(memory_space=pltpu.VMEM),
        scratch_shapes=[pltpu.VMEM((depth, fields, cols), f32)],
        compiler_params=params(),
        cost_estimate=cost(6 * depth * fields * cols * cols, 4 * cols * (2 * depth * fields + cols)),
        name="row_inverse",
    )(*gs, f, top, bot, eps, last, high, low)


def hdot(a, b, contract):
    return lax.dot_general(
        a, b, ((contract[0], contract[1]), ((), ())), precision=highest, preferred_element_type=f32
    )


def cholesky_apply(matrix, target):
    size = matrix.shape[0]
    step = 8
    mats = [matrix[i : i + step] for i in range(0, size, step)]
    tars = [target[i : i + step] for i in range(0, size, step)]
    local_row = lax.broadcasted_iota(jnp.int32, (step, 1), 0)
    for k in range(size):
        own, inner = divmod(k, step)
        pivot_row = mats[own][inner : inner + 1, :]
        target_row = tars[own][inner : inner + 1, :]
        inverse = 1.0 / pivot_row[:, k : k + 1]
        for i in range(own, size // step):
            factor = mats[i][:, k : k + 1] * inverse
            if i == own:
                factor = jnp.where(local_row > inner, factor, 0.0)
            mats[i] = mats[i] - factor * pivot_row
            tars[i] = tars[i] - factor * target_row
    matrix = jnp.concatenate(mats, 0)
    target = jnp.concatenate(tars, 0)
    row = lax.broadcasted_iota(jnp.int32, matrix.shape, 0)
    col = lax.broadcasted_iota(jnp.int32, matrix.shape, 1)
    pivots = jnp.sum(jnp.where(row == col, matrix, 0.0), 1, keepdims=True)
    return target * (1.0 / jnp.sqrt(pivots))


def ritz_kernel(fields, pixel_total, first_ref, second_ref, ritz_ref, coeff_ref):
    size = 3 * fields
    gram = second_ref[...]
    first = first_ref[...]
    row = lax.broadcasted_iota(jnp.int32, (LANES, size), 0)
    col = lax.broadcasted_iota(jnp.int32, (LANES, size), 1)
    place_a = jnp.zeros((LANES, size), jnp.bool_)
    place_b = jnp.zeros((LANES, size), jnp.bool_)
    for group, target in ((4, 0), (0, 1), (2, 2)):
        inside = (col >= target * fields) & (col < (target + 1) * fields)
        place_a = place_a | (inside & (row - group * fields == col - target * fields))
        place_b = place_b | (inside & (row - (group + 1) * fields == col - target * fields))
    place_a = place_a.astype(f32)
    place_b = place_b.astype(f32)
    srow = lax.broadcasted_iota(jnp.int32, (size, size), 0)
    scol = lax.broadcasted_iota(jnp.int32, (size, size), 1)
    same = srow // fields == scol // fields
    eye = (srow == scol).astype(f32)

    def assemble(place):
        part = hdot(gram, place, ((1,), (0,)))
        top = hdot(first, place, ((1,), (0,)))
        part = jnp.concatenate([part[:fields] + top, part[fields:]], 0)
        both = part + part.T
        return jnp.where(same, 0.5 * both, both)

    big_a = assemble(place_a)
    big_b = assemble(place_b)
    diagonal = big_b * eye
    scale_col = 1.0 / jnp.sqrt(jnp.sum(diagonal, 1, keepdims=True) + 1e-6)
    scale_row = 1.0 / jnp.sqrt(jnp.sum(diagonal, 0, keepdims=True) + 1e-6)
    norm_a = scale_col * big_a * scale_row
    norm_b = scale_col * big_b * scale_row
    inverse = cholesky_apply(norm_b, eye)
    reduced = hdot(hdot(inverse, norm_a, ((1,), (0,))), inverse, ((1,), (1,)))
    reduced = 0.5 * (reduced + reduced.T) + ritz_offset * eye
    power = hdot(reduced, reduced, ((1,), (0,)))
    power = hdot(power, power, ((1,), (0,)))
    images = power[:fields]
    basis = cholesky_apply(hdot(images, images, ((1,), (1,))), images)
    images = hdot(basis, power, ((1,), (0,)))
    basis = cholesky_apply(hdot(images, images, ((1,), (1,))), images)
    basis = cholesky_apply(hdot(basis, basis, ((1,), (1,))), basis)
    images = hdot(basis, reduced, ((1,), (0,)))
    ritz = jnp.sum(basis * images, 1, keepdims=True) - ritz_offset
    ritz_ref[...] = jnp.broadcast_to(ritz, ritz_ref.shape)
    coeff_ref[...] = math.sqrt(pixel_total) * hdot(basis, inverse, ((1,), (0,))) * scale_row


def ritz_step(first, second, fields, pixel_total):
    return pl.pallas_call(
        functools.partial(ritz_kernel, fields, pixel_total),
        out_shape=(
            jax.ShapeDtypeStruct((fields, LANES), f32),
            jax.ShapeDtypeStruct((fields, 3 * fields), f32),
        ),
        in_specs=[pl.BlockSpec(memory_space=pltpu.VMEM)] * 2,
        out_specs=(pl.BlockSpec(memory_space=pltpu.VMEM),) * 2,
        compiler_params=params(),
        cost_estimate=cost(1 << 25, 1 << 16),
        name="ritz",
    )(first, second)


def combine_kernel(coeff_ref, x_ref, h_ref, p_ref, block_ref, direction_ref):
    rows, fields, _ = x_ref.shape
    high, low = split(coeff_ref[...])
    left = jnp.concatenate([high, high, low], 1)

    def one_row(r, _):
        h_high, h_low = split(h_ref[r])
        p_high, p_low = split(p_ref[r])
        x_high, x_low = split(x_ref[r])
        right = jnp.concatenate(
            [x_high, h_high, p_high, x_low, h_low, p_low, x_high, h_high, p_high], 0
        )
        result = jnp.dot(left, right, preferred_element_type=f32)
        block_ref[r] = result[:fields]
        direction_ref[r] = result[fields:]
        return 0

    lax.fori_loop(0, rows, one_row, 0)


def combine(coeffs, x, h, p):
    rows, fields, width = x.shape
    zero = jnp.zeros((fields, fields), f32)
    both = jnp.concatenate([coeffs, jnp.concatenate([zero, coeffs[:, fields:]], 1)], 0)
    tile = 32
    spec = pl.BlockSpec((tile, fields, width), lambda i: (i, 0, 0))
    return pl.pallas_call(
        combine_kernel,
        grid=(rows // tile,),
        out_shape=(jax.ShapeDtypeStruct((rows, fields, width), f32),) * 2,
        in_specs=[pl.BlockSpec(both.shape, lambda i: (0, 0)), spec, spec, spec],
        out_specs=(spec, spec),
        compiler_params=params(),
        cost_estimate=cost(200 * rows * fields * width, 20 * rows * fields * width),
        name="combine",
    )(both, x, h, p)


def shifted(block, strips):
    down = [(i, i + 1) for i in range(strips - 1)]
    up = [(i + 1, i) for i in range(strips - 1)]
    return down, up


def local(intensity, start_block, old_direction):
    fields, height, width = start_block.shape
    chunks = lax.axis_size("col")
    strips = lax.axis_size("row") * chunks
    depth = height // chunks
    rows, cols = strips * depth, chunks * width
    strip = lax.axis_index("row") * chunks + lax.axis_index("col")
    down, up = shifted(None, strips)
    levels = strips.bit_length() - 1

    eps, last, gain, cross, top_all, bot_all = (
        jnp.asarray(t) for t in row_tables(strips, depth, cols)
    )
    high, low = (jnp.asarray(t) for t in cosine_tables(cols))
    top_mine = lax.dynamic_index_in_dim(top_all, strip, 0, False)
    bot_mine = lax.dynamic_index_in_dim(bot_all, strip, 0, False)

    def to_strips(block):
        return lax.all_to_all(block, "col", 0, 0)

    def total(value):
        for level in range(levels):
            value = value + lax.ppermute(value, BOTH, [(i, i ^ (1 << level)) for i in range(strips)])
        return value

    def halo(block):
        above = lax.ppermute(block[:, depth - 2 :], BOTH, down)
        below = lax.ppermute(block[:, :2], BOTH, up)
        return above, below

    x_rows = jnp.transpose(start_block.reshape(fields, chunks, depth, width), (1, 2, 0, 3))
    p_rows = jnp.transpose(old_direction.reshape(fields, chunks, depth, width), (1, 2, 0, 3))
    image = to_strips(intensity.reshape(chunks, depth, width))
    x_strip = to_strips(x_rows)
    p_strip = to_strips(p_rows)

    image = jnp.transpose(image, (1, 0, 2)).reshape(depth, cols)
    image = jnp.concatenate(
        [lax.ppermute(image[-2:], BOTH, down), image, lax.ppermute(image[:2], BOTH, up)], 0
    )
    w, deg = make_weights(strip, image, depth, rows)

    graph_x, gram_x = apply_graph(("v",), True, 4 * fields, x_strip, *halo(x_strip), w, deg)
    gram_x = total(gram_x)
    spectrum_g = cosine_forward(graph_x, None, high, low, depth, fields)
    spectrum_d = cosine_forward(x_strip, deg, high, low, depth, fields)
    (gram_p,) = apply_graph(
        ("x", "v"), False, 2 * fields, p_strip, *halo(p_strip), w, deg, x_strip
    )
    f, ends = row_solve(gram_x, spectrum_g, spectrum_d, eps, last)

    gs = []
    for level in range(levels):
        theirs = lax.ppermute(ends, BOTH, [(i, i ^ (1 << level)) for i in range(strips)])
        right = ((strip >> level) & 1) == 1
        lower = jnp.where(right, theirs, ends)
        upper = jnp.where(right, ends, theirs)
        g = (lower[1] - upper[0]) * gain[level]
        gs.append(g)
        ends = jnp.stack([lower[0] - g * cross[level], upper[1] + g * cross[level]])

    h_strip = row_inverse(gs, f, top_mine, bot_mine, eps, last, high, low, chunks)
    (gram_h,) = apply_graph(
        ("x", "v", "p"), False, 0, h_strip, *halo(h_strip), w, deg, x_strip, p_strip
    )
    h_block = lax.all_to_all(h_strip, "col", 0, 0).reshape(height, fields, width)
    zero = jnp.zeros((fields, LANES), f32)
    gram = gram_h + jnp.concatenate([gram_p[:fields], zero, gram_p[fields:]], 0)
    ritz, coeffs = ritz_step(gram_x, total(gram), fields, rows * cols)
    new_block, new_direction = combine(
        coeffs,
        x_rows.reshape(height, fields, width),
        h_block,
        p_rows.reshape(height, fields, width),
    )
    return (
        jnp.transpose(new_block, (1, 0, 2)),
        jnp.transpose(new_direction, (1, 0, 2)),
        ritz[:, 0],
    )


def solution(mesh):
    return jax.shard_map(
        local,
        mesh=mesh,
        in_specs=(P("row", "col"), P(None, "row", "col"), P(None, "row", "col")),
        out_specs=(P(None, "row", "col"), P(None, "row", "col"), P()),
        check_vma=False,
    )
```

```python
import functools
import math

import jax
import jax.numpy as jnp
import numpy as np
from jax import lax
from jax.experimental import pallas as pl
from jax.experimental.pallas import tpu as pltpu
from jax.sharding import PartitionSpec as P

SWEEPS = 8
beta_value = 4.0
spatial_rate = 0.25
shift_numerator = 16.0
ritz_offset = 1.5
highest = lax.Precision.HIGHEST
f32 = jnp.float32
bf16 = jnp.bfloat16
BOTH = ("row", "col")
LANES = 128
UNROLL = 4
OFFSETS = [(a, b) for a in range(-2, 3) for b in range(-2, 3)]


def params(*arrays, extra=4 * 2**20):
    total = extra
    for a in arrays:
        shape = (1, 1) + tuple(a.shape)
        padded = math.prod(shape[:-2]) * (-(-shape[-2] // 8) * 8) * (-(-shape[-1] // LANES) * LANES)
        total += padded * a.dtype.itemsize
    return pltpu.CompilerParams(vmem_limit_bytes=total)


def room(*shape):
    return jax.ShapeDtypeStruct(shape, f32)


def cost(flops, nbytes):
    return pl.CostEstimate(flops=int(flops), bytes_accessed=int(nbytes), transcendentals=0)


@functools.lru_cache(None)
def cosine_tables(length):
    k = np.arange(length)[:, None]
    n = np.arange(length)[None, :]
    table = np.cos(np.pi * ((2 * n + 1) * k % (4 * length)) / (2 * length)) * np.sqrt(2.0 / length)
    table[0] *= np.sqrt(0.5)
    high = table.astype(jnp.bfloat16)
    low = (table - high.astype(np.float64)).astype(jnp.bfloat16)
    return high, low


def ratio_sinh(a, b):
    return np.exp(a - b) * (1 - np.exp(-2 * a)) / (1 - np.exp(-2 * b))


@functools.lru_cache(None)
def row_tables(strips, depth, cols):
    rows = strips * depth
    lam = 4 * np.sin(np.pi * np.arange(cols) / (2 * cols)) ** 2
    mu = lam + shift_numerator / (rows * cols)
    excess = np.zeros((depth, cols))
    excess[0] = mu
    for r in range(1, depth):
        last = r == depth - 1
        prev = excess[r - 1]
        excess[r] = mu + prev / (1 + prev) - (1.0 if last else 0.0) + (0.0 if last else 0.0)
        if last:
            excess[r] = mu + prev / (1 + prev)
    eps = excess / (1 + excess)
    last_inv = 1.0 / (mu + eps[depth - 2])
    theta = 2 * np.arcsinh(np.sqrt(mu) / 2)
    levels = strips.bit_length() - 1
    gain, cross = [], []
    top = np.zeros((strips, levels, cols))
    bot = np.zeros((strips, levels, cols))
    for level in range(levels):
        m = 1 << level
        n = m * depth
        half = np.sinh(theta / 2)
        b = n * theta
        a = (n - 0.5) * theta
        end_end = np.exp(a - b) * (1 + np.exp(-2 * a)) / (1 - np.exp(-2 * b)) / (2 * half)
        first_last = 2 * np.cosh(theta / 2) * np.exp(-b) / (1 - np.exp(-2 * b)) / (2 * half)
        gain.append(1 / (1 + 2 * end_end))
        cross.append(first_last)
        rho = [ratio_sinh(p * depth * theta, b) for p in range(m + 1)]
        for s in range(strips):
            p = s % m
            if (s >> level) & 1:
                top[s, level], bot[s, level] = rho[m - p], rho[m - 1 - p]
            else:
                top[s, level], bot[s, level] = rho[p], rho[p + 1]
    cast = lambda x: np.asarray(x, np.float32)
    return cast(eps), cast(last_inv[None]), cast(gain), cast(cross), cast(top), cast(bot)


def split(x):
    high = x.astype(bf16)
    return high, (x - high.astype(f32)).astype(bf16)


def split3(x):
    high = x.astype(bf16)
    rest = x - high.astype(f32)
    middle = rest.astype(bf16)
    return high, middle, (rest - middle.astype(f32)).astype(bf16)


def weights_kernel(index_ref, image_ref, w_ref, deg_ref):
    depth, cols = deg_ref.shape
    total_rows = index_ref[1]
    center = image_ref[2 : 2 + depth, :]
    row = lax.broadcasted_iota(jnp.int32, (depth, cols), 0) + index_ref[0] * depth
    col = lax.broadcasted_iota(jnp.int32, (depth, cols), 1)
    degree = jnp.zeros((depth, cols), f32)
    for b in range(-2, 3):
        moved = pltpu.roll(center, b % cols, 1) if b else center
        col_ok = (col - b >= 0) & (col - b < cols)
        total = None
        for a in range(-2, 3):
            if a == 0 and b == 0:
                weight = jnp.ones((depth, cols), f32)
            else:
                contrast = moved - image_ref[2 + a : 2 + a + depth, :]
                ok = col_ok & (row + a >= 0) & (row + a < total_rows)
                weight = jnp.where(
                    ok,
                    jnp.exp(-beta_value * contrast * contrast - spatial_rate * (a * a + b * b)),
                    0.0,
                )
            w_ref[:, OFFSETS.index((a, b)), :] = weight
            total = weight if total is None else total + weight
        degree = degree + (pltpu.roll(total, (-b) % cols, 1) if b else total)
    deg_ref[...] = degree


def make_weights(strip_index, image, depth, total_rows):
    cols = image.shape[1]
    index = jnp.stack([strip_index, jnp.int32(total_rows)]).astype(jnp.int32)
    return pl.pallas_call(
        weights_kernel,
        out_shape=(
            jax.ShapeDtypeStruct((depth, 25, cols), f32),
            jax.ShapeDtypeStruct((depth, cols), f32),
        ),
        in_specs=[
            pl.BlockSpec(memory_space=pltpu.SMEM),
            pl.BlockSpec(memory_space=pltpu.VMEM),
        ],
        out_specs=(pl.BlockSpec(memory_space=pltpu.VMEM),) * 2,
        compiler_params=params(image, room(depth, 25, cols), extra=16 * 2**20),
        cost_estimate=cost(60 * depth * cols * 25, 25 * depth * cols * 4),
        name="weights",
    )(index, image)


def graph_kernel(order, keep, lane_shift, v_ref, top_ref, bot_ref, w_ref, deg_ref, *rest):
    others, rest = rest[: len(order) - 1], rest[len(order) - 1 :]
    if keep:
        g_ref, gram_ref, pad_ref, acc_ref, sum_ref = rest
    else:
        gram_ref, pad_ref, acc_ref, sum_ref = rest
    chunks, depth, fields, width = v_ref.shape
    cols = chunks * width
    for c in range(chunks):
        lanes = slice(c * width, (c + 1) * width)
        pad_ref[0:2, :, lanes] = top_ref[c]
        pad_ref[2 : 2 + depth, :, lanes] = v_ref[c]
        pad_ref[2 + depth : 4 + depth, :, lanes] = bot_ref[c]
    parts = len(order)
    groups = fields // 8

    def one_row(r, acc):
        for c in range(chunks):
            lanes = slice(c * width, (c + 1) * width)
            values = [pad_ref[r + a, :, lanes].reshape(groups, 8, width) for a in range(5)]
            for b in range(-2, 3):
                total = None
                for a in range(-2, 3):
                    value = values[a + 2]
                    if a or b:
                        o = OFFSETS.index((a, b))
                        weight = w_ref[r, o : o + 1, lanes]
                        value = weight[None] * value
                    total = value if total is None else total + value
                sum_ref[b + 2, :, lanes] = total.reshape(fields, width)
        result = sum_ref[2]
        for b in (-2, -1, 1, 2):
            result = result + pltpu.roll(sum_ref[b + 2], (-b) % cols, 1)
        if keep:
            g_ref[r] = result
        own = pad_ref[r + 2]
        weighted = deg_ref[pl.ds(r, 1), :] * own
        left, position = [], 0
        for which in order:
            if which == "v":
                left.append(split(own))
            else:
                ref = others[position]
                position += 1
                left.append(split(jnp.concatenate([ref[c, r] for c in range(chunks)], 1)))
        left = jnp.concatenate([p[0] for p in left] + [p[1] for p in left], 0)
        graph_pair, degree_pair = split(result), split(weighted)
        right = jnp.concatenate(
            [graph_pair[0], degree_pair[0], graph_pair[1], degree_pair[1]], 0
        )
        return acc + lax.dot_general(
            left, right, (((1,), (1,)), ((), ())), preferred_element_type=f32
        )

    start = jnp.zeros((2 * parts * fields, 4 * fields), f32)
    acc = lax.fori_loop(0, depth, one_row, start, unroll=UNROLL)
    half = parts * fields
    acc_ref[...] = jnp.zeros(acc_ref.shape, f32)
    acc_ref[:, 0 : 4 * fields] = acc[:half] + acc[half:]
    both = acc_ref[...]
    both = both + pltpu.roll(both, LANES - 2 * fields, 1)
    lane = lax.broadcasted_iota(jnp.int32, both.shape, 1)
    both = jnp.where(lane < 2 * fields, both, 0.0)
    if lane_shift:
        both = pltpu.roll(both, lane_shift, 1)
    gram_ref[...] = both


def apply_graph(order, keep, lane_shift, v, top, bot, w, deg, *others):
    chunks, depth, fields, width = v.shape
    cols = chunks * width
    parts = len(order)
    out_shape = (jax.ShapeDtypeStruct((parts * fields, LANES), f32),)
    if keep:
        out_shape = (jax.ShapeDtypeStruct((depth, fields, cols), f32),) + out_shape
    return pl.pallas_call(
        functools.partial(graph_kernel, order, keep, lane_shift),
        out_shape=out_shape,
        in_specs=[pl.BlockSpec(memory_space=pltpu.VMEM)] * (5 + len(others)),
        out_specs=(pl.BlockSpec(memory_space=pltpu.VMEM),) * len(out_shape),
        scratch_shapes=[
            pltpu.VMEM((depth + 4, fields, cols), f32),
            pltpu.VMEM((parts * fields, LANES), f32),
            pltpu.VMEM((5, fields, cols), f32),
        ],
        compiler_params=params(v, w, deg, *others, room(2 * depth + 10, fields, cols)),
        cost_estimate=cost(50 * fields * depth * cols * 4, 4 * cols * depth * (25 + 3 * fields)),
        name="graph_" + "".join(order),
    )(v, top, bot, w, deg, *others)


def forward_kernel(scaled, x_ref, *rest):
    if scaled:
        deg_ref, high_ref, low_ref, out_ref = rest
        chunks, depth, fields, width = x_ref.shape
    else:
        high_ref, low_ref, out_ref = rest
        depth, fields, _ = x_ref.shape
    cols = high_ref.shape[0]
    block = math.gcd(depth, 16)
    contract = (((1,), (0,)), ((), ()))

    def one_block(i, _):
        start = i * block
        if scaled:
            value = jnp.concatenate([x_ref[c, pl.ds(start, block)] for c in range(chunks)], 2)
            value = value * deg_ref[pl.ds(start, block), :][:, None, :]
        else:
            value = x_ref[pl.ds(start, block)]
        high, low = split(value.reshape(block * fields, cols))
        result = lax.dot_general(high, high_ref[...], contract, preferred_element_type=f32)
        result += lax.dot_general(high, low_ref[...], contract, preferred_element_type=f32)
        result += lax.dot_general(low, high_ref[...], contract, preferred_element_type=f32)
        out_ref[pl.ds(start, block)] = result.reshape(block, fields, cols)
        return 0

    lax.fori_loop(0, depth // block, one_block, 0)


def cosine_forward(x, deg, high, low, depth, fields):
    cols = high.shape[0]
    args = (x,) + ((deg,) if deg is not None else ()) + (high, low)
    return pl.pallas_call(
        functools.partial(forward_kernel, deg is not None),
        out_shape=jax.ShapeDtypeStruct((depth, fields, cols), f32),
        in_specs=[pl.BlockSpec(memory_space=pltpu.VMEM)] * len(args),
        out_specs=pl.BlockSpec(memory_space=pltpu.VMEM),
        compiler_params=params(*args, room(depth, fields, cols), extra=12 * 2**20),
        cost_estimate=cost(6 * depth * fields * cols * cols, 4 * cols * (2 * depth * fields + cols)),
        name="cosine_forward",
    )(*args)


def solve_kernel(gram_ref, fg_ref, fd_ref, eps_ref, last_ref, f_ref, ends_ref):
    depth, fields, cols = fg_ref.shape
    gram = gram_ref[...]
    affinity = pltpu.roll(gram, LANES - 4 * fields, 1)[:, :fields]
    mass = pltpu.roll(gram, LANES - 5 * fields, 1)[:, :fields]
    row = lax.broadcasted_iota(jnp.int32, (fields, fields), 0)
    for k in range(fields):
        inverse = 1.0 / mass[k : k + 1, k : k + 1]
        column = mass[:, k : k + 1]
        mass_row = mass[k : k + 1, :] * inverse
        affinity_row = affinity[k : k + 1, :] * inverse
        affinity = jnp.where(row == k, affinity_row, affinity - column * affinity_row)
        mass = jnp.where(row == k, mass_row, mass - column * mass_row)
    ray = split3(affinity.T)
    left = jnp.concatenate([ray[i] for i in (0, 0, 0, 1, 1, 2)], 1)

    def one_row(r, carry):
        piece = split3(fd_ref[r])
        right = jnp.concatenate([piece[i] for i in (0, 1, 2, 0, 1, 0)], 0)
        value = fg_ref[r] - jnp.dot(left, right, preferred_element_type=f32)
        f_ref[r] = value
        keep = eps_ref[pl.ds(jnp.maximum(r - 1, 0), 1), :]
        return value + (carry - keep * carry)

    down = lax.fori_loop(0, depth, one_row, jnp.zeros((fields, cols), f32), unroll=UNROLL)

    def back_row(i, carry):
        r = depth - 1 - i
        keep = eps_ref[pl.ds(jnp.maximum(i - 1, 0), 1), :]
        return f_ref[r] + (carry - keep * carry)

    up = lax.fori_loop(0, depth, back_row, jnp.zeros((fields, cols), f32), unroll=UNROLL)
    last = last_ref[...]
    ends_ref[0] = up * last
    ends_ref[1] = down * last


def row_solve(gram, fg, fd, eps, last):
    depth, fields, cols = fg.shape
    return pl.pallas_call(
        solve_kernel,
        out_shape=(
            jax.ShapeDtypeStruct((depth, fields, cols), f32),
            jax.ShapeDtypeStruct((2, fields, cols), f32),
        ),
        in_specs=[pl.BlockSpec(memory_space=pltpu.VMEM)] * 5,
        out_specs=(pl.BlockSpec(memory_space=pltpu.VMEM),) * 2,
        compiler_params=params(fg, fd, eps, room(depth, fields, cols)),
        cost_estimate=cost(200 * depth * fields * cols, 4 * 3 * depth * fields * cols),
        name="row_solve",
    )(gram, fg, fd, eps, last)


def inverse_kernel(levels, *refs):
    g_refs = refs[:levels]
    f_ref, top_ref, bot_ref, eps_ref, last_ref, high_ref, low_ref, out_ref, u_ref = refs[levels:]
    depth, fields, cols = f_ref.shape
    chunks, _, _, width = out_ref.shape
    flux_top = jnp.zeros((fields, cols), f32)
    flux_bot = jnp.zeros((fields, cols), f32)
    for level in range(levels):
        g = g_refs[level][...]
        flux_top = flux_top + g * top_ref[level : level + 1, :]
        flux_bot = flux_bot - g * bot_ref[level : level + 1, :]

    u_ref[0] = f_ref[0] + flux_top

    def down_row(r, carry):
        keep = eps_ref[pl.ds(r - 1, 1), :]
        value = f_ref[r] + (carry - keep * carry)
        u_ref[r] = value
        return value

    value = lax.fori_loop(1, depth, down_row, u_ref[0])
    value = (value + flux_bot) * last_ref[...]
    u_ref[depth - 1] = value

    def up_row(i, carry):
        r = depth - 2 - i
        keep = eps_ref[pl.ds(r, 1), :]
        total = u_ref[r] + carry
        total = total - keep * total
        u_ref[r] = total
        return total

    lax.fori_loop(0, depth - 1, up_row, value)
    block = 8

    def one_block(i, _):
        start = i * block
        high, low = split(u_ref[pl.ds(start, block)].reshape(block * fields, cols))
        result = jnp.dot(high, high_ref[...], preferred_element_type=f32)
        result += jnp.dot(high, low_ref[...], preferred_element_type=f32)
        result += jnp.dot(low, high_ref[...], preferred_element_type=f32)
        result = result.reshape(block, fields, cols)
        for c in range(chunks):
            out_ref[c, pl.ds(start, block)] = result[:, :, c * width : (c + 1) * width]
        return 0

    lax.fori_loop(0, depth // block, one_block, 0)


def row_inverse(gs, f, top, bot, eps, last, high, low, chunks):
    depth, fields, cols = f.shape
    return pl.pallas_call(
        functools.partial(inverse_kernel, len(gs)),
        out_shape=jax.ShapeDtypeStruct((chunks, depth, fields, cols // chunks), f32),
        in_specs=[pl.BlockSpec(memory_space=pltpu.VMEM)] * (len(gs) + 7),
        out_specs=pl.BlockSpec(memory_space=pltpu.VMEM),
        scratch_shapes=[pltpu.VMEM((depth, fields, cols), f32)],
        compiler_params=params(*gs, f, high, low, room(2 * depth, fields, cols), extra=12 * 2**20),
        cost_estimate=cost(6 * depth * fields * cols * cols, 4 * cols * (2 * depth * fields + cols)),
        name="row_inverse",
    )(*gs, f, top, bot, eps, last, high, low)


def hdot(a, b, contract):
    return lax.dot_general(
        a, b, ((contract[0], contract[1]), ((), ())), precision=highest, preferred_element_type=f32
    )


def cholesky_apply(matrix, target):
    size = matrix.shape[0]
    step = 8
    mats = [matrix[i : i + step] for i in range(0, size, step)]
    tars = [target[i : i + step] for i in range(0, size, step)]
    local_row = lax.broadcasted_iota(jnp.int32, (step, 1), 0)
    for k in range(size):
        own, inner = divmod(k, step)
        pivot_row = mats[own][inner : inner + 1, :]
        target_row = tars[own][inner : inner + 1, :]
        inverse = 1.0 / pivot_row[:, k : k + 1]
        for i in range(own, size // step):
            factor = mats[i][:, k : k + 1] * inverse
            if i == own:
                factor = jnp.where(local_row > inner, factor, 0.0)
            mats[i] = mats[i] - factor * pivot_row
            tars[i] = tars[i] - factor * target_row
    matrix = jnp.concatenate(mats, 0)
    target = jnp.concatenate(tars, 0)
    row = lax.broadcasted_iota(jnp.int32, matrix.shape, 0)
    col = lax.broadcasted_iota(jnp.int32, matrix.shape, 1)
    pivots = jnp.sum(jnp.where(row == col, matrix, 0.0), 1, keepdims=True)
    return target * (1.0 / jnp.sqrt(pivots))


def ritz_kernel(fields, pixel_total, first_ref, second_ref, ritz_ref, coeff_ref):
    size = 3 * fields
    gram = second_ref[...]
    first = first_ref[...]
    row = lax.broadcasted_iota(jnp.int32, (LANES, size), 0)
    col = lax.broadcasted_iota(jnp.int32, (LANES, size), 1)
    place_a = jnp.zeros((LANES, size), jnp.bool_)
    place_b = jnp.zeros((LANES, size), jnp.bool_)
    for group, target in ((4, 0), (0, 1), (2, 2)):
        inside = (col >= target * fields) & (col < (target + 1) * fields)
        place_a = place_a | (inside & (row - group * fields == col - target * fields))
        place_b = place_b | (inside & (row - (group + 1) * fields == col - target * fields))
    place_a = place_a.astype(f32)
    place_b = place_b.astype(f32)
    srow = lax.broadcasted_iota(jnp.int32, (size, size), 0)
    scol = lax.broadcasted_iota(jnp.int32, (size, size), 1)
    same = srow // fields == scol // fields
    eye = (srow == scol).astype(f32)

    def assemble(place):
        part = hdot(gram, place, ((1,), (0,)))
        top = hdot(first, place, ((1,), (0,)))
        part = jnp.concatenate([part[:fields] + top, part[fields:]], 0)
        both = part + part.T
        return jnp.where(same, 0.5 * both, both)

    big_a = assemble(place_a)
    big_b = assemble(place_b)
    diagonal = big_b * eye
    scale_col = 1.0 / jnp.sqrt(jnp.sum(diagonal, 1, keepdims=True) + 1e-6)
    scale_row = 1.0 / jnp.sqrt(jnp.sum(diagonal, 0, keepdims=True) + 1e-6)
    norm_a = scale_col * big_a * scale_row
    norm_b = scale_col * big_b * scale_row
    inverse = cholesky_apply(norm_b, eye)
    reduced = hdot(hdot(inverse, norm_a, ((1,), (0,))), inverse, ((1,), (1,)))
    reduced = 0.5 * (reduced + reduced.T) + ritz_offset * eye
    power = hdot(reduced, reduced, ((1,), (0,)))
    power = hdot(power, power, ((1,), (0,)))
    images = power[:fields]
    basis = cholesky_apply(hdot(images, images, ((1,), (1,))), images)
    images = hdot(basis, power, ((1,), (0,)))
    basis = cholesky_apply(hdot(images, images, ((1,), (1,))), images)
    basis = cholesky_apply(hdot(basis, basis, ((1,), (1,))), basis)
    images = hdot(basis, reduced, ((1,), (0,)))
    ritz = jnp.sum(basis * images, 1, keepdims=True) - ritz_offset
    ritz_ref[...] = jnp.broadcast_to(ritz, ritz_ref.shape)
    coeff_ref[...] = math.sqrt(pixel_total) * scale_col * hdot(inverse, basis, ((0,), (1,)))


def ritz_step(first, second, fields, pixel_total):
    return pl.pallas_call(
        functools.partial(ritz_kernel, fields, pixel_total),
        out_shape=(
            jax.ShapeDtypeStruct((fields, LANES), f32),
            jax.ShapeDtypeStruct((3 * fields, fields), f32),
        ),
        in_specs=[pl.BlockSpec(memory_space=pltpu.VMEM)] * 2,
        out_specs=(pl.BlockSpec(memory_space=pltpu.VMEM),) * 2,
        compiler_params=params(),
        cost_estimate=cost(1 << 25, 1 << 16),
        name="ritz",
    )(first, second)


def combine_kernel(tiles, coeff_ref, x_ref, h_ref, p_ref, block_ref, direction_ref, high_ref, low_ref):
    fields = x_ref.shape[0]
    width = x_ref.shape[2]
    group = 8 * fields

    @pl.when(pl.program_id(0) == 0)
    def _():
        r = lax.broadcasted_iota(jnp.int32, (group, fields), 0)
        c = lax.broadcasted_iota(jnp.int32, (group, fields), 1)
        rows_of = (r // 8 == c).astype(f32)
        f = lax.broadcasted_iota(jnp.int32, (fields, group), 0)
        q = lax.broadcasted_iota(jnp.int32, (fields, group), 1)
        row = lax.broadcasted_iota(jnp.int32, (group, group), 0)
        col = lax.broadcasted_iota(jnp.int32, (group, group), 1)
        coeffs = coeff_ref[...]
        for part in range(3):
            own = coeffs[part * fields : (part + 1) * fields, :].T
            if part == 1:
                cols_of, same = q % fields == f, row % 8 == col // fields
            else:
                cols_of, same = q // 8 == f, row % 8 == col % 8
            wide = hdot(own, cols_of.astype(f32), ((1,), (0,)))
            wide = jnp.where(same, hdot(rows_of, wide, ((1,), (0,))), 0.0)
            lanes = slice(part * group, (part + 1) * group)
            high_ref[:, lanes], low_ref[:, lanes] = split(wide)

    dot = functools.partial(jnp.dot, preferred_element_type=f32)
    for t in range(tiles):
        rows = slice(8 * t, 8 * t + 8)
        x = split(x_ref[:, rows, :].reshape(group, width))
        h = split(h_ref[rows].reshape(group, width))
        p = split(p_ref[:, rows, :].reshape(group, width))
        hp = [jnp.concatenate([h[i], p[i]], 0) for i in range(2)]
        x_high, x_low = high_ref[:, :group], low_ref[:, :group]
        hp_high, hp_low = high_ref[:, group:], low_ref[:, group:]
        direction = dot(hp_high, hp[0]) + dot(hp_low, hp[0]) + dot(hp_high, hp[1])
        x_left = jnp.concatenate([x_high, x_high, x_low], 1)
        block = direction + dot(x_left, jnp.concatenate([x[0], x[1], x[0]], 0))
        block_ref[:, rows, :] = block.reshape(fields, 8, width)
        direction_ref[:, rows, :] = direction.reshape(fields, 8, width)


def combine(coeffs, x, h, p):
    fields, rows, width = x.shape
    tile = 32
    spec = pl.BlockSpec((fields, tile, width), lambda i: (0, i, 0))
    h_spec = pl.BlockSpec((tile, fields, width), lambda i: (i, 0, 0))
    return pl.pallas_call(
        functools.partial(combine_kernel, tile // 8),
        grid=(rows // tile,),
        out_shape=(jax.ShapeDtypeStruct((fields, rows, width), f32),) * 2,
        in_specs=[pl.BlockSpec(coeffs.shape, lambda i: (0, 0)), spec, h_spec, spec],
        out_specs=(spec, spec),
        scratch_shapes=[pltpu.VMEM((8 * fields, 24 * fields), bf16)] * 2,
        compiler_params=params(room(12 * tile, fields, width)),
        cost_estimate=cost(200 * rows * fields * width, 20 * rows * fields * width),
        name="combine",
    )(coeffs, x, h, p)


def shifted(block, strips):
    down = [(i, i + 1) for i in range(strips - 1)]
    up = [(i + 1, i) for i in range(strips - 1)]
    return down, up


def local(intensity, start_block, old_direction):
    fields, height, width = start_block.shape
    chunks = lax.axis_size("col")
    strips = lax.axis_size("row") * chunks
    depth = height // chunks
    rows, cols = strips * depth, chunks * width
    strip = lax.axis_index("row") * chunks + lax.axis_index("col")
    down, up = shifted(None, strips)
    levels = strips.bit_length() - 1

    eps, last, gain, cross, top_all, bot_all = (
        jnp.asarray(t) for t in row_tables(strips, depth, cols)
    )
    high, low = (jnp.asarray(t) for t in cosine_tables(cols))
    high_t, low_t = (jnp.asarray(t.T.copy()) for t in cosine_tables(cols))
    top_mine = lax.dynamic_index_in_dim(top_all, strip, 0, False)
    bot_mine = lax.dynamic_index_in_dim(bot_all, strip, 0, False)

    def to_strips(block):
        return lax.all_to_all(block, "col", 0, 0)

    def total(value):
        first = chunks.bit_length() - 1
        for level in [*range(first, levels), *range(first)]:
            value = value + lax.ppermute(value, BOTH, [(i, i ^ (1 << level)) for i in range(strips)])
        return value

    def halo(block):
        above = lax.ppermute(block[:, depth - 2 :], BOTH, down)
        below = lax.ppermute(block[:, :2], BOTH, up)
        return above, below

    x_rows = jnp.transpose(start_block.reshape(fields, chunks, depth, width), (1, 2, 0, 3))
    p_rows = jnp.transpose(old_direction.reshape(fields, chunks, depth, width), (1, 2, 0, 3))
    image = to_strips(intensity.reshape(chunks, depth, width))
    x_strip = to_strips(x_rows)

    image = jnp.transpose(image, (1, 0, 2)).reshape(depth, cols)
    image = jnp.concatenate(
        [lax.ppermute(image[-2:], BOTH, down), image, lax.ppermute(image[:2], BOTH, up)], 0
    )
    w, deg = make_weights(strip, image, depth, rows)

    x_strip, w, p_rows = lax.optimization_barrier((x_strip, w, p_rows))
    x_halo = halo(x_strip)
    p_rows, x_halo = lax.optimization_barrier((p_rows, x_halo))
    p_strip = to_strips(p_rows)
    graph_x, gram_x = apply_graph(("v",), True, 4 * fields, x_strip, *x_halo, w, deg)
    gram_x = total(gram_x)
    spectrum_g = cosine_forward(graph_x, None, high_t, low_t, depth, fields)
    spectrum_d = cosine_forward(x_strip, deg, high_t, low_t, depth, fields)
    gram_x, p_strip = lax.optimization_barrier((gram_x, p_strip))
    f, ends = row_solve(gram_x, spectrum_g, spectrum_d, eps, last)
    (gram_p,) = apply_graph(
        ("x", "v"), False, 2 * fields, p_strip, *halo(p_strip), w, deg, x_strip
    )

    gs = []
    for level in range(levels):
        theirs = lax.ppermute(ends, BOTH, [(i, i ^ (1 << level)) for i in range(strips)])
        right = ((strip >> level) & 1) == 1
        lower = jnp.where(right, theirs, ends)
        upper = jnp.where(right, ends, theirs)
        g = (lower[1] - upper[0]) * gain[level]
        gs.append(g)
        ends = jnp.stack([lower[0] - g * cross[level], upper[1] + g * cross[level]])

    gs[-1], gram_p = lax.optimization_barrier((gs[-1], gram_p))
    h_strip = row_inverse(gs, f, top_mine, bot_mine, eps, last, high, low, chunks)
    h_halo = halo(h_strip)
    h_send, h_halo = lax.optimization_barrier((h_strip, h_halo))
    h_block = lax.all_to_all(h_send, "col", 0, 0).reshape(height, fields, width)
    (gram_h,) = apply_graph(
        ("x", "v", "p"), False, 0, h_strip, *h_halo, w, deg, x_strip, p_strip
    )
    zero = jnp.zeros((fields, LANES), f32)
    gram = gram_h + jnp.concatenate([gram_p[:fields], zero, gram_p[fields:]], 0)
    ritz, coeffs = ritz_step(gram_x, total(gram), fields, rows * cols)
    new_block, new_direction = combine(coeffs, start_block, h_block, old_direction)
    return new_block, new_direction, ritz[:, 0]


def solution(mesh):
    return jax.shard_map(
        local,
        mesh=mesh,
        in_specs=(P("row", "col"), P(None, "row", "col"), P(None, "row", "col")),
        out_specs=(P(None, "row", "col"), P(None, "row", "col"), P()),
        check_vma=False,
    )
```

```python
import functools
import math

import jax
import jax.numpy as jnp
import numpy as np
from jax import lax
from jax.experimental import pallas as pl
from jax.experimental.pallas import tpu as pltpu
from jax.sharding import PartitionSpec as P

SWEEPS = 8
beta_value = 4.0
spatial_rate = 0.25
shift_numerator = 16.0
ritz_offset = 1.5
highest = lax.Precision.HIGHEST
f32 = jnp.float32
bf16 = jnp.bfloat16
BOTH = ("row", "col")
LANES = 128
UNROLL = 4
VMEM = pl.BlockSpec(memory_space=pltpu.VMEM)
SMEM = pl.BlockSpec(memory_space=pltpu.SMEM)
OFFSETS = [(a, b) for a in range(-2, 3) for b in range(-2, 3)]


def params(*arrays, extra=4 * 2**20):
    total = extra
    for a in arrays:
        shape = (1, 1) + tuple(a.shape)
        padded = math.prod(shape[:-2]) * (-(-shape[-2] // 8) * 8) * (-(-shape[-1] // LANES) * LANES)
        total += padded * a.dtype.itemsize
    return pltpu.CompilerParams(vmem_limit_bytes=total)


def room(*shape):
    return jax.ShapeDtypeStruct(shape, f32)


def cost(flops, nbytes):
    return pl.CostEstimate(flops=int(flops), bytes_accessed=int(nbytes), transcendentals=0)


@functools.lru_cache(None)
def cosine_tables(length):
    k = np.arange(length)[:, None]
    n = np.arange(length)[None, :]
    table = np.cos(np.pi * ((2 * n + 1) * k % (4 * length)) / (2 * length)) * np.sqrt(2.0 / length)
    table[0] *= np.sqrt(0.5)
    high = table.astype(jnp.bfloat16)
    low = (table - high.astype(np.float64)).astype(jnp.bfloat16)
    return high, low


def ratio_sinh(a, b):
    return np.exp(a - b) * (1 - np.exp(-2 * a)) / (1 - np.exp(-2 * b))


@functools.lru_cache(None)
def row_tables(strips, depth, cols):
    rows = strips * depth
    lam = 4 * np.sin(np.pi * np.arange(cols) / (2 * cols)) ** 2
    mu = lam + shift_numerator / (rows * cols)
    excess = np.zeros((depth, cols))
    excess[0] = mu
    for r in range(1, depth):
        last = r == depth - 1
        prev = excess[r - 1]
        excess[r] = mu + prev / (1 + prev) - (1.0 if last else 0.0) + (0.0 if last else 0.0)
        if last:
            excess[r] = mu + prev / (1 + prev)
    eps = excess / (1 + excess)
    last_inv = 1.0 / (mu + eps[depth - 2])
    theta = 2 * np.arcsinh(np.sqrt(mu) / 2)
    levels = strips.bit_length() - 1
    gain, cross = [], []
    top = np.zeros((strips, levels, cols))
    bot = np.zeros((strips, levels, cols))
    for level in range(levels):
        m = 1 << level
        n = m * depth
        half = np.sinh(theta / 2)
        b = n * theta
        a = (n - 0.5) * theta
        end_end = np.exp(a - b) * (1 + np.exp(-2 * a)) / (1 - np.exp(-2 * b)) / (2 * half)
        first_last = 2 * np.cosh(theta / 2) * np.exp(-b) / (1 - np.exp(-2 * b)) / (2 * half)
        gain.append(1 / (1 + 2 * end_end))
        cross.append(first_last)
        rho = [ratio_sinh(p * depth * theta, b) for p in range(m + 1)]
        for s in range(strips):
            p = s % m
            if (s >> level) & 1:
                top[s, level], bot[s, level] = rho[m - p], rho[m - 1 - p]
            else:
                top[s, level], bot[s, level] = rho[p], rho[p + 1]
    cast = lambda x: np.asarray(x, np.float32)
    return cast(eps), cast(last_inv[None]), cast(gain), cast(cross), cast(top), cast(bot)


def split(x):
    high = x.astype(bf16)
    return high, (x - high.astype(f32)).astype(bf16)


def split3(x):
    high = x.astype(bf16)
    rest = x - high.astype(f32)
    middle = rest.astype(bf16)
    return high, middle, (rest - middle.astype(f32)).astype(bf16)


def image_rows(count, fields):
    return -(-count // fields)


def spread(info_ref, chunk_refs, target):
    width = chunk_refs[0].shape[-1]
    count = target.shape[0]
    for d, ref in enumerate(chunk_refs):
        start = pl.multiple_of(info_ref[1 + d] * width, width)
        if len(target.shape) == 3:
            target[:, :, pl.ds(start, width)] = ref[0:count]
        else:
            below = ref[ref.shape[0] - image_rows(count, ref.shape[1]) :]
            target[:, pl.ds(start, width)] = below.reshape(-1, width)[:count]


def edges_kernel(x_top, x_bot, p_top, p_bot, i_top, i_bot, head_ref, tail_ref):
    fields, _, _ = x_top.shape
    for out_ref, rows, refs in (
        (head_ref, slice(0, 2), (x_top, p_top, i_top)),
        (tail_ref, slice(6, 8), (x_bot, p_bot, i_bot)),
    ):
        for f in range(fields):
            out_ref[:, f, :] = refs[0][f, rows, :]
            out_ref[:, fields + f, :] = refs[1][f, rows, :]
        out_ref[:, 2 * fields, :] = refs[2][rows, :]


def edges(x, p, image):
    fields, height, width = x.shape
    bottom = height // 8 - 1
    top = pl.BlockSpec((fields, 8, width), lambda i: (0, 0, 0))
    bot = pl.BlockSpec((fields, 8, width), lambda i: (0, bottom, 0))
    image_top = pl.BlockSpec((8, width), lambda i: (0, 0))
    image_bot = pl.BlockSpec((8, width), lambda i: (bottom, 0))
    out = pl.BlockSpec((2, 2 * fields + 1, width), lambda i: (0, 0, 0))
    return pl.pallas_call(
        edges_kernel,
        grid=(1,),
        out_shape=(room(2, 2 * fields + 1, width),) * 2,
        in_specs=[top, bot, top, bot, image_top, image_bot],
        out_specs=(out, out),
        compiler_params=pltpu.CompilerParams(vmem_limit_bytes=56 * 2**20),
        cost_estimate=cost(0, 8 * 4 * fields * width * 4),
        name="edges",
    )(x, x, p, p, image, image)


def pack_kernel(chunks, depth, with_image, info_ref, x_ref, *refs):
    fields, height, width = x_ref.shape
    if with_image:
        image_ref, *pieces = refs
    else:
        pieces = refs
    for d in range(chunks):
        place = info_ref[1 + chunks + d]
        start = pl.multiple_of(place * depth, depth)
        before = pl.multiple_of(jnp.maximum(start - 8, 0), 8)
        after = pl.multiple_of(jnp.minimum(start + depth, height - 8), 8)
        piece = pieces[d]
        for f in range(fields):
            piece[2 : 2 + depth, f, :] = x_ref[f, pl.ds(start, depth), :]
            piece[0:2, f, :] = x_ref[f, pl.ds(before, 8), :][6:8]
            piece[2 + depth : 4 + depth, f, :] = x_ref[f, pl.ds(after, 8), :][0:2]
        if with_image:
            rows = jnp.concatenate(
                [
                    image_ref[pl.ds(before, 8), :][6:8],
                    image_ref[pl.ds(start, depth), :],
                    image_ref[pl.ds(after, 8), :][0:2],
                ],
                0,
            )
            count = depth + 4
            for r in range(0, count, fields):
                size = min(fields, count - r)
                piece[depth + 4 + r // fields, 0:size, :] = rows[r : r + size]
            rest = -count % fields
            if rest:
                piece[depth + 3 + image_rows(count, fields), fields - rest :, :] = jnp.zeros(
                    (rest, width), f32
                )


def pack(info, x, image, chunks):
    fields, height, width = x.shape
    depth = height // chunks
    count = depth + 4 + (image_rows(depth + 4, fields) if image is not None else 0)
    args = (x,) if image is None else (x, image)
    return pl.pallas_call(
        functools.partial(pack_kernel, chunks, depth, image is not None),
        out_shape=(room(count, fields, width),) * chunks,
        in_specs=[SMEM] + [VMEM] * len(args),
        out_specs=(VMEM,) * chunks,
        compiler_params=params(*args, *(room(count, fields, width),) * chunks),
        cost_estimate=cost(0, 8 * fields * height * width),
        name="pack",
    )(info, *args)


def fill_kernel(chunks, depth, first, with_image, info_ref, above_ref, below_ref, *refs):
    pieces = refs[chunks:]
    fields = pieces[0].shape[1]
    for d in range(chunks):
        place = info_ref[1 + chunks + d]
        piece = pieces[d]
        for which, rows_ref, row in ((0, above_ref, 0), (chunks - 1, below_ref, depth + 2)):

            @pl.when(place == which)
            def _(piece=piece, rows_ref=rows_ref, row=row):
                piece[row : row + 2] = rows_ref[:, first : first + fields, :]
                if with_image:
                    for i in range(2):
                        line = depth + 4 + (row + i) // fields
                        at = (row + i) % fields
                        image = rows_ref[i, 2 * fields : 2 * fields + 1, :]
                        piece[line, at : at + 1, :] = image


def fill(info, above, below, pieces, first, with_image):
    chunks = len(pieces)
    count, fields, width = pieces[0].shape
    depth = count - 4
    if with_image:
        depth = next(n for n in range(1, count) if n + 4 + image_rows(n + 4, fields) == count)
    return pl.pallas_call(
        functools.partial(fill_kernel, chunks, depth, first, with_image),
        out_shape=(room(count, fields, width),) * chunks,
        in_specs=[SMEM] + [VMEM] * (2 + chunks),
        out_specs=(VMEM,) * chunks,
        input_output_aliases={3 + d: d for d in range(chunks)},
        compiler_params=params(*pieces),
        cost_estimate=cost(0, 16 * fields * width),
        name="fill",
    )(info, above, below, *pieces)


def weights_kernel(chunks, total_rows, info_ref, *rest):
    chunk_refs, (w_ref, deg_ref, image_ref) = rest[:chunks], rest[chunks:]
    depth, cols = deg_ref.shape
    spread(info_ref, chunk_refs, image_ref)
    center = image_ref[2 : 2 + depth, :]
    row = lax.broadcasted_iota(jnp.int32, (depth, cols), 0) + info_ref[0] * depth
    col = lax.broadcasted_iota(jnp.int32, (depth, cols), 1)
    degree = jnp.zeros((depth, cols), f32)
    for b in range(-2, 3):
        moved = pltpu.roll(center, b % cols, 1) if b else center
        col_ok = (col - b >= 0) & (col - b < cols)
        total = None
        for a in range(-2, 3):
            if a == 0 and b == 0:
                weight = jnp.ones((depth, cols), f32)
            else:
                contrast = moved - image_ref[2 + a : 2 + a + depth, :]
                ok = col_ok & (row + a >= 0) & (row + a < total_rows)
                weight = jnp.where(
                    ok,
                    jnp.exp(-beta_value * contrast * contrast - spatial_rate * (a * a + b * b)),
                    0.0,
                )
            w_ref[:, OFFSETS.index((a, b)), :] = weight
            total = weight if total is None else total + weight
        degree = degree + (pltpu.roll(total, (-b) % cols, 1) if b else total)
    deg_ref[...] = degree


def make_weights(info, pieces, depth, total_rows):
    cols = pieces[0].shape[2] * len(pieces)
    return pl.pallas_call(
        functools.partial(weights_kernel, len(pieces), total_rows),
        out_shape=(room(depth, 25, cols), room(depth, cols)),
        in_specs=[SMEM] + [VMEM] * len(pieces),
        out_specs=(VMEM,) * 2,
        scratch_shapes=[pltpu.VMEM((depth + 4, cols), f32)],
        compiler_params=params(*pieces, room(depth, 25, cols), extra=16 * 2**20),
        cost_estimate=cost(60 * depth * cols * 25, 25 * depth * cols * 4),
        name="weights",
    )(info, *pieces)


def graph_kernel(order, keep, lane_shift, chunks, *refs):
    if chunks:
        info_ref, chunk_refs, refs = refs[0], refs[1 : 1 + chunks], refs[1 + chunks :]
    else:
        v_ref, top_ref, bot_ref, *refs = refs
    (w_ref, deg_ref), refs = refs[:2], refs[2:]
    others, refs = refs[: len(order) - 1], list(refs[len(order) - 1 :])
    g_ref = refs.pop(0) if keep else None
    own_ref = refs.pop(0) if chunks else None
    gram_ref, pad_ref, acc_ref, sum_ref = refs
    depth, cols = deg_ref.shape
    fields = pad_ref.shape[1]
    if chunks:
        spread(info_ref, chunk_refs, pad_ref)
    else:
        pad_ref[0:2] = top_ref[...]
        pad_ref[2 : 2 + depth] = v_ref[...]
        pad_ref[2 + depth : 4 + depth] = bot_ref[...]
    parts = len(order)
    groups = fields // 8
    width = 256

    def one_row(r, acc):
        for c in range(cols // width):
            lanes = slice(c * width, (c + 1) * width)
            values = [pad_ref[r + a, :, lanes].reshape(groups, 8, width) for a in range(5)]
            for b in range(-2, 3):
                total = None
                for a in range(-2, 3):
                    value = values[a + 2]
                    if a or b:
                        o = OFFSETS.index((a, b))
                        value = w_ref[r, o : o + 1, lanes][None] * value
                    total = value if total is None else total + value
                sum_ref[b + 2, :, lanes] = total.reshape(fields, width)
        result = sum_ref[2]
        for b in (-2, -1, 1, 2):
            result = result + pltpu.roll(sum_ref[b + 2], (-b) % cols, 1)
        if keep:
            g_ref[r] = result
        own = pad_ref[r + 2]
        if chunks:
            own_ref[r] = own
        weighted = deg_ref[pl.ds(r, 1), :] * own
        left, position = [], 0
        for which in order:
            if which == "v":
                left.append(split(own))
            else:
                left.append(split(others[position][r]))
                position += 1
        left = jnp.concatenate([p[0] for p in left] + [p[1] for p in left], 0)
        graph_pair, degree_pair = split(result), split(weighted)
        right = jnp.concatenate(
            [graph_pair[0], degree_pair[0], graph_pair[1], degree_pair[1]], 0
        )
        return acc + lax.dot_general(
            left, right, (((1,), (1,)), ((), ())), preferred_element_type=f32
        )

    start = jnp.zeros((2 * parts * fields, 4 * fields), f32)
    acc = lax.fori_loop(0, depth, one_row, start, unroll=UNROLL)
    half = parts * fields
    acc_ref[...] = jnp.zeros(acc_ref.shape, f32)
    acc_ref[:, 0 : 4 * fields] = acc[:half] + acc[half:]
    both = acc_ref[...]
    both = both + pltpu.roll(both, LANES - 2 * fields, 1)
    lane = lax.broadcasted_iota(jnp.int32, both.shape, 1)
    both = jnp.where(lane < 2 * fields, both, 0.0)
    if lane_shift:
        both = pltpu.roll(both, lane_shift, 1)
    gram_ref[...] = both


def apply_graph(order, keep, lane_shift, fields_in, w, deg, *others, info=None):
    depth, cols = deg.shape
    fields = fields_in[0].shape[1]
    parts = len(order)
    chunks = len(fields_in) if info is not None else 0
    out_shape = [room(depth, fields, cols)] * (int(keep) + int(chunks > 0))
    out_shape += [room(parts * fields, LANES)]
    args = ((info,) if chunks else ()) + tuple(fields_in) + (w, deg) + others
    return pl.pallas_call(
        functools.partial(graph_kernel, order, keep, lane_shift, chunks),
        out_shape=tuple(out_shape),
        in_specs=[SMEM] * int(chunks > 0) + [VMEM] * (len(args) - int(chunks > 0)),
        out_specs=(VMEM,) * len(out_shape),
        scratch_shapes=[
            pltpu.VMEM((depth + 4, fields, cols), f32),
            pltpu.VMEM((parts * fields, LANES), f32),
            pltpu.VMEM((5, fields, cols), f32),
        ],
        compiler_params=params(w, deg, *fields_in, *others, *out_shape, room(depth + 9, fields, cols)),
        cost_estimate=cost(50 * fields * depth * cols * 4, 4 * cols * depth * (25 + 3 * fields)),
        name="graph_" + "".join(order),
    )(*args)


def forward_kernel(scaled, x_ref, *rest):
    if scaled:
        deg_ref, high_ref, low_ref, out_ref = rest
    else:
        high_ref, low_ref, out_ref = rest
    depth, fields, _ = x_ref.shape
    cols = high_ref.shape[0]
    block = math.gcd(depth, 16)
    contract = (((1,), (0,)), ((), ()))

    def one_block(i, _):
        start = i * block
        value = x_ref[pl.ds(start, block)]
        if scaled:
            value = value * deg_ref[pl.ds(start, block), :][:, None, :]
        high, low = split(value.reshape(block * fields, cols))
        result = lax.dot_general(high, high_ref[...], contract, preferred_element_type=f32)
        result += lax.dot_general(high, low_ref[...], contract, preferred_element_type=f32)
        result += lax.dot_general(low, high_ref[...], contract, preferred_element_type=f32)
        out_ref[pl.ds(start, block)] = result.reshape(block, fields, cols)
        return 0

    lax.fori_loop(0, depth // block, one_block, 0)


def cosine_forward(x, deg, high, low, depth, fields):
    cols = high.shape[0]
    args = (x,) + ((deg,) if deg is not None else ()) + (high, low)
    return pl.pallas_call(
        functools.partial(forward_kernel, deg is not None),
        out_shape=jax.ShapeDtypeStruct((depth, fields, cols), f32),
        in_specs=[pl.BlockSpec(memory_space=pltpu.VMEM)] * len(args),
        out_specs=pl.BlockSpec(memory_space=pltpu.VMEM),
        compiler_params=params(*args, room(depth, fields, cols), extra=12 * 2**20),
        cost_estimate=cost(6 * depth * fields * cols * cols, 4 * cols * (2 * depth * fields + cols)),
        name="cosine_forward",
    )(*args)


def solve_kernel(gram_ref, fg_ref, fd_ref, eps_ref, last_ref, f_ref, ends_ref):
    depth, fields, cols = fg_ref.shape
    gram = gram_ref[...]
    affinity = pltpu.roll(gram, LANES - 4 * fields, 1)[:, :fields]
    mass = pltpu.roll(gram, LANES - 5 * fields, 1)[:, :fields]
    row = lax.broadcasted_iota(jnp.int32, (fields, fields), 0)
    for k in range(fields):
        inverse = 1.0 / mass[k : k + 1, k : k + 1]
        column = mass[:, k : k + 1]
        mass_row = mass[k : k + 1, :] * inverse
        affinity_row = affinity[k : k + 1, :] * inverse
        affinity = jnp.where(row == k, affinity_row, affinity - column * affinity_row)
        mass = jnp.where(row == k, mass_row, mass - column * mass_row)
    ray = split3(affinity.T)
    left = jnp.concatenate([ray[i] for i in (0, 0, 0, 1, 1, 2)], 1)

    def one_row(r, carry):
        piece = split3(fd_ref[r])
        right = jnp.concatenate([piece[i] for i in (0, 1, 2, 0, 1, 0)], 0)
        value = fg_ref[r] - jnp.dot(left, right, preferred_element_type=f32)
        f_ref[r] = value
        keep = eps_ref[pl.ds(jnp.maximum(r - 1, 0), 1), :]
        return value + (carry - keep * carry)

    down = lax.fori_loop(0, depth, one_row, jnp.zeros((fields, cols), f32), unroll=UNROLL)

    def back_row(i, carry):
        r = depth - 1 - i
        keep = eps_ref[pl.ds(jnp.maximum(i - 1, 0), 1), :]
        return f_ref[r] + (carry - keep * carry)

    up = lax.fori_loop(0, depth, back_row, jnp.zeros((fields, cols), f32), unroll=UNROLL)
    last = last_ref[...]
    ends_ref[0] = up * last
    ends_ref[1] = down * last


def row_solve(gram, fg, fd, eps, last):
    depth, fields, cols = fg.shape
    return pl.pallas_call(
        solve_kernel,
        out_shape=(
            jax.ShapeDtypeStruct((depth, fields, cols), f32),
            jax.ShapeDtypeStruct((2, fields, cols), f32),
        ),
        in_specs=[pl.BlockSpec(memory_space=pltpu.VMEM)] * 5,
        out_specs=(pl.BlockSpec(memory_space=pltpu.VMEM),) * 2,
        compiler_params=params(fg, fd, eps, room(depth, fields, cols)),
        cost_estimate=cost(200 * depth * fields * cols, 4 * 3 * depth * fields * cols),
        name="row_solve",
    )(gram, fg, fd, eps, last)


def merge_kernel(level, last, info_ref, mine_ref, theirs_ref, gain_ref, cross_ref, g_ref, *ends_ref):
    right = ((info_ref[0] >> level) & 1) == 1
    mine, theirs = mine_ref[...], theirs_ref[...]
    lower = jnp.where(right, theirs, mine)
    upper = jnp.where(right, mine, theirs)
    g = (lower[1] - upper[0]) * gain_ref[level : level + 1, :]
    g_ref[...] = g
    if not last:
        moved = g * cross_ref[level : level + 1, :]
        ends_ref[0][0] = lower[0] - moved
        ends_ref[0][1] = upper[1] + moved


def merge(level, last, info, mine, theirs, gain, cross):
    _, fields, cols = mine.shape
    out_shape = (room(fields, cols),) + (() if last else (room(2, fields, cols),))
    return pl.pallas_call(
        functools.partial(merge_kernel, level, last),
        out_shape=out_shape,
        in_specs=[SMEM] + [VMEM] * 4,
        out_specs=(VMEM,) * len(out_shape),
        compiler_params=params(),
        cost_estimate=cost(10 * fields * cols, 28 * fields * cols),
        name="merge",
    )(info, mine, theirs, gain, cross)


def inverse_kernel(levels, chunks, info_ref, *refs):
    g_refs = refs[:levels]
    f_ref, flux_ref, eps_ref, last_ref, high_ref, low_ref = refs[levels : levels + 6]
    out_ref, head_ref, tail_ref, *piece_refs, u_ref = refs[levels + 6 :]
    depth, fields, cols = f_ref.shape
    width = cols // chunks
    flux_top = jnp.zeros((fields, cols), f32)
    flux_bot = jnp.zeros((fields, cols), f32)
    for level in range(levels):
        g = g_refs[level][...]
        flux_top = flux_top + g * flux_ref[level : level + 1, :]
        flux_bot = flux_bot - g * flux_ref[levels + level : levels + level + 1, :]

    u_ref[0] = f_ref[0] + flux_top

    def down_row(r, carry):
        keep = eps_ref[pl.ds(r - 1, 1), :]
        value = f_ref[r] + (carry - keep * carry)
        u_ref[r] = value
        return value

    value = lax.fori_loop(1, depth, down_row, u_ref[0])
    value = (value + flux_bot) * last_ref[...]
    u_ref[depth - 1] = value

    def up_row(i, carry):
        r = depth - 2 - i
        keep = eps_ref[pl.ds(r, 1), :]
        total = u_ref[r] + carry
        total = total - keep * total
        u_ref[r] = total
        return total

    lax.fori_loop(0, depth - 1, up_row, value)
    block = 8

    def one_block(i, _):
        start = i * block
        high, low = split(u_ref[pl.ds(start, block)].reshape(block * fields, cols))
        result = jnp.dot(high, high_ref[...], preferred_element_type=f32)
        result += jnp.dot(high, low_ref[...], preferred_element_type=f32)
        result += jnp.dot(low, high_ref[...], preferred_element_type=f32)
        out_ref[pl.ds(start, block)] = result.reshape(block, fields, cols)
        for d in range(chunks):
            lane = pl.multiple_of(info_ref[1 + d] * width, width)
            piece_refs[d][pl.ds(start, block)] = out_ref[pl.ds(start, block), :, pl.ds(lane, width)]
        return 0

    lax.fori_loop(0, depth // block, one_block, 0)
    head_ref[...] = out_ref[0:2]
    tail_ref[...] = out_ref[depth - 2 : depth]


def row_inverse(info, gs, f, flux, eps, last, high, low, chunks):
    depth, fields, cols = f.shape
    out_shape = (room(depth, fields, cols),) + (room(2, fields, cols),) * 2
    out_shape += (room(depth, fields, cols // chunks),) * chunks
    return pl.pallas_call(
        functools.partial(inverse_kernel, len(gs), chunks),
        out_shape=out_shape,
        in_specs=[SMEM] + [VMEM] * (len(gs) + 6),
        out_specs=(VMEM,) * len(out_shape),
        scratch_shapes=[pltpu.VMEM((depth, fields, cols), f32)],
        compiler_params=params(*gs, f, high, low, *out_shape, f, extra=12 * 2**20),
        cost_estimate=cost(6 * depth * fields * cols * cols, 4 * cols * (2 * depth * fields + cols)),
        name="row_inverse",
    )(info, *gs, f, flux, eps, last, high, low)


def hdot(a, b, contract):
    return lax.dot_general(
        a, b, ((contract[0], contract[1]), ((), ())), precision=highest, preferred_element_type=f32
    )


def cholesky_apply(matrix, target):
    size = matrix.shape[0]
    step = 8
    mats = [matrix[i : i + step] for i in range(0, size, step)]
    tars = [target[i : i + step] for i in range(0, size, step)]
    local_row = lax.broadcasted_iota(jnp.int32, (step, 1), 0)
    for k in range(size):
        own, inner = divmod(k, step)
        pivot_row = mats[own][inner : inner + 1, :]
        target_row = tars[own][inner : inner + 1, :]
        inverse = 1.0 / pivot_row[:, k : k + 1]
        for i in range(own, size // step):
            factor = mats[i][:, k : k + 1] * inverse
            if i == own:
                factor = jnp.where(local_row > inner, factor, 0.0)
            mats[i] = mats[i] - factor * pivot_row
            tars[i] = tars[i] - factor * target_row
    matrix = jnp.concatenate(mats, 0)
    target = jnp.concatenate(tars, 0)
    row = lax.broadcasted_iota(jnp.int32, matrix.shape, 0)
    col = lax.broadcasted_iota(jnp.int32, matrix.shape, 1)
    pivots = jnp.sum(jnp.where(row == col, matrix, 0.0), 1, keepdims=True)
    return target * (1.0 / jnp.sqrt(pivots))


def ritz_kernel(fields, pixel_total, first_ref, second_ref, ritz_ref, coeff_ref):
    size = 3 * fields
    gram = second_ref[...]
    first = first_ref[...]
    row = lax.broadcasted_iota(jnp.int32, (LANES, size), 0)
    col = lax.broadcasted_iota(jnp.int32, (LANES, size), 1)
    place_a = jnp.zeros((LANES, size), jnp.bool_)
    place_b = jnp.zeros((LANES, size), jnp.bool_)
    for group, target in ((4, 0), (0, 1), (2, 2)):
        inside = (col >= target * fields) & (col < (target + 1) * fields)
        place_a = place_a | (inside & (row - group * fields == col - target * fields))
        place_b = place_b | (inside & (row - (group + 1) * fields == col - target * fields))
    place_a = place_a.astype(f32)
    place_b = place_b.astype(f32)
    srow = lax.broadcasted_iota(jnp.int32, (size, size), 0)
    scol = lax.broadcasted_iota(jnp.int32, (size, size), 1)
    same = srow // fields == scol // fields
    eye = (srow == scol).astype(f32)

    def assemble(place):
        part = hdot(gram, place, ((1,), (0,)))
        top = hdot(first, place, ((1,), (0,)))
        part = jnp.concatenate([part[:fields] + top, part[fields:]], 0)
        both = part + part.T
        return jnp.where(same, 0.5 * both, both)

    big_a = assemble(place_a)
    big_b = assemble(place_b)
    diagonal = big_b * eye
    scale_col = 1.0 / jnp.sqrt(jnp.sum(diagonal, 1, keepdims=True) + 1e-6)
    scale_row = 1.0 / jnp.sqrt(jnp.sum(diagonal, 0, keepdims=True) + 1e-6)
    norm_a = scale_col * big_a * scale_row
    norm_b = scale_col * big_b * scale_row
    inverse = cholesky_apply(norm_b, eye)
    reduced = hdot(hdot(inverse, norm_a, ((1,), (0,))), inverse, ((1,), (1,)))
    reduced = 0.5 * (reduced + reduced.T) + ritz_offset * eye
    power = hdot(reduced, reduced, ((1,), (0,)))
    power = hdot(power, power, ((1,), (0,)))
    images = power[:fields]
    basis = cholesky_apply(hdot(images, images, ((1,), (1,))), images)
    images = hdot(basis, power, ((1,), (0,)))
    basis = cholesky_apply(hdot(images, images, ((1,), (1,))), images)
    basis = cholesky_apply(hdot(basis, basis, ((1,), (1,))), basis)
    images = hdot(basis, reduced, ((1,), (0,)))
    ritz = jnp.sum(basis * images, 1, keepdims=True) - ritz_offset
    ritz_ref[...] = jnp.broadcast_to(ritz, ritz_ref.shape)
    coeff_ref[...] = math.sqrt(pixel_total) * scale_col * hdot(inverse, basis, ((0,), (1,)))


def ritz_step(first, second, fields, pixel_total):
    return pl.pallas_call(
        functools.partial(ritz_kernel, fields, pixel_total),
        out_shape=(
            jax.ShapeDtypeStruct((fields, LANES), f32),
            jax.ShapeDtypeStruct((3 * fields, fields), f32),
        ),
        in_specs=[pl.BlockSpec(memory_space=pltpu.VMEM)] * 2,
        out_specs=(pl.BlockSpec(memory_space=pltpu.VMEM),) * 2,
        compiler_params=params(),
        cost_estimate=cost(1 << 25, 1 << 16),
        name="ritz",
    )(first, second)


def combine_kernel(chunks, info_ref, coeff_ref, x_ref, p_ref, *refs):
    pieces, (block_ref, direction_ref, h_ref, high_ref, low_ref) = refs[:chunks], refs[chunks:]
    fields = x_ref.shape[0]
    width = x_ref.shape[2]
    group = 8 * fields

    @pl.when(pl.program_id(0) == 0)
    def _():
        r = lax.broadcasted_iota(jnp.int32, (group, fields), 0)
        c = lax.broadcasted_iota(jnp.int32, (group, fields), 1)
        rows_of = (r // 8 == c).astype(f32)
        f = lax.broadcasted_iota(jnp.int32, (fields, group), 0)
        q = lax.broadcasted_iota(jnp.int32, (fields, group), 1)
        row = lax.broadcasted_iota(jnp.int32, (group, group), 0)
        col = lax.broadcasted_iota(jnp.int32, (group, group), 1)
        coeffs = coeff_ref[...]
        for part in range(3):
            own = coeffs[part * fields : (part + 1) * fields, :].T
            if part == 1:
                cols_of, same = q % fields == f, row % 8 == col // fields
            else:
                cols_of, same = q // 8 == f, row % 8 == col % 8
            wide = hdot(own, cols_of.astype(f32), ((1,), (0,)))
            wide = jnp.where(same, hdot(rows_of, wide, ((1,), (0,))), 0.0)
            lanes = slice(part * group, (part + 1) * group)
            high_ref[:, lanes], low_ref[:, lanes] = split(wide)

    for d in range(chunks):

        @pl.when(pl.program_id(0) == d)
        def _(d=d):
            h_ref[...] = pieces[d][...]

    dot = functools.partial(jnp.dot, preferred_element_type=f32)
    for t in range(x_ref.shape[1] // 8):
        rows = slice(8 * t, 8 * t + 8)
        x = split(x_ref[:, rows, :].reshape(group, width))
        h = split(h_ref[rows].reshape(group, width))
        p = split(p_ref[:, rows, :].reshape(group, width))
        hp = [jnp.concatenate([h[i], p[i]], 0) for i in range(2)]
        x_high, x_low = high_ref[:, :group], low_ref[:, :group]
        hp_high, hp_low = high_ref[:, group:], low_ref[:, group:]
        direction = dot(hp_high, hp[0]) + dot(hp_low, hp[0]) + dot(hp_high, hp[1])
        x_left = jnp.concatenate([x_high, x_high, x_low], 1)
        block = direction + dot(x_left, jnp.concatenate([x[0], x[1], x[0]], 0))
        block_ref[:, rows, :] = block.reshape(fields, 8, width)
        direction_ref[:, rows, :] = direction.reshape(fields, 8, width)


def combine(info, coeffs, x, p, pieces):
    fields, rows, width = x.shape
    chunks = len(pieces)
    depth = rows // chunks
    spec = pl.BlockSpec((fields, depth, width), lambda i, s: (0, s[1 + chunks + i], 0))
    whole = pl.BlockSpec((depth, fields, width), lambda i, s: (0, 0, 0))
    return pl.pallas_call(
        functools.partial(combine_kernel, chunks),
        out_shape=(room(fields, rows, width),) * 2,
        grid_spec=pltpu.PrefetchScalarGridSpec(
            num_scalar_prefetch=1,
            grid=(chunks,),
            in_specs=[pl.BlockSpec(coeffs.shape, lambda i, s: (0, 0)), spec, spec] + [whole] * chunks,
            out_specs=(spec, spec),
            scratch_shapes=[pltpu.VMEM((depth, fields, width), f32)]
            + [pltpu.VMEM((8 * fields, 24 * fields), bf16)] * 2,
        ),
        compiler_params=params(room(16 * depth, fields, width)),
        cost_estimate=cost(200 * rows * fields * width, 20 * rows * fields * width),
        name="combine",
    )(info, coeffs, x, p, *pieces)


def ring_order(count):
    half = count // 2
    return [*range(half), *reversed(range(half, count))] if count > 1 else [0]


@functools.lru_cache(None)
def device_table(strips, chunks):
    order = ring_order(chunks)
    place = [order.index(c) for c in range(chunks)]
    table = []
    for device in range(strips):
        row, col = divmod(device, chunks)
        others = [col ^ d for d in range(chunks)]
        table.append([row * chunks + place[col], *others, *[place[c] for c in others]])
    return np.asarray(table, np.int32)


def local(intensity, start_block, old_direction):
    fields, height, width = start_block.shape
    chunks = lax.axis_size("col")
    row_count = lax.axis_size("row")
    strips = row_count * chunks
    depth = height // chunks
    rows, cols = strips * depth, chunks * width
    device = lax.axis_index("row") * chunks + lax.axis_index("col")
    levels = strips.bit_length() - 1
    order = ring_order(chunks)
    owner = [(s // chunks) * chunks + order[s % chunks] for s in range(strips)]

    table = device_table(strips, chunks)
    eps, last, gain, cross, top_all, bot_all = row_tables(strips, depth, cols)
    by_device = np.concatenate([top_all[table[:, 0]], bot_all[table[:, 0]]], 1)
    high, low = (jnp.asarray(t) for t in cosine_tables(cols))
    high_t, low_t = (jnp.asarray(t.T.copy()) for t in cosine_tables(cols))
    eps, last, gain, cross = (jnp.asarray(t) for t in (eps, last, gain, cross))
    info = lax.dynamic_index_in_dim(jnp.asarray(table), device, 0, False)
    flux = lax.dynamic_index_in_dim(jnp.asarray(by_device), device, 0, False)

    def total(value, tied=()):
        first = chunks.bit_length() - 1
        for level in [*range(first, levels), *range(first)]:
            if level == 0:
                value, tied = lax.optimization_barrier((value, tied))
            value = value + lax.ppermute(value, BOTH, [(i, i ^ (1 << level)) for i in range(strips)])
        return value, tied

    def exchange(pieces):
        return [pieces[0]] + [
            lax.ppermute(pieces[d], "col", [(c, c ^ d) for c in range(chunks)])
            for d in range(1, chunks)
        ]

    head, tail = edges(start_block, old_direction, intensity)
    above = lax.ppermute(tail, "row", [(i, i + 1) for i in range(row_count - 1)])
    below = lax.ppermute(head, "row", [(i + 1, i) for i in range(row_count - 1)])
    x_pieces = pack(info, start_block, intensity, chunks)
    x_pieces = exchange(fill(info, above, below, x_pieces, 0, True))
    p_pieces = pack(info, old_direction, None, chunks)
    p_pieces = exchange(fill(info, above, below, p_pieces, fields, False))
    x_pieces, flux = lax.optimization_barrier((x_pieces, flux))
    w, deg = make_weights(info, x_pieces, depth, rows)
    graph_x, x, gram_x = apply_graph(("v",), True, 4 * fields, x_pieces, w, deg, info=info)
    gram_x, p_pieces = total(gram_x, p_pieces)
    spectrum_g = cosine_forward(graph_x, None, high_t, low_t, depth, fields)
    spectrum_d = cosine_forward(x, deg, high_t, low_t, depth, fields)
    f, ends = row_solve(gram_x, spectrum_g, spectrum_d, eps, last)

    gs = []
    for level in range(levels):
        theirs = lax.ppermute(ends, BOTH, [(i, i ^ (1 << level)) for i in range(strips)])
        g, *ends = merge(level, level == levels - 1, info, ends, theirs, gain, cross)
        ends = ends[0] if ends else None
        gs.append(g)

    h, head, tail, *h_pieces = row_inverse(info, gs, f, flux, eps, last, high, low, chunks)
    h_above = lax.ppermute(tail, BOTH, [(owner[s], owner[s + 1]) for s in range(strips - 1)])
    h_below = lax.ppermute(head, BOTH, [(owner[s + 1], owner[s]) for s in range(strips - 1)])
    p_pieces, h = lax.optimization_barrier((p_pieces, h))
    p, gram_p = apply_graph(("x", "v"), False, 2 * fields, p_pieces, w, deg, x, info=info)
    h_pieces, h_above, h_below, gram_p = lax.optimization_barrier(
        (h_pieces, h_above, h_below, gram_p)
    )
    h_pieces = exchange(h_pieces)
    (gram_h,) = apply_graph(("x", "v", "p"), False, 0, (h, h_above, h_below), w, deg, x, p)
    zero = jnp.zeros((fields, LANES), f32)
    gram = gram_h + jnp.concatenate([gram_p[:fields], zero, gram_p[fields:]], 0)
    ritz, coeffs = ritz_step(gram_x, total(gram)[0], fields, rows * cols)
    new_block, new_direction = combine(info, coeffs, start_block, old_direction, h_pieces)
    return new_block, new_direction, ritz[:, 0]


def solution(mesh):
    return jax.shard_map(
        local,
        mesh=mesh,
        in_specs=(P("row", "col"), P(None, "row", "col"), P(None, "row", "col")),
        out_specs=(P(None, "row", "col"), P(None, "row", "col"), P()),
        check_vma=False,
    )
```

```python
import functools
import math

import jax
import jax.numpy as jnp
import numpy as np
from jax import lax
from jax.experimental import pallas as pl
from jax.experimental.pallas import tpu as pltpu
from jax.sharding import PartitionSpec as P

SWEEPS = 8
beta_value = 4.0
spatial_rate = 0.25
shift_numerator = 16.0
ritz_offset = 1.5
highest = lax.Precision.HIGHEST
f32 = jnp.float32
bf16 = jnp.bfloat16
BOTH = ("row", "col")
LANES = 128
UNROLL = 4
VMEM = pl.BlockSpec(memory_space=pltpu.VMEM)
SMEM = pl.BlockSpec(memory_space=pltpu.SMEM)
OFFSETS = [(a, b) for a in range(-2, 3) for b in range(-2, 3)]


def params(*arrays, extra=4 * 2**20):
    total = extra
    for a in arrays:
        shape = (1, 1) + tuple(a.shape)
        padded = math.prod(shape[:-2]) * (-(-shape[-2] // 8) * 8) * (-(-shape[-1] // LANES) * LANES)
        total += padded * a.dtype.itemsize
    return pltpu.CompilerParams(vmem_limit_bytes=total)


def room(*shape):
    return jax.ShapeDtypeStruct(shape, f32)


def cost(flops, nbytes):
    return pl.CostEstimate(flops=int(flops), bytes_accessed=int(nbytes), transcendentals=0)


@functools.lru_cache(None)
def cosine_tables(length):
    k = np.arange(length)[:, None]
    n = np.arange(length)[None, :]
    table = np.cos(np.pi * ((2 * n + 1) * k % (4 * length)) / (2 * length)) * np.sqrt(2.0 / length)
    table[0] *= np.sqrt(0.5)
    high = table.astype(jnp.bfloat16)
    low = (table - high.astype(np.float64)).astype(jnp.bfloat16)
    return high, low


def ratio_sinh(a, b):
    return np.exp(a - b) * (1 - np.exp(-2 * a)) / (1 - np.exp(-2 * b))


@functools.lru_cache(None)
def row_tables(strips, depth, cols):
    rows = strips * depth
    lam = 4 * np.sin(np.pi * np.arange(cols) / (2 * cols)) ** 2
    mu = lam + shift_numerator / (rows * cols)
    excess = np.zeros((depth, cols))
    excess[0] = mu
    for r in range(1, depth):
        last = r == depth - 1
        prev = excess[r - 1]
        excess[r] = mu + prev / (1 + prev) - (1.0 if last else 0.0) + (0.0 if last else 0.0)
        if last:
            excess[r] = mu + prev / (1 + prev)
    eps = excess / (1 + excess)
    last_inv = 1.0 / (mu + eps[depth - 2])
    theta = 2 * np.arcsinh(np.sqrt(mu) / 2)
    levels = strips.bit_length() - 1
    gain, cross = [], []
    top = np.zeros((strips, levels, cols))
    bot = np.zeros((strips, levels, cols))
    for level in range(levels):
        m = 1 << level
        n = m * depth
        half = np.sinh(theta / 2)
        b = n * theta
        a = (n - 0.5) * theta
        end_end = np.exp(a - b) * (1 + np.exp(-2 * a)) / (1 - np.exp(-2 * b)) / (2 * half)
        first_last = 2 * np.cosh(theta / 2) * np.exp(-b) / (1 - np.exp(-2 * b)) / (2 * half)
        gain.append(1 / (1 + 2 * end_end))
        cross.append(first_last)
        rho = [ratio_sinh(p * depth * theta, b) for p in range(m + 1)]
        for s in range(strips):
            p = s % m
            if (s >> level) & 1:
                top[s, level], bot[s, level] = rho[m - p], rho[m - 1 - p]
            else:
                top[s, level], bot[s, level] = rho[p], rho[p + 1]
    cast = lambda x: np.asarray(x, np.float32)
    return cast(eps), cast(last_inv[None]), cast(gain), cast(cross), cast(top), cast(bot)


def split(x):
    high = x.astype(bf16)
    return high, (x - high.astype(f32)).astype(bf16)


def split3(x):
    high = x.astype(bf16)
    rest = x - high.astype(f32)
    middle = rest.astype(bf16)
    return high, middle, (rest - middle.astype(f32)).astype(bf16)


def image_rows(count, fields):
    return -(-count // fields)


def spread(info_ref, chunk_refs, target):
    width = chunk_refs[0].shape[-1]
    count = target.shape[0]
    for d, ref in enumerate(chunk_refs):
        start = pl.multiple_of(info_ref[1 + d] * width, width)
        if len(target.shape) == 3:
            target[:, :, pl.ds(start, width)] = ref[0:count]
        else:
            below = ref[ref.shape[0] - image_rows(count, ref.shape[1]) :]
            target[:, pl.ds(start, width)] = below.reshape(-1, width)[:count]


def edges_kernel(x_top, x_bot, p_top, p_bot, i_top, i_bot, head_ref, tail_ref):
    fields, _, _ = x_top.shape
    for out_ref, rows, refs in (
        (head_ref, slice(0, 2), (x_top, p_top, i_top)),
        (tail_ref, slice(6, 8), (x_bot, p_bot, i_bot)),
    ):
        for f in range(fields):
            out_ref[:, f, :] = refs[0][f, rows, :]
            out_ref[:, fields + f, :] = refs[1][f, rows, :]
        out_ref[:, 2 * fields, :] = refs[2][rows, :]


def edges(x, p, image):
    fields, height, width = x.shape
    bottom = height // 8 - 1
    top = pl.BlockSpec((fields, 8, width), lambda i: (0, 0, 0))
    bot = pl.BlockSpec((fields, 8, width), lambda i: (0, bottom, 0))
    image_top = pl.BlockSpec((8, width), lambda i: (0, 0))
    image_bot = pl.BlockSpec((8, width), lambda i: (bottom, 0))
    out = pl.BlockSpec((2, 2 * fields + 1, width), lambda i: (0, 0, 0))
    return pl.pallas_call(
        edges_kernel,
        grid=(1,),
        out_shape=(room(2, 2 * fields + 1, width),) * 2,
        in_specs=[top, bot, top, bot, image_top, image_bot],
        out_specs=(out, out),
        compiler_params=pltpu.CompilerParams(vmem_limit_bytes=56 * 2**20),
        cost_estimate=cost(0, 8 * 4 * fields * width * 4),
        name="edges",
    )(x, x, p, p, image, image)


def pack_kernel(chunks, depth, with_image, info_ref, x_ref, *refs):
    fields, height, width = x_ref.shape
    if with_image:
        image_ref, *pieces = refs
    else:
        pieces = refs
    for d in range(chunks):
        place = info_ref[1 + chunks + d]
        start = pl.multiple_of(place * depth, depth)
        before = pl.multiple_of(jnp.maximum(start - 8, 0), 8)
        after = pl.multiple_of(jnp.minimum(start + depth, height - 8), 8)
        piece = pieces[d]
        for f in range(fields):
            piece[2 : 2 + depth, f, :] = x_ref[f, pl.ds(start, depth), :]
            piece[0:2, f, :] = x_ref[f, pl.ds(before, 8), :][6:8]
            piece[2 + depth : 4 + depth, f, :] = x_ref[f, pl.ds(after, 8), :][0:2]
        if with_image:
            rows = jnp.concatenate(
                [
                    image_ref[pl.ds(before, 8), :][6:8],
                    image_ref[pl.ds(start, depth), :],
                    image_ref[pl.ds(after, 8), :][0:2],
                ],
                0,
            )
            count = depth + 4
            for r in range(0, count, fields):
                size = min(fields, count - r)
                piece[depth + 4 + r // fields, 0:size, :] = rows[r : r + size]
            rest = -count % fields
            if rest:
                piece[depth + 3 + image_rows(count, fields), fields - rest :, :] = jnp.zeros(
                    (rest, width), f32
                )


def pack(info, x, image, chunks):
    fields, height, width = x.shape
    depth = height // chunks
    count = depth + 4 + (image_rows(depth + 4, fields) if image is not None else 0)
    args = (x,) if image is None else (x, image)
    return pl.pallas_call(
        functools.partial(pack_kernel, chunks, depth, image is not None),
        out_shape=(room(count, fields, width),) * chunks,
        in_specs=[SMEM] + [VMEM] * len(args),
        out_specs=(VMEM,) * chunks,
        compiler_params=params(*args, *(room(count, fields, width),) * chunks),
        cost_estimate=cost(0, 8 * fields * height * width),
        name="pack",
    )(info, *args)


def fill_kernel(chunks, depth, first, with_image, info_ref, above_ref, below_ref, *refs):
    pieces = refs[chunks:]
    fields = pieces[0].shape[1]
    for d in range(chunks):
        place = info_ref[1 + chunks + d]
        piece = pieces[d]
        for which, rows_ref, row in ((0, above_ref, 0), (chunks - 1, below_ref, depth + 2)):

            @pl.when(place == which)
            def _(piece=piece, rows_ref=rows_ref, row=row):
                piece[row : row + 2] = rows_ref[:, first : first + fields, :]
                if with_image:
                    for i in range(2):
                        line = depth + 4 + (row + i) // fields
                        at = (row + i) % fields
                        image = rows_ref[i, 2 * fields : 2 * fields + 1, :]
                        piece[line, at : at + 1, :] = image


def fill(info, above, below, pieces, first, with_image):
    chunks = len(pieces)
    count, fields, width = pieces[0].shape
    depth = count - 4
    if with_image:
        depth = next(n for n in range(1, count) if n + 4 + image_rows(n + 4, fields) == count)
    return pl.pallas_call(
        functools.partial(fill_kernel, chunks, depth, first, with_image),
        out_shape=(room(count, fields, width),) * chunks,
        in_specs=[SMEM] + [VMEM] * (2 + chunks),
        out_specs=(VMEM,) * chunks,
        input_output_aliases={3 + d: d for d in range(chunks)},
        compiler_params=params(*pieces),
        cost_estimate=cost(0, 16 * fields * width),
        name="fill",
    )(info, above, below, *pieces)


def weights_kernel(chunks, total_rows, info_ref, *rest):
    chunk_refs, (w_ref, deg_ref, image_ref) = rest[:chunks], rest[chunks:]
    depth, cols = deg_ref.shape
    spread(info_ref, chunk_refs, image_ref)
    center = image_ref[2 : 2 + depth, :]
    row = lax.broadcasted_iota(jnp.int32, (depth, cols), 0) + info_ref[0] * depth
    col = lax.broadcasted_iota(jnp.int32, (depth, cols), 1)
    degree = jnp.zeros((depth, cols), f32)
    for b in range(-2, 3):
        moved = pltpu.roll(center, b % cols, 1) if b else center
        col_ok = (col - b >= 0) & (col - b < cols)
        total = None
        for a in range(-2, 3):
            if a == 0 and b == 0:
                weight = jnp.ones((depth, cols), f32)
            else:
                contrast = moved - image_ref[2 + a : 2 + a + depth, :]
                ok = col_ok & (row + a >= 0) & (row + a < total_rows)
                weight = jnp.where(
                    ok,
                    jnp.exp(-beta_value * contrast * contrast - spatial_rate * (a * a + b * b)),
                    0.0,
                )
            w_ref[:, OFFSETS.index((a, b)), :] = weight
            total = weight if total is None else total + weight
        degree = degree + (pltpu.roll(total, (-b) % cols, 1) if b else total)
    deg_ref[...] = degree


def make_weights(info, pieces, depth, total_rows):
    cols = pieces[0].shape[2] * len(pieces)
    return pl.pallas_call(
        functools.partial(weights_kernel, len(pieces), total_rows),
        out_shape=(room(depth, 25, cols), room(depth, cols)),
        in_specs=[SMEM] + [VMEM] * len(pieces),
        out_specs=(VMEM,) * 2,
        scratch_shapes=[pltpu.VMEM((depth + 4, cols), f32)],
        compiler_params=params(*pieces, room(depth, 25, cols), extra=16 * 2**20),
        cost_estimate=cost(60 * depth * cols * 25, 25 * depth * cols * 4),
        name="weights",
    )(info, *pieces)


def graph_kernel(order, keep, lane_shift, chunks, *refs):
    if chunks:
        info_ref, chunk_refs, refs = refs[0], refs[1 : 1 + chunks], refs[1 + chunks :]
    else:
        v_ref, top_ref, bot_ref, *refs = refs
    (w_ref, deg_ref), refs = refs[:2], refs[2:]
    others, refs = refs[: len(order) - 1], list(refs[len(order) - 1 :])
    g_ref = refs.pop(0) if keep else None
    own_ref = refs.pop(0) if chunks else None
    gram_ref, pad_ref, acc_ref, sum_ref = refs
    depth, cols = deg_ref.shape
    fields = pad_ref.shape[1]
    if chunks:
        spread(info_ref, chunk_refs, pad_ref)
    else:
        pad_ref[0:2] = top_ref[...]
        pad_ref[2 : 2 + depth] = v_ref[...]
        pad_ref[2 + depth : 4 + depth] = bot_ref[...]
    parts = len(order)
    groups = fields // 8
    width = 256

    def one_row(r, acc):
        for c in range(cols // width):
            lanes = slice(c * width, (c + 1) * width)
            values = [pad_ref[r + a, :, lanes].reshape(groups, 8, width) for a in range(5)]
            for b in range(-2, 3):
                total = None
                for a in range(-2, 3):
                    value = values[a + 2]
                    if a or b:
                        o = OFFSETS.index((a, b))
                        value = w_ref[r, o : o + 1, lanes][None] * value
                    total = value if total is None else total + value
                sum_ref[b + 2, :, lanes] = total.reshape(fields, width)
        result = sum_ref[2]
        for b in (-2, -1, 1, 2):
            result = result + pltpu.roll(sum_ref[b + 2], (-b) % cols, 1)
        if keep:
            g_ref[r] = result
        own = pad_ref[r + 2]
        if chunks:
            own_ref[r] = own
        weighted = deg_ref[pl.ds(r, 1), :] * own
        left, position = [], 0
        for which in order:
            if which == "v":
                left.append(split(own))
            else:
                left.append(split(others[position][r]))
                position += 1
        left = jnp.concatenate([p[0] for p in left] + [p[1] for p in left], 0)
        graph_pair, degree_pair = split(result), split(weighted)
        right = jnp.concatenate(
            [graph_pair[0], degree_pair[0], graph_pair[1], degree_pair[1]], 0
        )
        return acc + lax.dot_general(
            left, right, (((1,), (1,)), ((), ())), preferred_element_type=f32
        )

    start = jnp.zeros((2 * parts * fields, 4 * fields), f32)
    acc = lax.fori_loop(0, depth, one_row, start, unroll=UNROLL)
    half = parts * fields
    acc_ref[...] = jnp.zeros(acc_ref.shape, f32)
    acc_ref[:, 0 : 4 * fields] = acc[:half] + acc[half:]
    both = acc_ref[...]
    both = both + pltpu.roll(both, LANES - 2 * fields, 1)
    lane = lax.broadcasted_iota(jnp.int32, both.shape, 1)
    both = jnp.where(lane < 2 * fields, both, 0.0)
    if lane_shift:
        both = pltpu.roll(both, lane_shift, 1)
    gram_ref[...] = both


def apply_graph(order, keep, lane_shift, fields_in, w, deg, *others, info=None):
    depth, cols = deg.shape
    fields = fields_in[0].shape[1]
    parts = len(order)
    chunks = len(fields_in) if info is not None else 0
    out_shape = [room(depth, fields, cols)] * (int(keep) + int(chunks > 0))
    out_shape += [room(parts * fields, LANES)]
    args = ((info,) if chunks else ()) + tuple(fields_in) + (w, deg) + others
    return pl.pallas_call(
        functools.partial(graph_kernel, order, keep, lane_shift, chunks),
        out_shape=tuple(out_shape),
        in_specs=[SMEM] * int(chunks > 0) + [VMEM] * (len(args) - int(chunks > 0)),
        out_specs=(VMEM,) * len(out_shape),
        scratch_shapes=[
            pltpu.VMEM((depth + 4, fields, cols), f32),
            pltpu.VMEM((parts * fields, LANES), f32),
            pltpu.VMEM((5, fields, cols), f32),
        ],
        compiler_params=params(w, deg, *fields_in, *others, *out_shape, room(depth + 9, fields, cols)),
        cost_estimate=cost(50 * fields * depth * cols * 4, 4 * cols * depth * (25 + 3 * fields)),
        name="graph_" + "".join(order),
    )(*args)


def forward_kernel(scaled, x_ref, *rest):
    if scaled:
        deg_ref, high_ref, low_ref, out_ref = rest
    else:
        high_ref, low_ref, out_ref = rest
    depth, fields, _ = x_ref.shape
    cols = high_ref.shape[0]
    block = math.gcd(depth, 16)
    contract = (((1,), (0,)), ((), ()))

    def one_block(i, _):
        start = i * block
        value = x_ref[pl.ds(start, block)]
        if scaled:
            value = value * deg_ref[pl.ds(start, block), :][:, None, :]
        high, low = split(value.reshape(block * fields, cols))
        result = lax.dot_general(high, high_ref[...], contract, preferred_element_type=f32)
        result += lax.dot_general(high, low_ref[...], contract, preferred_element_type=f32)
        result += lax.dot_general(low, high_ref[...], contract, preferred_element_type=f32)
        out_ref[pl.ds(start, block)] = result.reshape(block, fields, cols)
        return 0

    lax.fori_loop(0, depth // block, one_block, 0)


def cosine_forward(x, deg, high, low, depth, fields):
    cols = high.shape[0]
    args = (x,) + ((deg,) if deg is not None else ()) + (high, low)
    return pl.pallas_call(
        functools.partial(forward_kernel, deg is not None),
        out_shape=jax.ShapeDtypeStruct((depth, fields, cols), f32),
        in_specs=[pl.BlockSpec(memory_space=pltpu.VMEM)] * len(args),
        out_specs=pl.BlockSpec(memory_space=pltpu.VMEM),
        compiler_params=params(*args, room(depth, fields, cols), extra=12 * 2**20),
        cost_estimate=cost(6 * depth * fields * cols * cols, 4 * cols * (2 * depth * fields + cols)),
        name="cosine_forward",
    )(*args)


def solve_kernel(gram_ref, fg_ref, fd_ref, eps_ref, last_ref, f_ref, ends_ref):
    depth, fields, cols = fg_ref.shape
    gram = gram_ref[...]
    affinity = pltpu.roll(gram, LANES - 4 * fields, 1)[:, :fields]
    mass = pltpu.roll(gram, LANES - 5 * fields, 1)[:, :fields]
    row = lax.broadcasted_iota(jnp.int32, (fields, fields), 0)
    for k in range(fields):
        inverse = 1.0 / mass[k : k + 1, k : k + 1]
        column = mass[:, k : k + 1]
        mass_row = mass[k : k + 1, :] * inverse
        affinity_row = affinity[k : k + 1, :] * inverse
        affinity = jnp.where(row == k, affinity_row, affinity - column * affinity_row)
        mass = jnp.where(row == k, mass_row, mass - column * mass_row)
    ray = split3(affinity.T)
    left = jnp.concatenate([ray[i] for i in (0, 0, 0, 1, 1, 2)], 1)

    def one_row(r, carry):
        piece = split3(fd_ref[r])
        right = jnp.concatenate([piece[i] for i in (0, 1, 2, 0, 1, 0)], 0)
        value = fg_ref[r] - jnp.dot(left, right, preferred_element_type=f32)
        f_ref[r] = value
        keep = eps_ref[pl.ds(jnp.maximum(r - 1, 0), 1), :]
        return value + (carry - keep * carry)

    down = lax.fori_loop(0, depth, one_row, jnp.zeros((fields, cols), f32), unroll=UNROLL)

    def back_row(i, carry):
        r = depth - 1 - i
        keep = eps_ref[pl.ds(jnp.maximum(i - 1, 0), 1), :]
        return f_ref[r] + (carry - keep * carry)

    up = lax.fori_loop(0, depth, back_row, jnp.zeros((fields, cols), f32), unroll=UNROLL)
    last = last_ref[...]
    ends_ref[0] = up * last
    ends_ref[1] = down * last


def row_solve(gram, fg, fd, eps, last):
    depth, fields, cols = fg.shape
    return pl.pallas_call(
        solve_kernel,
        out_shape=(
            jax.ShapeDtypeStruct((depth, fields, cols), f32),
            jax.ShapeDtypeStruct((2, fields, cols), f32),
        ),
        in_specs=[pl.BlockSpec(memory_space=pltpu.VMEM)] * 5,
        out_specs=(pl.BlockSpec(memory_space=pltpu.VMEM),) * 2,
        compiler_params=params(fg, fd, eps, room(depth, fields, cols)),
        cost_estimate=cost(200 * depth * fields * cols, 4 * 3 * depth * fields * cols),
        name="row_solve",
    )(gram, fg, fd, eps, last)


def merge_kernel(level, count, last, info_ref, gain_ref, cross_ref, *refs):
    groups, outs = [ref[...] for ref in refs[:count]], refs[count:]
    place = info_ref[0] >> level

    def join(own, other, step, keep):
        right = ((place >> step) & 1) == 1
        lower, upper = jnp.where(right, other, own), jnp.where(right, own, other)
        row = slice(level + step, level + step + 1)
        g = (lower[1] - upper[0]) * gain_ref[row, :]
        moved = g * cross_ref[row, :]
        return g, jnp.stack([lower[0] - moved, upper[1] + moved]) if keep else None

    g, ends = join(groups[0], groups[1], 0, count == 4 or not last)
    outs[0][...] = g
    if count == 4:
        _, others = join(groups[2], groups[3], 0, True)
        g, ends = join(ends, others, 1, not last)
        outs[1][...] = g
    if not last:
        outs[-1][...] = ends


def merge(level, last, info, groups, gain, cross):
    _, fields, cols = groups[0].shape
    count = len(groups)
    out_shape = (room(fields, cols),) * (count // 2) + (() if last else (room(2, fields, cols),))
    return pl.pallas_call(
        functools.partial(merge_kernel, level, count, last),
        out_shape=out_shape,
        in_specs=[SMEM] + [VMEM] * (2 + count),
        out_specs=(VMEM,) * len(out_shape),
        compiler_params=params(*groups, *out_shape),
        cost_estimate=cost(10 * fields * cols, 28 * fields * cols),
        name="merge",
    )(info, gain, cross, *groups)


def inverse_kernel(levels, chunks, info_ref, *refs):
    g_refs = refs[:levels]
    f_ref, flux_ref, eps_ref, last_ref, high_ref, low_ref = refs[levels : levels + 6]
    out_ref, head_ref, tail_ref, *piece_refs, u_ref = refs[levels + 6 :]
    depth, fields, cols = f_ref.shape
    width = cols // chunks
    flux_top = jnp.zeros((fields, cols), f32)
    flux_bot = jnp.zeros((fields, cols), f32)
    for level in range(levels):
        g = g_refs[level][...]
        flux_top = flux_top + g * flux_ref[level : level + 1, :]
        flux_bot = flux_bot - g * flux_ref[levels + level : levels + level + 1, :]

    u_ref[0] = f_ref[0] + flux_top

    def down_row(r, carry):
        keep = eps_ref[pl.ds(r - 1, 1), :]
        value = f_ref[r] + (carry - keep * carry)
        u_ref[r] = value
        return value

    value = lax.fori_loop(1, depth, down_row, u_ref[0])
    value = (value + flux_bot) * last_ref[...]
    u_ref[depth - 1] = value

    def up_row(i, carry):
        r = depth - 2 - i
        keep = eps_ref[pl.ds(r, 1), :]
        total = u_ref[r] + carry
        total = total - keep * total
        u_ref[r] = total
        return total

    lax.fori_loop(0, depth - 1, up_row, value)
    block = 8

    def one_block(i, _):
        start = i * block
        high, low = split(u_ref[pl.ds(start, block)].reshape(block * fields, cols))
        result = jnp.dot(high, high_ref[...], preferred_element_type=f32)
        result += jnp.dot(high, low_ref[...], preferred_element_type=f32)
        result += jnp.dot(low, high_ref[...], preferred_element_type=f32)
        out_ref[pl.ds(start, block)] = result.reshape(block, fields, cols)
        for d in range(chunks):
            lane = pl.multiple_of(info_ref[1 + d] * width, width)
            piece_refs[d][pl.ds(start, block)] = out_ref[pl.ds(start, block), :, pl.ds(lane, width)]
        return 0

    lax.fori_loop(0, depth // block, one_block, 0)
    head_ref[...] = out_ref[0:2]
    tail_ref[...] = out_ref[depth - 2 : depth]


def row_inverse(info, gs, f, flux, eps, last, high, low, chunks):
    depth, fields, cols = f.shape
    out_shape = (room(depth, fields, cols),) + (room(2, fields, cols),) * 2
    out_shape += (room(depth, fields, cols // chunks),) * chunks
    return pl.pallas_call(
        functools.partial(inverse_kernel, len(gs), chunks),
        out_shape=out_shape,
        in_specs=[SMEM] + [VMEM] * (len(gs) + 6),
        out_specs=(VMEM,) * len(out_shape),
        scratch_shapes=[pltpu.VMEM((depth, fields, cols), f32)],
        compiler_params=params(*gs, f, high, low, *out_shape, f, extra=12 * 2**20),
        cost_estimate=cost(6 * depth * fields * cols * cols, 4 * cols * (2 * depth * fields + cols)),
        name="row_inverse",
    )(info, *gs, f, flux, eps, last, high, low)


def hdot(a, b, contract):
    return lax.dot_general(
        a, b, ((contract[0], contract[1]), ((), ())), precision=highest, preferred_element_type=f32
    )


def cholesky_apply(matrix, target):
    size = matrix.shape[0]
    step = 8
    mats = [matrix[i : i + step] for i in range(0, size, step)]
    tars = [target[i : i + step] for i in range(0, size, step)]
    local_row = lax.broadcasted_iota(jnp.int32, (step, 1), 0)
    for k in range(size):
        own, inner = divmod(k, step)
        pivot_row = mats[own][inner : inner + 1, :]
        target_row = tars[own][inner : inner + 1, :]
        inverse = 1.0 / pivot_row[:, k : k + 1]
        for i in range(own, size // step):
            factor = mats[i][:, k : k + 1] * inverse
            if i == own:
                factor = jnp.where(local_row > inner, factor, 0.0)
            mats[i] = mats[i] - factor * pivot_row
            tars[i] = tars[i] - factor * target_row
    matrix = jnp.concatenate(mats, 0)
    target = jnp.concatenate(tars, 0)
    row = lax.broadcasted_iota(jnp.int32, matrix.shape, 0)
    col = lax.broadcasted_iota(jnp.int32, matrix.shape, 1)
    pivots = jnp.sum(jnp.where(row == col, matrix, 0.0), 1, keepdims=True)
    return target * (1.0 / jnp.sqrt(pivots))


def ritz_kernel(fields, pixel_total, first_ref, second_ref, ritz_ref, coeff_ref):
    size = 3 * fields
    gram = second_ref[...]
    first = first_ref[...]
    row = lax.broadcasted_iota(jnp.int32, (LANES, size), 0)
    col = lax.broadcasted_iota(jnp.int32, (LANES, size), 1)
    place_a = jnp.zeros((LANES, size), jnp.bool_)
    place_b = jnp.zeros((LANES, size), jnp.bool_)
    for group, target in ((4, 0), (0, 1), (2, 2)):
        inside = (col >= target * fields) & (col < (target + 1) * fields)
        place_a = place_a | (inside & (row - group * fields == col - target * fields))
        place_b = place_b | (inside & (row - (group + 1) * fields == col - target * fields))
    place_a = place_a.astype(f32)
    place_b = place_b.astype(f32)
    srow = lax.broadcasted_iota(jnp.int32, (size, size), 0)
    scol = lax.broadcasted_iota(jnp.int32, (size, size), 1)
    same = srow // fields == scol // fields
    eye = (srow == scol).astype(f32)

    def assemble(place):
        part = hdot(gram, place, ((1,), (0,)))
        top = hdot(first, place, ((1,), (0,)))
        part = jnp.concatenate([part[:fields] + top, part[fields:]], 0)
        both = part + part.T
        return jnp.where(same, 0.5 * both, both)

    big_a = assemble(place_a)
    big_b = assemble(place_b)
    diagonal = big_b * eye
    scale_col = 1.0 / jnp.sqrt(jnp.sum(diagonal, 1, keepdims=True) + 1e-6)
    scale_row = 1.0 / jnp.sqrt(jnp.sum(diagonal, 0, keepdims=True) + 1e-6)
    norm_a = scale_col * big_a * scale_row
    norm_b = scale_col * big_b * scale_row
    inverse = cholesky_apply(norm_b, eye)
    reduced = hdot(hdot(inverse, norm_a, ((1,), (0,))), inverse, ((1,), (1,)))
    reduced = 0.5 * (reduced + reduced.T) + ritz_offset * eye
    power = hdot(reduced, reduced, ((1,), (0,)))
    power = hdot(power, power, ((1,), (0,)))
    images = power[:fields]
    basis = cholesky_apply(hdot(images, images, ((1,), (1,))), images)
    images = hdot(basis, power, ((1,), (0,)))
    basis = cholesky_apply(hdot(images, images, ((1,), (1,))), images)
    images = hdot(basis, reduced, ((1,), (0,)))
    ones = jnp.ones((8, size), f32)
    ritz_ref[...] = hdot(ones, basis * images, ((1,), (1,)))[0:1] - ritz_offset
    coeff_ref[...] = math.sqrt(pixel_total) * scale_col * hdot(inverse, basis, ((0,), (1,)))


def ritz_step(first, second, fields, pixel_total):
    return pl.pallas_call(
        functools.partial(ritz_kernel, fields, pixel_total),
        out_shape=(
            room(1, fields),
            room(3 * fields, fields),
        ),
        in_specs=[pl.BlockSpec(memory_space=pltpu.VMEM)] * 2,
        out_specs=(pl.BlockSpec(memory_space=pltpu.VMEM),) * 2,
        compiler_params=params(),
        cost_estimate=cost(1 << 25, 1 << 16),
        name="ritz",
    )(first, second)


def combine_kernel(chunks, info_ref, coeff_ref, x_ref, p_ref, *refs):
    pieces, (block_ref, direction_ref, h_ref, high_ref, low_ref) = refs[:chunks], refs[chunks:]
    fields = x_ref.shape[0]
    width = x_ref.shape[2]
    group = 8 * fields

    @pl.when(pl.program_id(0) == 0)
    def _():
        r = lax.broadcasted_iota(jnp.int32, (group, fields), 0)
        c = lax.broadcasted_iota(jnp.int32, (group, fields), 1)
        rows_of = (r // 8 == c).astype(f32)
        f = lax.broadcasted_iota(jnp.int32, (fields, group), 0)
        q = lax.broadcasted_iota(jnp.int32, (fields, group), 1)
        row = lax.broadcasted_iota(jnp.int32, (group, group), 0)
        col = lax.broadcasted_iota(jnp.int32, (group, group), 1)
        coeffs = coeff_ref[...]
        for part in range(3):
            own = coeffs[part * fields : (part + 1) * fields, :].T
            if part == 1:
                cols_of, same = q % fields == f, row % 8 == col // fields
            else:
                cols_of, same = q // 8 == f, row % 8 == col % 8
            wide = hdot(own, cols_of.astype(f32), ((1,), (0,)))
            wide = jnp.where(same, hdot(rows_of, wide, ((1,), (0,))), 0.0)
            lanes = slice(part * group, (part + 1) * group)
            high_ref[:, lanes], low_ref[:, lanes] = split(wide)

    for d in range(chunks):

        @pl.when(pl.program_id(0) == d)
        def _(d=d):
            h_ref[...] = pieces[d][...]

    dot = functools.partial(jnp.dot, preferred_element_type=f32)
    for t in range(x_ref.shape[1] // 8):
        rows = slice(8 * t, 8 * t + 8)
        x = split(x_ref[:, rows, :].reshape(group, width))
        h = split(h_ref[rows].reshape(group, width))
        p = split(p_ref[:, rows, :].reshape(group, width))
        hp = [jnp.concatenate([h[i], p[i]], 0) for i in range(2)]
        x_high, x_low = high_ref[:, :group], low_ref[:, :group]
        hp_high, hp_low = high_ref[:, group:], low_ref[:, group:]
        direction = dot(hp_high, hp[0]) + dot(hp_low, hp[0]) + dot(hp_high, hp[1])
        x_left = jnp.concatenate([x_high, x_high, x_low], 1)
        block = direction + dot(x_left, jnp.concatenate([x[0], x[1], x[0]], 0))
        block_ref[:, rows, :] = block.reshape(fields, 8, width)
        direction_ref[:, rows, :] = direction.reshape(fields, 8, width)


def combine(info, coeffs, x, p, pieces):
    fields, rows, width = x.shape
    chunks = len(pieces)
    depth = rows // chunks
    spec = pl.BlockSpec((fields, depth, width), lambda i, s: (0, s[1 + chunks + i], 0))
    whole = pl.BlockSpec((depth, fields, width), lambda i, s: (0, 0, 0))
    return pl.pallas_call(
        functools.partial(combine_kernel, chunks),
        out_shape=(room(fields, rows, width),) * 2,
        grid_spec=pltpu.PrefetchScalarGridSpec(
            num_scalar_prefetch=1,
            grid=(chunks,),
            in_specs=[pl.BlockSpec(coeffs.shape, lambda i, s: (0, 0)), spec, spec] + [whole] * chunks,
            out_specs=(spec, spec),
            scratch_shapes=[pltpu.VMEM((depth, fields, width), f32)]
            + [pltpu.VMEM((8 * fields, 24 * fields), bf16)] * 2,
        ),
        compiler_params=params(room(16 * depth, fields, width)),
        cost_estimate=cost(200 * rows * fields * width, 20 * rows * fields * width),
        name="combine",
    )(info, coeffs, x, p, *pieces)


def ring_order(count):
    half = count // 2
    return [*range(half), *reversed(range(half, count))] if count > 1 else [0]


@functools.lru_cache(None)
def device_table(strips, chunks):
    order = ring_order(chunks)
    place = [order.index(c) for c in range(chunks)]
    table = []
    for device in range(strips):
        row, col = divmod(device, chunks)
        others = [col ^ d for d in range(chunks)]
        table.append([row * chunks + place[col], *others, *[place[c] for c in others]])
    return np.asarray(table, np.int32)


def local(intensity, start_block, old_direction):
    fields, height, width = start_block.shape
    chunks = lax.axis_size("col")
    row_count = lax.axis_size("row")
    strips = row_count * chunks
    depth = height // chunks
    rows, cols = strips * depth, chunks * width
    device = lax.axis_index("row") * chunks + lax.axis_index("col")
    levels = strips.bit_length() - 1
    order = ring_order(chunks)
    owner = [(s // chunks) * chunks + order[s % chunks] for s in range(strips)]

    table = device_table(strips, chunks)
    eps, last, gain, cross, top_all, bot_all = row_tables(strips, depth, cols)
    by_device = np.concatenate([top_all[table[:, 0]], bot_all[table[:, 0]]], 1)
    high, low = (jnp.asarray(t) for t in cosine_tables(cols))
    high_t, low_t = (jnp.asarray(t.T.copy()) for t in cosine_tables(cols))
    eps, last, gain, cross = (jnp.asarray(t) for t in (eps, last, gain, cross))
    info = lax.dynamic_index_in_dim(jnp.asarray(table), device, 0, False)
    flux = lax.dynamic_index_in_dim(jnp.asarray(by_device), device, 0, False)

    first = chunks.bit_length() - 1
    row_groups = [[first]] + [[*range(b, min(b + 2, levels))] for b in range(first + 1, levels, 2)]
    col_groups = [[*range(b, min(b + 2, first))] for b in range(0, first, 2)]

    def add_up(value, groups, late=None):
        for group in groups:
            away = [1 << b for b in group]
            away += [sum(away)] if len(away) == 2 else []
            got = [lax.ppermute(value, BOTH, [(i, i ^ m) for i in range(strips)]) for m in away]
            if late is not None and group is groups[-1]:
                late, got = lax.optimization_barrier((late, got))
            value = value + got[0] + (got[1] + got[2]) if len(got) == 3 else value + got[0]
        return value, late

    def away(piece, d):
        return lax.ppermute(piece, "col", [(c, c ^ d) for c in range(chunks)])

    def exchange(pieces):
        return [pieces[0]] + [away(pieces[d], d) for d in range(1, chunks)]

    head, tail = edges(start_block, old_direction, intensity)
    above = lax.ppermute(tail, "row", [(i, i + 1) for i in range(row_count - 1)])
    below = lax.ppermute(head, "row", [(i + 1, i) for i in range(row_count - 1)])
    x_pieces = pack(info, start_block, intensity, chunks)
    x_pieces = exchange(fill(info, above, below, x_pieces, 0, True))
    p_pieces = pack(info, old_direction, None, chunks)
    p_pieces = exchange(fill(info, above, below, p_pieces, fields, False))
    x_pieces, flux = lax.optimization_barrier((x_pieces, flux))
    w, deg = make_weights(info, x_pieces, depth, rows)
    graph_x, x, gram_x = apply_graph(("v",), True, 4 * fields, x_pieces, w, deg, info=info)
    gram_x, _ = add_up(gram_x, row_groups)
    gram_x, p_pieces = lax.optimization_barrier((gram_x, p_pieces))
    gram_x, _ = add_up(gram_x, col_groups)
    spectrum_g = cosine_forward(graph_x, None, high_t, low_t, depth, fields)
    spectrum_d = cosine_forward(x, deg, high_t, low_t, depth, fields)
    f, ends = row_solve(gram_x, spectrum_g, spectrum_d, eps, last)

    gs = []
    groups = col_groups + row_groups
    for group in groups:
        level = group[0]
        found = {0: ends}
        for d in range(1, 1 << len(group)):
            place = (int(table[d << level, 0]) ^ int(table[0, 0])) >> level
            pairs = [(i, i ^ (d << level)) for i in range(strips)]
            found[place & (1 << len(group)) - 1] = lax.ppermute(ends, BOTH, pairs)
        is_last = group is groups[-1]
        *new, ends = merge(level, is_last, info, [found[e] for e in sorted(found)], gain, cross) + (
            (None,) if is_last else ()
        )
        gs += new
        if group is groups[-2]:
            p_pieces, ends = lax.optimization_barrier((p_pieces, ends))
    p, gram_p = apply_graph(("x", "v"), False, 2 * fields, p_pieces, w, deg, x, info=info)
    gs[-1], gram_p = lax.optimization_barrier((gs[-1], gram_p))

    h, head, tail, *h_pieces = row_inverse(info, gs, f, flux, eps, last, high, low, chunks)
    h_above = lax.ppermute(tail, BOTH, [(owner[s], owner[s + 1]) for s in range(strips - 1)])
    h_below = lax.ppermute(head, BOTH, [(owner[s + 1], owner[s]) for s in range(strips - 1)])
    h_own, *h_early, h_late = h_pieces
    h_early, h_above, h_below = lax.optimization_barrier((h_early, h_above, h_below))
    h_early = [away(piece, d) for d, piece in enumerate(h_early, 1)]
    (gram_h,) = apply_graph(("x", "v", "p"), False, 0, (h, h_above, h_below), w, deg, x, p)
    zero = jnp.zeros((fields, LANES), f32)
    gram = gram_h + jnp.concatenate([gram_p[:fields], zero, gram_p[fields:]], 0)
    gram, _ = add_up(gram, row_groups)
    gram, h_early = lax.optimization_barrier((gram, h_early))
    gram, h_late = add_up(gram, col_groups, h_late)
    h_pieces = [h_own, *h_early, away(h_late, chunks - 1)]
    ritz, coeffs = ritz_step(gram_x, gram, fields, rows * cols)
    new_block, new_direction = combine(info, coeffs, start_block, old_direction, h_pieces)
    return new_block, new_direction, ritz.reshape(fields)


def solution(mesh):
    return jax.shard_map(
        local,
        mesh=mesh,
        in_specs=(P("row", "col"), P(None, "row", "col"), P(None, "row", "col")),
        out_specs=(P(None, "row", "col"), P(None, "row", "col"), P()),
        check_vma=False,
    )
```

```python
import functools
import math

import jax
import jax.numpy as jnp
import numpy as np
from jax import lax
from jax.experimental import pallas as pl
from jax.experimental.pallas import tpu as pltpu
from jax.sharding import PartitionSpec as P

SWEEPS = 8
beta_value = 4.0
spatial_rate = 0.25
shift_numerator = 16.0
ritz_offset = 1.5
highest = lax.Precision.HIGHEST
f32 = jnp.float32
bf16 = jnp.bfloat16
BOTH = ("row", "col")
LANES = 128
UNROLL = 4
VMEM = pl.BlockSpec(memory_space=pltpu.VMEM)
SMEM = pl.BlockSpec(memory_space=pltpu.SMEM)
OFFSETS = [(a, b) for a in range(-2, 3) for b in range(-2, 3)]


def params(*arrays, extra=4 * 2**20):
    total = extra
    for a in arrays:
        shape = (1, 1) + tuple(a.shape)
        padded = math.prod(shape[:-2]) * (-(-shape[-2] // 8) * 8) * (-(-shape[-1] // LANES) * LANES)
        total += padded * a.dtype.itemsize
    return pltpu.CompilerParams(vmem_limit_bytes=total)


def room(*shape):
    return jax.ShapeDtypeStruct(shape, f32)


def cost(flops, nbytes):
    return pl.CostEstimate(flops=int(flops), bytes_accessed=int(nbytes), transcendentals=0)


@functools.lru_cache(None)
def cosine_tables(length):
    k = np.arange(length)[:, None]
    n = np.arange(length)[None, :]
    table = np.cos(np.pi * ((2 * n + 1) * k % (4 * length)) / (2 * length)) * np.sqrt(2.0 / length)
    table[0] *= np.sqrt(0.5)
    high = table.astype(jnp.bfloat16)
    low = (table - high.astype(np.float64)).astype(jnp.bfloat16)
    return high, low


def ratio_sinh(a, b):
    return np.exp(a - b) * (1 - np.exp(-2 * a)) / (1 - np.exp(-2 * b))


@functools.lru_cache(None)
def row_tables(strips, depth, cols):
    rows = strips * depth
    lam = 4 * np.sin(np.pi * np.arange(cols) / (2 * cols)) ** 2
    mu = lam + shift_numerator / (rows * cols)
    excess = np.zeros((depth, cols))
    excess[0] = mu
    for r in range(1, depth):
        last = r == depth - 1
        prev = excess[r - 1]
        excess[r] = mu + prev / (1 + prev) - (1.0 if last else 0.0) + (0.0 if last else 0.0)
        if last:
            excess[r] = mu + prev / (1 + prev)
    eps = excess / (1 + excess)
    last_inv = 1.0 / (mu + eps[depth - 2])
    theta = 2 * np.arcsinh(np.sqrt(mu) / 2)
    levels = strips.bit_length() - 1
    gain, cross = [], []
    top = np.zeros((strips, levels, cols))
    bot = np.zeros((strips, levels, cols))
    for level in range(levels):
        m = 1 << level
        n = m * depth
        half = np.sinh(theta / 2)
        b = n * theta
        a = (n - 0.5) * theta
        end_end = np.exp(a - b) * (1 + np.exp(-2 * a)) / (1 - np.exp(-2 * b)) / (2 * half)
        first_last = 2 * np.cosh(theta / 2) * np.exp(-b) / (1 - np.exp(-2 * b)) / (2 * half)
        gain.append(1 / (1 + 2 * end_end))
        cross.append(first_last)
        rho = [ratio_sinh(p * depth * theta, b) for p in range(m + 1)]
        for s in range(strips):
            p = s % m
            if (s >> level) & 1:
                top[s, level], bot[s, level] = rho[m - p], rho[m - 1 - p]
            else:
                top[s, level], bot[s, level] = rho[p], rho[p + 1]
    cast = lambda x: np.asarray(x, np.float32)
    return cast(eps), cast(last_inv[None]), cast(gain), cast(cross), cast(top), cast(bot)


def split(x):
    high = x.astype(bf16)
    return high, (x - high.astype(f32)).astype(bf16)


def split3(x):
    high = x.astype(bf16)
    rest = x - high.astype(f32)
    middle = rest.astype(bf16)
    return high, middle, (rest - middle.astype(f32)).astype(bf16)


def image_rows(count, fields):
    return -(-count // fields)


def spread(info_ref, chunk_refs, target):
    width = chunk_refs[0].shape[-1]
    count = target.shape[0]
    for d, ref in enumerate(chunk_refs):
        start = pl.multiple_of(info_ref[1 + d] * width, width)
        if len(target.shape) == 3:
            target[:, :, pl.ds(start, width)] = ref[0:count]
        else:
            below = ref[ref.shape[0] - image_rows(count, ref.shape[1]) :]
            target[:, pl.ds(start, width)] = below.reshape(-1, width)[:count]


def edges_kernel(x_top, x_bot, p_top, p_bot, i_top, i_bot, head_ref, tail_ref):
    fields, _, _ = x_top.shape
    for out_ref, rows, refs in (
        (head_ref, slice(0, 2), (x_top, p_top, i_top)),
        (tail_ref, slice(6, 8), (x_bot, p_bot, i_bot)),
    ):
        for f in range(fields):
            out_ref[:, f, :] = refs[0][f, rows, :]
            out_ref[:, fields + f, :] = refs[1][f, rows, :]
        out_ref[:, 2 * fields, :] = refs[2][rows, :]


def edges(x, p, image):
    fields, height, width = x.shape
    bottom = height // 8 - 1
    top = pl.BlockSpec((fields, 8, width), lambda i: (0, 0, 0))
    bot = pl.BlockSpec((fields, 8, width), lambda i: (0, bottom, 0))
    image_top = pl.BlockSpec((8, width), lambda i: (0, 0))
    image_bot = pl.BlockSpec((8, width), lambda i: (bottom, 0))
    out = pl.BlockSpec((2, 2 * fields + 1, width), lambda i: (0, 0, 0))
    return pl.pallas_call(
        edges_kernel,
        grid=(1,),
        out_shape=(room(2, 2 * fields + 1, width),) * 2,
        in_specs=[top, bot, top, bot, image_top, image_bot],
        out_specs=(out, out),
        compiler_params=pltpu.CompilerParams(vmem_limit_bytes=56 * 2**20),
        cost_estimate=cost(0, 8 * 4 * fields * width * 4),
        name="edges",
    )(x, x, p, p, image, image)


def pack_kernel(chunks, depth, with_image, info_ref, x_ref, *refs):
    fields, height, width = x_ref.shape
    if with_image:
        image_ref, *pieces = refs
    else:
        pieces = refs
    for d in range(chunks):
        place = info_ref[1 + chunks + d]
        start = pl.multiple_of(place * depth, depth)
        before = pl.multiple_of(jnp.maximum(start - 8, 0), 8)
        after = pl.multiple_of(jnp.minimum(start + depth, height - 8), 8)
        piece = pieces[d]
        for f in range(fields):
            piece[2 : 2 + depth, f, :] = x_ref[f, pl.ds(start, depth), :]
            piece[0:2, f, :] = x_ref[f, pl.ds(before, 8), :][6:8]
            piece[2 + depth : 4 + depth, f, :] = x_ref[f, pl.ds(after, 8), :][0:2]
        if with_image:
            rows = jnp.concatenate(
                [
                    image_ref[pl.ds(before, 8), :][6:8],
                    image_ref[pl.ds(start, depth), :],
                    image_ref[pl.ds(after, 8), :][0:2],
                ],
                0,
            )
            count = depth + 4
            for r in range(0, count, fields):
                size = min(fields, count - r)
                piece[depth + 4 + r // fields, 0:size, :] = rows[r : r + size]
            rest = -count % fields
            if rest:
                piece[depth + 3 + image_rows(count, fields), fields - rest :, :] = jnp.zeros(
                    (rest, width), f32
                )


def pack(info, x, image, chunks):
    fields, height, width = x.shape
    depth = height // chunks
    count = depth + 4 + (image_rows(depth + 4, fields) if image is not None else 0)
    args = (x,) if image is None else (x, image)
    return pl.pallas_call(
        functools.partial(pack_kernel, chunks, depth, image is not None),
        out_shape=(room(count, fields, width),) * chunks,
        in_specs=[SMEM] + [VMEM] * len(args),
        out_specs=(VMEM,) * chunks,
        compiler_params=params(*args, *(room(count, fields, width),) * chunks),
        cost_estimate=cost(0, 8 * fields * height * width),
        name="pack",
    )(info, *args)


def fill_kernel(chunks, depth, first, with_image, info_ref, above_ref, below_ref, *refs):
    pieces = refs[chunks:]
    fields = pieces[0].shape[1]
    for d in range(chunks):
        place = info_ref[1 + chunks + d]
        piece = pieces[d]
        for which, rows_ref, row in ((0, above_ref, 0), (chunks - 1, below_ref, depth + 2)):

            @pl.when(place == which)
            def _(piece=piece, rows_ref=rows_ref, row=row):
                piece[row : row + 2] = rows_ref[:, first : first + fields, :]
                if with_image:
                    for i in range(2):
                        line = depth + 4 + (row + i) // fields
                        at = (row + i) % fields
                        image = rows_ref[i, 2 * fields : 2 * fields + 1, :]
                        piece[line, at : at + 1, :] = image


def fill(info, above, below, pieces, first, with_image):
    chunks = len(pieces)
    count, fields, width = pieces[0].shape
    depth = count - 4
    if with_image:
        depth = next(n for n in range(1, count) if n + 4 + image_rows(n + 4, fields) == count)
    return pl.pallas_call(
        functools.partial(fill_kernel, chunks, depth, first, with_image),
        out_shape=(room(count, fields, width),) * chunks,
        in_specs=[SMEM] + [VMEM] * (2 + chunks),
        out_specs=(VMEM,) * chunks,
        input_output_aliases={3 + d: d for d in range(chunks)},
        compiler_params=params(*pieces),
        cost_estimate=cost(0, 16 * fields * width),
        name="fill",
    )(info, above, below, *pieces)


def weights_kernel(chunks, total_rows, info_ref, *rest):
    chunk_refs, (w_ref, deg_ref, image_ref) = rest[:chunks], rest[chunks:]
    depth, cols = deg_ref.shape
    spread(info_ref, chunk_refs, image_ref)
    center = image_ref[2 : 2 + depth, :]
    row = lax.broadcasted_iota(jnp.int32, (depth, cols), 0) + info_ref[0] * depth
    col = lax.broadcasted_iota(jnp.int32, (depth, cols), 1)
    degree = jnp.zeros((depth, cols), f32)
    for b in range(-2, 3):
        moved = pltpu.roll(center, b % cols, 1) if b else center
        col_ok = (col - b >= 0) & (col - b < cols)
        total = None
        for a in range(-2, 3):
            if a == 0 and b == 0:
                weight = jnp.ones((depth, cols), f32)
            else:
                contrast = moved - image_ref[2 + a : 2 + a + depth, :]
                ok = col_ok & (row + a >= 0) & (row + a < total_rows)
                weight = jnp.where(
                    ok,
                    jnp.exp(-beta_value * contrast * contrast - spatial_rate * (a * a + b * b)),
                    0.0,
                )
            w_ref[:, OFFSETS.index((a, b)), :] = weight
            total = weight if total is None else total + weight
        degree = degree + (pltpu.roll(total, (-b) % cols, 1) if b else total)
    deg_ref[...] = degree


def make_weights(info, pieces, depth, total_rows):
    cols = pieces[0].shape[2] * len(pieces)
    return pl.pallas_call(
        functools.partial(weights_kernel, len(pieces), total_rows),
        out_shape=(room(depth, 25, cols), room(depth, cols)),
        in_specs=[SMEM] + [VMEM] * len(pieces),
        out_specs=(VMEM,) * 2,
        scratch_shapes=[pltpu.VMEM((depth + 4, cols), f32)],
        compiler_params=params(*pieces, room(depth, 25, cols), extra=16 * 2**20),
        cost_estimate=cost(60 * depth * cols * 25, 25 * depth * cols * 4),
        name="weights",
    )(info, *pieces)


def graph_kernel(order, keep, lane_shift, chunks, part, *refs):
    if chunks:
        info_ref, chunk_refs, refs = refs[0], refs[1 : 1 + chunks], refs[1 + chunks :]
    elif part == "inner":
        v_ref, *refs = refs
    else:
        v_ref, top_ref, bot_ref, *refs = refs
    (w_ref, deg_ref), refs = refs[:2], refs[2:]
    others, refs = refs[: len(order) - 1], list(refs[len(order) - 1 :])
    g_ref = refs.pop(0) if keep else None
    own_ref = refs.pop(0) if chunks else None
    gram_ref, pad_ref, acc_ref, sum_ref = refs
    depth, cols = deg_ref.shape
    fields = sum_ref.shape[1]
    if chunks:
        spread(info_ref, chunk_refs, pad_ref)
    elif part == "outer":
        pad_ref[0:2] = top_ref[...]
        pad_ref[2:6] = v_ref[0:4]
        pad_ref[depth - 2 : depth + 2] = v_ref[depth - 4 : depth]
        pad_ref[2 + depth : 4 + depth] = bot_ref[...]
    parts = len(order)
    groups = fields // 8
    width = 256
    source_ref, shift = (v_ref, 2) if part == "inner" else (pad_ref, 0)

    def one_row(r, acc):
        for c in range(cols // width):
            lanes = slice(c * width, (c + 1) * width)
            values = [
                source_ref[r + a - shift, :, lanes].reshape(groups, 8, width) for a in range(5)
            ]
            for b in range(-2, 3):
                total = None
                for a in range(-2, 3):
                    value = values[a + 2]
                    if a or b:
                        o = OFFSETS.index((a, b))
                        value = w_ref[r, o : o + 1, lanes][None] * value
                    total = value if total is None else total + value
                sum_ref[b + 2, :, lanes] = total.reshape(fields, width)
        result = sum_ref[2]
        for b in (-2, -1, 1, 2):
            result = result + pltpu.roll(sum_ref[b + 2], (-b) % cols, 1)
        if keep:
            g_ref[r] = result
        own = source_ref[r + 2 - shift]
        if chunks:
            own_ref[r] = own
        weighted = deg_ref[pl.ds(r, 1), :] * own
        left, position = [], 0
        for which in order:
            if which == "v":
                left.append(split(own))
            else:
                left.append(split(others[position][r]))
                position += 1
        left = jnp.concatenate([p[0] for p in left] + [p[1] for p in left], 0)
        graph_pair, degree_pair = split(result), split(weighted)
        right = jnp.concatenate(
            [graph_pair[0], degree_pair[0], graph_pair[1], degree_pair[1]], 0
        )
        return acc + lax.dot_general(
            left, right, (((1,), (1,)), ((), ())), preferred_element_type=f32
        )

    start = jnp.zeros((2 * parts * fields, 4 * fields), f32)
    if part == "outer":
        acc = start
        for r in (0, 1, depth - 2, depth - 1):
            acc = one_row(r, acc)
    else:
        skip = 2 if part == "inner" else 0
        acc = lax.fori_loop(skip, depth - skip, one_row, start, unroll=UNROLL)
    half = parts * fields
    acc_ref[...] = jnp.zeros(acc_ref.shape, f32)
    acc_ref[:, 0 : 4 * fields] = acc[:half] + acc[half:]
    both = acc_ref[...]
    both = both + pltpu.roll(both, LANES - 2 * fields, 1)
    lane = lax.broadcasted_iota(jnp.int32, both.shape, 1)
    both = jnp.where(lane < 2 * fields, both, 0.0)
    if lane_shift:
        both = pltpu.roll(both, lane_shift, 1)
    gram_ref[...] = both


def apply_graph(order, keep, lane_shift, fields_in, w, deg, *others, info=None, part="all"):
    depth, cols = deg.shape
    fields = fields_in[0].shape[1]
    parts = len(order)
    chunks = len(fields_in) if info is not None else 0
    out_shape = [room(depth, fields, cols)] * (int(keep) + int(chunks > 0))
    out_shape += [room(parts * fields, LANES)]
    args = ((info,) if chunks else ()) + tuple(fields_in) + (w, deg) + others
    return pl.pallas_call(
        functools.partial(graph_kernel, order, keep, lane_shift, chunks, part),
        out_shape=tuple(out_shape),
        in_specs=[SMEM] * int(chunks > 0) + [VMEM] * (len(args) - int(chunks > 0)),
        out_specs=(VMEM,) * len(out_shape),
        scratch_shapes=[
            pltpu.VMEM((8 if part == "inner" else depth + 4, fields, cols), f32),
            pltpu.VMEM((parts * fields, LANES), f32),
            pltpu.VMEM((5, fields, cols), f32),
        ],
        compiler_params=params(w, deg, *fields_in, *others, *out_shape, room(depth + 9, fields, cols)),
        cost_estimate=cost(50 * fields * depth * cols * 4, 4 * cols * depth * (25 + 3 * fields)),
        name="graph_" + "".join(order) + "_" + part,
    )(*args)


def solve_rayleigh(affinity, mass):
    fields = mass.shape[0]
    row = lax.broadcasted_iota(jnp.int32, (fields, fields), 0)
    for k in range(fields):
        inverse = 1.0 / mass[k : k + 1, k : k + 1]
        column = mass[:, k : k + 1]
        mass_row = mass[k : k + 1, :] * inverse
        affinity_row = affinity[k : k + 1, :] * inverse
        affinity = jnp.where(row == k, affinity_row, affinity - column * affinity_row)
        mass = jnp.where(row == k, mass_row, mass - column * mass_row)
    return affinity


def residual_kernel(gram_ref, g_ref, x_ref, deg_ref, eps_ref, last_ref, high_ref, low_ref, f_ref, ends_ref):
    depth, fields, cols = x_ref.shape
    gram = gram_ref[...]
    affinity = pltpu.roll(gram, LANES - 4 * fields, 1)[:, :fields]
    mass = pltpu.roll(gram, LANES - 5 * fields, 1)[:, :fields]
    ray = split3(solve_rayleigh(affinity, mass).T)
    left = jnp.concatenate([ray[i] for i in (0, 0, 0, 1, 1, 2)], 1)
    block = math.gcd(depth, 16)
    dot = functools.partial(jnp.dot, preferred_element_type=f32)

    def one_block(i, _):
        start = pl.multiple_of(i * block, block)
        rows = []
        for r in range(block):
            piece = split3(x_ref[start + r] * deg_ref[pl.ds(start + r, 1), :])
            right = jnp.concatenate([piece[i] for i in (0, 1, 2, 0, 1, 0)], 0)
            rows.append(g_ref[start + r] - dot(left, right))
        high, low = split(jnp.concatenate(rows, 0))
        result = dot(high, high_ref[...]) + dot(high, low_ref[...]) + dot(low, high_ref[...])
        f_ref[pl.ds(start, block)] = result.reshape(block, fields, cols)
        return 0

    lax.fori_loop(0, depth // block, one_block, 0)

    def sweep(i, carry):
        up, down = carry
        keep = eps_ref[pl.ds(jnp.maximum(i - 1, 0), 1), :]
        return f_ref[depth - 1 - i] + (up - keep * up), f_ref[i] + (down - keep * down)

    zero = jnp.zeros((fields, cols), f32)
    up, down = lax.fori_loop(0, depth, sweep, (zero, zero), unroll=UNROLL)
    last = last_ref[...]
    ends_ref[0] = up * last
    ends_ref[1] = down * last


def residual_spectrum(gram, g, x, deg, eps, last, high, low):
    depth, fields, cols = x.shape
    out_shape = (room(depth, fields, cols), room(2, fields, cols))
    return pl.pallas_call(
        residual_kernel,
        out_shape=out_shape,
        in_specs=[VMEM] * 8,
        out_specs=(VMEM,) * 2,
        compiler_params=params(g, x, deg, high, low, *out_shape, extra=12 * 2**20),
        cost_estimate=cost(6 * depth * fields * cols * cols, 12 * depth * fields * cols),
        name="residual_spectrum",
    )(gram, g, x, deg, eps, last, high, low)


def merge_kernel(level, count, last, info_ref, gain_ref, cross_ref, *refs):
    groups, outs = [ref[...] for ref in refs[:count]], refs[count:]
    place = info_ref[0] >> level

    def join(own, other, step, keep):
        right = ((place >> step) & 1) == 1
        lower, upper = jnp.where(right, other, own), jnp.where(right, own, other)
        row = slice(level + step, level + step + 1)
        g = (lower[1] - upper[0]) * gain_ref[row, :]
        moved = g * cross_ref[row, :]
        return g, jnp.stack([lower[0] - moved, upper[1] + moved]) if keep else None

    g, ends = join(groups[0], groups[1], 0, count == 4 or not last)
    outs[0][...] = g
    if count == 4:
        _, others = join(groups[2], groups[3], 0, True)
        g, ends = join(ends, others, 1, not last)
        outs[1][...] = g
    if not last:
        outs[-1][...] = ends


def merge(level, last, info, groups, gain, cross):
    _, fields, cols = groups[0].shape
    count = len(groups)
    out_shape = (room(fields, cols),) * (count // 2) + (() if last else (room(2, fields, cols),))
    return pl.pallas_call(
        functools.partial(merge_kernel, level, count, last),
        out_shape=out_shape,
        in_specs=[SMEM] + [VMEM] * (2 + count),
        out_specs=(VMEM,) * len(out_shape),
        compiler_params=params(*groups, *out_shape),
        cost_estimate=cost(10 * fields * cols, 28 * fields * cols),
        name="merge",
    )(info, gain, cross, *groups)


def inverse_kernel(levels, chunks, info_ref, *refs):
    g_refs = refs[:levels]
    f_ref, flux_ref, eps_ref, last_ref, high_ref, low_ref = refs[levels : levels + 6]
    out_ref, head_ref, tail_ref, *piece_refs, u_ref = refs[levels + 6 :]
    depth, fields, cols = f_ref.shape
    width = cols // chunks
    flux_top = jnp.zeros((fields, cols), f32)
    flux_bot = jnp.zeros((fields, cols), f32)
    for level in range(levels):
        g = g_refs[level][...]
        flux_top = flux_top + g * flux_ref[level : level + 1, :]
        flux_bot = flux_bot - g * flux_ref[levels + level : levels + level + 1, :]

    value = f_ref[0] + flux_top
    u_ref[0] = value
    for r in range(1, depth):
        value = f_ref[r] + (value - eps_ref[r - 1 : r, :] * value)
        u_ref[r] = value
    value = (value + flux_bot) * last_ref[...]
    u_ref[depth - 1] = value
    for r in range(depth - 2, -1, -1):
        value = u_ref[r] + value
        value = value - eps_ref[r : r + 1, :] * value
        u_ref[r] = value
    block = math.gcd(depth, 16)

    def one_block(i, _):
        start = i * block
        high, low = split(u_ref[pl.ds(start, block)].reshape(block * fields, cols))
        result = jnp.dot(high, high_ref[...], preferred_element_type=f32)
        result += jnp.dot(high, low_ref[...], preferred_element_type=f32)
        result += jnp.dot(low, high_ref[...], preferred_element_type=f32)
        out_ref[pl.ds(start, block)] = result.reshape(block, fields, cols)
        for d in range(chunks):
            lane = pl.multiple_of(info_ref[1 + d] * width, width)
            piece_refs[d][pl.ds(start, block)] = out_ref[pl.ds(start, block), :, pl.ds(lane, width)]
        return 0

    lax.fori_loop(0, depth // block, one_block, 0)
    head_ref[...] = out_ref[0:2]
    tail_ref[...] = out_ref[depth - 2 : depth]


def row_inverse(info, gs, f, flux, eps, last, high, low, chunks):
    depth, fields, cols = f.shape
    out_shape = (room(depth, fields, cols),) + (room(2, fields, cols),) * 2
    out_shape += (room(depth, fields, cols // chunks),) * chunks
    return pl.pallas_call(
        functools.partial(inverse_kernel, len(gs), chunks),
        out_shape=out_shape,
        in_specs=[SMEM] + [VMEM] * (len(gs) + 6),
        out_specs=(VMEM,) * len(out_shape),
        scratch_shapes=[pltpu.VMEM((depth, fields, cols), f32)],
        compiler_params=params(*gs, f, high, low, *out_shape, f, extra=12 * 2**20),
        cost_estimate=cost(6 * depth * fields * cols * cols, 4 * cols * (2 * depth * fields + cols)),
        name="row_inverse",
    )(info, *gs, f, flux, eps, last, high, low)


def hdot(a, b, contract):
    return lax.dot_general(
        a, b, ((contract[0], contract[1]), ((), ())), precision=highest, preferred_element_type=f32
    )


def cholesky_apply(matrix, target):
    size = matrix.shape[0]
    step = 8
    mats = [matrix[i : i + step] for i in range(0, size, step)]
    tars = [target[i : i + step] for i in range(0, size, step)]
    local_row = lax.broadcasted_iota(jnp.int32, (step, 1), 0)
    for k in range(size):
        own, inner = divmod(k, step)
        pivot_row = mats[own][inner : inner + 1, :]
        target_row = tars[own][inner : inner + 1, :]
        inverse = 1.0 / pivot_row[:, k : k + 1]
        for i in range(own, size // step):
            factor = mats[i][:, k : k + 1] * inverse
            if i == own:
                factor = jnp.where(local_row > inner, factor, 0.0)
            mats[i] = mats[i] - factor * pivot_row
            tars[i] = tars[i] - factor * target_row
    matrix = jnp.concatenate(mats, 0)
    target = jnp.concatenate(tars, 0)
    row = lax.broadcasted_iota(jnp.int32, matrix.shape, 0)
    col = lax.broadcasted_iota(jnp.int32, matrix.shape, 1)
    pivots = jnp.sum(jnp.where(row == col, matrix, 0.0), 1, keepdims=True)
    return target * (1.0 / jnp.sqrt(pivots))


def ritz_kernel(fields, pixel_total, first_ref, second_ref, ritz_ref, coeff_ref):
    size = 3 * fields
    gram = second_ref[...]
    first = first_ref[...]
    row = lax.broadcasted_iota(jnp.int32, (LANES, size), 0)
    col = lax.broadcasted_iota(jnp.int32, (LANES, size), 1)
    place_a = jnp.zeros((LANES, size), jnp.bool_)
    place_b = jnp.zeros((LANES, size), jnp.bool_)
    for group, target in ((4, 0), (0, 1), (2, 2)):
        inside = (col >= target * fields) & (col < (target + 1) * fields)
        place_a = place_a | (inside & (row - group * fields == col - target * fields))
        place_b = place_b | (inside & (row - (group + 1) * fields == col - target * fields))
    place_a = place_a.astype(f32)
    place_b = place_b.astype(f32)
    srow = lax.broadcasted_iota(jnp.int32, (size, size), 0)
    scol = lax.broadcasted_iota(jnp.int32, (size, size), 1)
    same = srow // fields == scol // fields
    eye = (srow == scol).astype(f32)

    def assemble(place):
        part = hdot(gram, place, ((1,), (0,)))
        top = hdot(first, place, ((1,), (0,)))
        part = jnp.concatenate([part[:fields] + top, part[fields:]], 0)
        both = part + part.T
        return jnp.where(same, 0.5 * both, both)

    big_a = assemble(place_a)
    big_b = assemble(place_b)
    diagonal = big_b * eye
    scale_col = 1.0 / jnp.sqrt(jnp.sum(diagonal, 1, keepdims=True) + 1e-6)
    scale_row = 1.0 / jnp.sqrt(jnp.sum(diagonal, 0, keepdims=True) + 1e-6)
    norm_a = scale_col * big_a * scale_row
    norm_b = scale_col * big_b * scale_row
    inverse = cholesky_apply(norm_b, eye)
    reduced = hdot(hdot(inverse, norm_a, ((1,), (0,))), inverse, ((1,), (1,)))
    reduced = 0.5 * (reduced + reduced.T) + ritz_offset * eye
    power = hdot(reduced, reduced, ((1,), (0,)))
    power = hdot(power, power, ((1,), (0,)))
    images = power[:fields]
    basis = cholesky_apply(hdot(images, images, ((1,), (1,))), images)
    images = hdot(basis, power, ((1,), (0,)))
    basis = cholesky_apply(hdot(images, images, ((1,), (1,))), images)
    images = hdot(basis, reduced, ((1,), (0,)))
    ones = jnp.ones((8, size), f32)
    ritz_ref[...] = hdot(ones, basis * images, ((1,), (1,)))[0:1] - ritz_offset
    coeff_ref[...] = math.sqrt(pixel_total) * scale_col * hdot(inverse, basis, ((0,), (1,)))


def ritz_step(first, second, fields, pixel_total):
    return pl.pallas_call(
        functools.partial(ritz_kernel, fields, pixel_total),
        out_shape=(
            room(1, fields),
            room(3 * fields, fields),
        ),
        in_specs=[pl.BlockSpec(memory_space=pltpu.VMEM)] * 2,
        out_specs=(pl.BlockSpec(memory_space=pltpu.VMEM),) * 2,
        compiler_params=params(),
        cost_estimate=cost(1 << 25, 1 << 16),
        name="ritz",
    )(first, second)


def combine_kernel(count, begun, info_ref, coeff_ref, x_ref, p_ref, *refs):
    pieces, refs = refs[:count], refs[count:]
    if begun:
        _, _, high_ref, low_ref, block_ref, direction_ref, h_ref = refs
    else:
        block_ref, direction_ref, high_ref, low_ref, h_ref = refs
    fields = x_ref.shape[0]
    width = x_ref.shape[2]
    group = 8 * fields

    @pl.when((pl.program_id(0) == 0) & (not begun))
    def _():
        r = lax.broadcasted_iota(jnp.int32, (group, fields), 0)
        c = lax.broadcasted_iota(jnp.int32, (group, fields), 1)
        rows_of = (r // 8 == c).astype(f32)
        f = lax.broadcasted_iota(jnp.int32, (fields, group), 0)
        q = lax.broadcasted_iota(jnp.int32, (fields, group), 1)
        row = lax.broadcasted_iota(jnp.int32, (group, group), 0)
        col = lax.broadcasted_iota(jnp.int32, (group, group), 1)
        coeffs = coeff_ref[...]
        for part in range(3):
            own = coeffs[part * fields : (part + 1) * fields, :].T
            if part == 1:
                cols_of, same = q % fields == f, row % 8 == col // fields
            else:
                cols_of, same = q // 8 == f, row % 8 == col % 8
            wide = hdot(own, cols_of.astype(f32), ((1,), (0,)))
            wide = jnp.where(same, hdot(rows_of, wide, ((1,), (0,))), 0.0)
            lanes = slice(part * group, (part + 1) * group)
            high_ref[:, lanes], low_ref[:, lanes] = split(wide)

    for d in range(count):

        @pl.when(pl.program_id(0) == d)
        def _(d=d):
            h_ref[...] = pieces[d][...]

    dot = functools.partial(jnp.dot, preferred_element_type=f32)
    for t in range(x_ref.shape[1] // 8):
        rows = slice(8 * t, 8 * t + 8)
        x = split(x_ref[:, rows, :].reshape(group, width))
        h = split(h_ref[rows].reshape(group, width))
        p = split(p_ref[:, rows, :].reshape(group, width))
        hp = [jnp.concatenate([h[i], p[i]], 0) for i in range(2)]
        x_high, x_low = high_ref[:, :group], low_ref[:, :group]
        hp_high, hp_low = high_ref[:, group:], low_ref[:, group:]
        direction = dot(hp_high, hp[0]) + dot(hp_low, hp[0]) + dot(hp_high, hp[1])
        x_left = jnp.concatenate([x_high, x_high, x_low], 1)
        block = direction + dot(x_left, jnp.concatenate([x[0], x[1], x[0]], 0))
        block_ref[:, rows, :] = block.reshape(fields, 8, width)
        direction_ref[:, rows, :] = direction.reshape(fields, 8, width)


def combine(info, coeffs, x, p, pieces, chunks, first=0, begun=()):
    fields, rows, width = x.shape
    count = len(pieces)
    depth = rows // chunks
    spec = pl.BlockSpec((fields, depth, width), lambda i, s: (0, s[1 + chunks + first + i], 0))
    whole = pl.BlockSpec((depth, fields, width), lambda i, s: (0, 0, 0))
    left = pl.BlockSpec(memory_space=pl.ANY)
    wide = (8 * fields, 24 * fields)
    same = pl.BlockSpec(wide, lambda i, s: (0, 0))
    again = (jax.ShapeDtypeStruct(wide, bf16),) * 2
    return pl.pallas_call(
        functools.partial(combine_kernel, count, bool(begun)),
        out_shape=(room(fields, rows, width),) * 2 + (() if begun else again),
        grid_spec=pltpu.PrefetchScalarGridSpec(
            num_scalar_prefetch=1,
            grid=(count,),
            in_specs=[pl.BlockSpec(coeffs.shape, lambda i, s: (0, 0)), spec, spec]
            + [whole] * count
            + ([left, left, same, same] if begun else []),
            out_specs=(spec, spec) + (() if begun else (same, same)),
            scratch_shapes=[pltpu.VMEM((depth, fields, width), f32)],
        ),
        input_output_aliases={4 + count + i: i for i in range(2)} if begun else {},
        compiler_params=params(room(16 * depth, fields, width)),
        cost_estimate=cost(50 * count * depth * fields * width, 20 * count * depth * fields * width),
        name="combine",
    )(info, coeffs, x, p, *pieces, *begun)


def ring_order(count):
    half = count // 2
    return [*range(half), *reversed(range(half, count))] if count > 1 else [0]


@functools.lru_cache(None)
def device_table(strips, chunks):
    order = ring_order(chunks)
    place = [order.index(c) for c in range(chunks)]
    table = []
    for device in range(strips):
        row, col = divmod(device, chunks)
        others = [col ^ d for d in range(chunks)]
        table.append([row * chunks + place[col], *others, *[place[c] for c in others]])
    return np.asarray(table, np.int32)


def local(intensity, start_block, old_direction):
    fields, height, width = start_block.shape
    chunks = lax.axis_size("col")
    row_count = lax.axis_size("row")
    strips = row_count * chunks
    depth = height // chunks
    rows, cols = strips * depth, chunks * width
    device = lax.axis_index("row") * chunks + lax.axis_index("col")
    levels = strips.bit_length() - 1
    order = ring_order(chunks)
    owner = [(s // chunks) * chunks + order[s % chunks] for s in range(strips)]

    table = device_table(strips, chunks)
    eps, last, gain, cross, top_all, bot_all = row_tables(strips, depth, cols)
    by_device = np.concatenate([top_all[table[:, 0]], bot_all[table[:, 0]]], 1)
    high, low = (jnp.asarray(t) for t in cosine_tables(cols))
    high_t, low_t = (jnp.asarray(t.T.copy()) for t in cosine_tables(cols))
    eps, last, gain, cross = (jnp.asarray(t) for t in (eps, last, gain, cross))
    info = lax.dynamic_index_in_dim(jnp.asarray(table), device, 0, False)
    flux = lax.dynamic_index_in_dim(jnp.asarray(by_device), device, 0, False)

    first = chunks.bit_length() - 1
    row_groups = [[first]] + [[*range(b, min(b + 2, levels))] for b in range(first + 1, levels, 2)]
    col_groups = [[*range(b, min(b + 2, first))] for b in range(0, first, 2)]

    def add_up(value, groups, late=None):
        for group in groups:
            away = [1 << b for b in group]
            away += [sum(away)] if len(away) == 2 else []
            got = [lax.ppermute(value, BOTH, [(i, i ^ m) for i in range(strips)]) for m in away]
            if late is not None and group is groups[-1]:
                late, got = lax.optimization_barrier((late, got))
            value = value + got[0] + (got[1] + got[2]) if len(got) == 3 else value + got[0]
        return value, late

    def away(piece, d):
        return lax.ppermute(piece, "col", [(c, c ^ d) for c in range(chunks)])

    def exchange(pieces):
        return [pieces[0]] + [away(pieces[d], d) for d in range(1, chunks)]

    head, tail = edges(start_block, old_direction, intensity)
    above = lax.ppermute(tail, "row", [(i, i + 1) for i in range(row_count - 1)])
    below = lax.ppermute(head, "row", [(i + 1, i) for i in range(row_count - 1)])
    x_pieces = pack(info, start_block, intensity, chunks)
    x_pieces = exchange(fill(info, above, below, x_pieces, 0, True))
    p_pieces = pack(info, old_direction, None, chunks)
    p_own, *p_early, p_late = fill(info, above, below, p_pieces, fields, False)
    p_early = [away(piece, d) for d, piece in enumerate(p_early, 1)]
    p_late, x_pieces[1] = lax.optimization_barrier((p_late, x_pieces[1]))
    p_pieces = [p_own, *p_early, away(p_late, chunks - 1)]
    x_pieces, flux = lax.optimization_barrier((x_pieces, flux))
    w, deg = make_weights(info, x_pieces, depth, rows)
    graph_x, x, gram_x = apply_graph(("v",), True, 4 * fields, x_pieces, w, deg, info=info)
    gram_x, _ = add_up(gram_x, row_groups)
    gram_x, p_pieces = lax.optimization_barrier((gram_x, p_pieces))
    gram_x, _ = add_up(gram_x, col_groups)
    f, ends = residual_spectrum(gram_x, graph_x, x, deg, eps, last, high_t, low_t)

    gs = []
    groups = col_groups + row_groups
    for group in groups:
        level = group[0]
        found = {0: ends}
        for d in range(1, 1 << len(group)):
            place = (int(table[d << level, 0]) ^ int(table[0, 0])) >> level
            pairs = [(i, i ^ (d << level)) for i in range(strips)]
            found[place & (1 << len(group)) - 1] = lax.ppermute(ends, BOTH, pairs)
        is_last = group is groups[-1]
        *new, ends = merge(level, is_last, info, [found[e] for e in sorted(found)], gain, cross) + (
            (None,) if is_last else ()
        )
        gs += new
        if group is groups[-2]:
            p_pieces, ends = lax.optimization_barrier((p_pieces, ends))
    p, gram_p = apply_graph(("x", "v"), False, 2 * fields, p_pieces, w, deg, x, info=info)
    gs[-1], gram_p = lax.optimization_barrier((gs[-1], gram_p))

    h, head, tail, *h_pieces = row_inverse(info, gs, f, flux, eps, last, high, low, chunks)
    h_above = lax.ppermute(tail, BOTH, [(owner[s], owner[s + 1]) for s in range(strips - 1)])
    h_below = lax.ppermute(head, BOTH, [(owner[s + 1], owner[s]) for s in range(strips - 1)])
    h_own, *h_early, h_late = h_pieces
    (gram_inner,) = apply_graph(("x", "v", "p"), False, 0, (h,), w, deg, x, p, part="inner")
    h_early, h_above, h_below, gram_inner = lax.optimization_barrier(
        (h_early, h_above, h_below, gram_inner)
    )
    h_early = [away(piece, d) for d, piece in enumerate(h_early, 1)]
    (gram_outer,) = apply_graph(
        ("x", "v", "p"), False, 0, (h, h_above, h_below), w, deg, x, p, part="outer"
    )
    zero = jnp.zeros((fields, LANES), f32)
    gram = gram_inner + gram_outer + jnp.concatenate([gram_p[:fields], zero, gram_p[fields:]], 0)
    gram, _ = add_up(gram, row_groups)
    gram, h_early = lax.optimization_barrier((gram, h_early))
    gram, h_late = add_up(gram, col_groups, h_late)
    h_late = away(h_late, chunks - 1)
    ritz, coeffs = ritz_step(gram_x, gram, fields, rows * cols)
    given = info, coeffs, start_block, old_direction
    begun = combine(*given, [h_own, *h_early], chunks)
    new_block, new_direction = combine(*given, [h_late], chunks, chunks - 1, begun)
    return new_block, new_direction, ritz.reshape(fields)


def solution(mesh):
    return jax.shard_map(
        local,
        mesh=mesh,
        in_specs=(P("row", "col"), P(None, "row", "col"), P(None, "row", "col")),
        out_specs=(P(None, "row", "col"), P(None, "row", "col"), P()),
        check_vma=False,
    )
```

```python
import functools
import math

import jax
import jax.numpy as jnp
import numpy as np
from jax import lax
from jax.experimental import pallas as pl
from jax.experimental.pallas import tpu as pltpu
from jax.sharding import PartitionSpec as P

SWEEPS = 8
beta_value = 4.0
spatial_rate = 0.25
shift_numerator = 16.0
ritz_offset = 1.5
far = 1e4
highest = lax.Precision.HIGHEST
f32 = jnp.float32
bf16 = jnp.bfloat16
BOTH = ("row", "col")
LANES = 128
UNROLL = 4
VMEM = pl.BlockSpec(memory_space=pltpu.VMEM)
SMEM = pl.BlockSpec(memory_space=pltpu.SMEM)
OFFSETS = [(a, b) for a in range(-2, 3) for b in range(-2, 3)]


def params(*arrays, extra=4 * 2**20):
    total = extra
    for a in arrays:
        shape = (1, 1) + tuple(a.shape)
        padded = math.prod(shape[:-2]) * (-(-shape[-2] // 8) * 8) * (-(-shape[-1] // LANES) * LANES)
        total += padded * a.dtype.itemsize
    return pltpu.CompilerParams(vmem_limit_bytes=total)


def room(*shape):
    return jax.ShapeDtypeStruct(shape, f32)


def cost(flops, nbytes):
    return pl.CostEstimate(flops=int(flops), bytes_accessed=int(nbytes), transcendentals=0)


@functools.lru_cache(None)
def cosine_tables(length):
    k = np.arange(length)[:, None]
    n = np.arange(length)[None, :]
    table = np.cos(np.pi * ((2 * n + 1) * k % (4 * length)) / (2 * length)) * np.sqrt(2.0 / length)
    table[0] *= np.sqrt(0.5)
    high = table.astype(jnp.bfloat16)
    low = (table - high.astype(np.float64)).astype(jnp.bfloat16)
    return high, low


def ratio_sinh(a, b):
    return np.exp(a - b) * (1 - np.exp(-2 * a)) / (1 - np.exp(-2 * b))


@functools.lru_cache(None)
def row_tables(strips, depth, cols):
    rows = strips * depth
    lam = 4 * np.sin(np.pi * np.arange(cols) / (2 * cols)) ** 2
    mu = lam + shift_numerator / (rows * cols)
    excess = np.zeros((depth, cols))
    excess[0] = mu
    for r in range(1, depth):
        last = r == depth - 1
        prev = excess[r - 1]
        excess[r] = mu + prev / (1 + prev) - (1.0 if last else 0.0) + (0.0 if last else 0.0)
        if last:
            excess[r] = mu + prev / (1 + prev)
    eps = excess / (1 + excess)
    last_inv = 1.0 / (mu + eps[depth - 2])
    theta = 2 * np.arcsinh(np.sqrt(mu) / 2)
    levels = strips.bit_length() - 1
    gain, cross = [], []
    top = np.zeros((strips, levels, cols))
    bot = np.zeros((strips, levels, cols))
    for level in range(levels):
        m = 1 << level
        n = m * depth
        half = np.sinh(theta / 2)
        b = n * theta
        a = (n - 0.5) * theta
        end_end = np.exp(a - b) * (1 + np.exp(-2 * a)) / (1 - np.exp(-2 * b)) / (2 * half)
        first_last = 2 * np.cosh(theta / 2) * np.exp(-b) / (1 - np.exp(-2 * b)) / (2 * half)
        gain.append(1 / (1 + 2 * end_end))
        cross.append(first_last)
        rho = [ratio_sinh(p * depth * theta, b) for p in range(m + 1)]
        for s in range(strips):
            p = s % m
            if (s >> level) & 1:
                top[s, level], bot[s, level] = rho[m - p], rho[m - 1 - p]
            else:
                top[s, level], bot[s, level] = rho[p], rho[p + 1]
    cast = lambda x: np.asarray(x, np.float32)
    return cast(eps), cast(last_inv[None]), cast(gain), cast(cross), cast(top), cast(bot)


def split(x):
    high = x.astype(bf16)
    return high, (x - high.astype(f32)).astype(bf16)


def split3(x):
    high = x.astype(bf16)
    rest = x - high.astype(f32)
    middle = rest.astype(bf16)
    return high, middle, (rest - middle.astype(f32)).astype(bf16)


def image_rows(count, fields):
    return -(-count // fields)


def spread(info_ref, chunk_refs, target):
    width = chunk_refs[0].shape[-1]
    count = target.shape[0]
    for d, ref in enumerate(chunk_refs):
        start = pl.multiple_of(info_ref[1 + d] * width, width)
        if len(target.shape) == 3:
            target[:, :, pl.ds(start, width)] = ref[0:count]
        else:
            below = ref[ref.shape[0] - image_rows(count, ref.shape[1]) :]
            target[:, pl.ds(start, width)] = below.reshape(-1, width)[:count]


def edges_kernel(x_top, x_bot, p_top, p_bot, i_top, i_bot, head_ref, tail_ref):
    fields, _, _ = x_top.shape
    for out_ref, rows, refs in (
        (head_ref, slice(0, 2), (x_top, p_top, i_top)),
        (tail_ref, slice(6, 8), (x_bot, p_bot, i_bot)),
    ):
        for f in range(fields):
            out_ref[:, f, :] = refs[0][f, rows, :]
            out_ref[:, fields + f, :] = refs[1][f, rows, :]
        out_ref[:, 2 * fields, :] = refs[2][rows, :]


def edges(x, p, image):
    fields, height, width = x.shape
    bottom = height // 8 - 1
    top = pl.BlockSpec((fields, 8, width), lambda i: (0, 0, 0))
    bot = pl.BlockSpec((fields, 8, width), lambda i: (0, bottom, 0))
    image_top = pl.BlockSpec((8, width), lambda i: (0, 0))
    image_bot = pl.BlockSpec((8, width), lambda i: (bottom, 0))
    out = pl.BlockSpec((2, 2 * fields + 1, width), lambda i: (0, 0, 0))
    return pl.pallas_call(
        edges_kernel,
        grid=(1,),
        out_shape=(room(2, 2 * fields + 1, width),) * 2,
        in_specs=[top, bot, top, bot, image_top, image_bot],
        out_specs=(out, out),
        compiler_params=pltpu.CompilerParams(vmem_limit_bytes=56 * 2**20),
        cost_estimate=cost(0, 8 * 4 * fields * width * 4),
        name="edges",
    )(x, x, p, p, image, image)


def pack_kernel(chunks, depth, with_image, info_ref, x_ref, *refs):
    fields, height, width = x_ref.shape
    if with_image:
        image_ref, *pieces = refs
    else:
        pieces = refs
    for d in range(chunks):
        place = info_ref[1 + chunks + d]
        start = pl.multiple_of(place * depth, depth)
        before = pl.multiple_of(jnp.maximum(start - 8, 0), 8)
        after = pl.multiple_of(jnp.minimum(start + depth, height - 8), 8)
        piece = pieces[d]
        for f in range(fields):
            piece[2 : 2 + depth, f, :] = x_ref[f, pl.ds(start, depth), :]
            piece[0:2, f, :] = x_ref[f, pl.ds(before, 8), :][6:8]
            piece[2 + depth : 4 + depth, f, :] = x_ref[f, pl.ds(after, 8), :][0:2]
        if with_image:
            rows = jnp.concatenate(
                [
                    image_ref[pl.ds(before, 8), :][6:8],
                    image_ref[pl.ds(start, depth), :],
                    image_ref[pl.ds(after, 8), :][0:2],
                ],
                0,
            )
            count = depth + 4
            for r in range(0, count, fields):
                size = min(fields, count - r)
                piece[depth + 4 + r // fields, 0:size, :] = rows[r : r + size]
            rest = -count % fields
            if rest:
                piece[depth + 3 + image_rows(count, fields), fields - rest :, :] = jnp.zeros(
                    (rest, width), f32
                )


def pack(info, x, image, chunks):
    fields, height, width = x.shape
    depth = height // chunks
    count = depth + 4 + (image_rows(depth + 4, fields) if image is not None else 0)
    args = (x,) if image is None else (x, image)
    return pl.pallas_call(
        functools.partial(pack_kernel, chunks, depth, image is not None),
        out_shape=(room(count, fields, width),) * chunks,
        in_specs=[SMEM] + [VMEM] * len(args),
        out_specs=(VMEM,) * chunks,
        compiler_params=params(*args, *(room(count, fields, width),) * chunks),
        cost_estimate=cost(0, 8 * fields * height * width),
        name="pack",
    )(info, *args)


def fill_kernel(chunks, depth, first, with_image, info_ref, above_ref, below_ref, *refs):
    pieces = refs[chunks:]
    fields = pieces[0].shape[1]
    for d in range(chunks):
        place = info_ref[1 + chunks + d]
        piece = pieces[d]
        for which, rows_ref, row in ((0, above_ref, 0), (chunks - 1, below_ref, depth + 2)):

            @pl.when(place == which)
            def _(piece=piece, rows_ref=rows_ref, row=row):
                piece[row : row + 2] = rows_ref[:, first : first + fields, :]
                if with_image:
                    for i in range(2):
                        line = depth + 4 + (row + i) // fields
                        at = (row + i) % fields
                        image = rows_ref[i, 2 * fields : 2 * fields + 1, :]
                        piece[line, at : at + 1, :] = image


def fill(info, above, below, pieces, first, with_image):
    chunks = len(pieces)
    count, fields, width = pieces[0].shape
    depth = count - 4
    if with_image:
        depth = next(n for n in range(1, count) if n + 4 + image_rows(n + 4, fields) == count)
    return pl.pallas_call(
        functools.partial(fill_kernel, chunks, depth, first, with_image),
        out_shape=(room(count, fields, width),) * chunks,
        in_specs=[SMEM] + [VMEM] * (2 + chunks),
        out_specs=(VMEM,) * chunks,
        input_output_aliases={3 + d: d for d in range(chunks)},
        compiler_params=params(*pieces),
        cost_estimate=cost(0, 16 * fields * width),
        name="fill",
    )(info, above, below, *pieces)


def weights_kernel(chunks, total_rows, info_ref, *rest):
    chunk_refs, (w_ref, deg_ref, image_ref) = rest[:chunks], rest[chunks:]
    depth, cols = deg_ref.shape
    spread(info_ref, chunk_refs, image_ref)
    row = lax.broadcasted_iota(jnp.int32, (2, cols), 0) + info_ref[0] * depth
    image_ref[0:2, :] = jnp.where(row - 2 >= 0, image_ref[0:2, :], far)
    inside = row + depth < total_rows
    image_ref[2 + depth :, :] = jnp.where(inside, image_ref[2 + depth :, :], far)
    center = image_ref[2 : 2 + depth, :]
    col = lax.broadcasted_iota(jnp.int32, (depth, cols), 1)
    degree = jnp.zeros((depth, cols), f32)
    for b in range(-2, 3):
        moved = center
        if b:
            col_ok = (col - b >= 0) & (col - b < cols)
            moved = jnp.where(col_ok, pltpu.roll(center, b % cols, 1), -far)
        total = None
        for a in range(-2, 3):
            if a == 0 and b == 0:
                weight = jnp.ones((depth, cols), f32)
            else:
                contrast = moved - image_ref[2 + a : 2 + a + depth, :]
                weight = jnp.exp(-beta_value * contrast * contrast - spatial_rate * (a * a + b * b))
            w_ref[:, OFFSETS.index((a, b)), :] = weight
            total = weight if total is None else total + weight
        degree = degree + (pltpu.roll(total, (-b) % cols, 1) if b else total)
    deg_ref[...] = degree


def make_weights(info, pieces, depth, total_rows):
    cols = pieces[0].shape[2] * len(pieces)
    return pl.pallas_call(
        functools.partial(weights_kernel, len(pieces), total_rows),
        out_shape=(room(depth, 25, cols), room(depth, cols)),
        in_specs=[SMEM] + [VMEM] * len(pieces),
        out_specs=(VMEM,) * 2,
        scratch_shapes=[pltpu.VMEM((depth + 4, cols), f32)],
        compiler_params=params(*pieces, room(depth, 25, cols), extra=16 * 2**20),
        cost_estimate=cost(60 * depth * cols * 25, 25 * depth * cols * 4),
        name="weights",
    )(info, *pieces)


def graph_kernel(order, keep, lane_shift, chunks, part, *refs):
    if chunks:
        info_ref, chunk_refs, refs = refs[0], refs[1 : 1 + chunks], refs[1 + chunks :]
    elif part == "inner":
        v_ref, *refs = refs
    else:
        v_ref, top_ref, bot_ref, *refs = refs
    (w_ref, deg_ref), refs = refs[:2], refs[2:]
    others, refs = refs[: len(order) - 1], list(refs[len(order) - 1 :])
    g_ref = refs.pop(0) if keep else None
    own_ref = refs.pop(0) if chunks else None
    gram_ref, pad_ref, acc_ref, sum_ref = refs
    depth, cols = deg_ref.shape
    fields = sum_ref.shape[1]
    if chunks:
        spread(info_ref, chunk_refs, pad_ref)
    elif part == "outer":
        pad_ref[0:2] = top_ref[...]
        pad_ref[2:6] = v_ref[0:4]
        pad_ref[depth - 2 : depth + 2] = v_ref[depth - 4 : depth]
        pad_ref[2 + depth : 4 + depth] = bot_ref[...]
    parts = len(order)
    groups = fields // 8
    width = 256
    source_ref, shift = (v_ref, 2) if part == "inner" else (pad_ref, 0)

    def one_row(r, acc):
        for c in range(cols // width):
            lanes = slice(c * width, (c + 1) * width)
            values = [
                source_ref[r + a - shift, :, lanes].reshape(groups, 8, width) for a in range(5)
            ]
            for b in range(-2, 3):
                total = None
                for a in range(-2, 3):
                    value = values[a + 2]
                    if a or b:
                        o = OFFSETS.index((a, b))
                        value = w_ref[r, o : o + 1, lanes][None] * value
                    total = value if total is None else total + value
                sum_ref[b + 2, :, lanes] = total.reshape(fields, width)
        result = sum_ref[2]
        for b in (-2, -1, 1, 2):
            result = result + pltpu.roll(sum_ref[b + 2], (-b) % cols, 1)
        if keep:
            g_ref[r] = result
        own = source_ref[r + 2 - shift]
        if chunks:
            own_ref[r] = own
        weighted = deg_ref[pl.ds(r, 1), :] * own
        left, position = [], 0
        for which in order:
            if which == "v":
                left.append(split(own))
            else:
                left.append(split(others[position][r]))
                position += 1
        left = jnp.concatenate([p[0] for p in left] + [p[1] for p in left], 0)
        graph_pair, degree_pair = split(result), split(weighted)
        right = jnp.concatenate(
            [graph_pair[0], degree_pair[0], graph_pair[1], degree_pair[1]], 0
        )
        return acc + lax.dot_general(
            left, right, (((1,), (1,)), ((), ())), preferred_element_type=f32
        )

    start = jnp.zeros((2 * parts * fields, 4 * fields), f32)
    if part == "outer":
        acc = start
        for r in (0, 1, depth - 2, depth - 1):
            acc = one_row(r, acc)
    else:
        skip = 2 if part == "inner" else 0
        acc = lax.fori_loop(skip, depth - skip, one_row, start, unroll=UNROLL)
    half = parts * fields
    acc_ref[...] = jnp.zeros(acc_ref.shape, f32)
    acc_ref[:, 0 : 4 * fields] = acc[:half] + acc[half:]
    both = acc_ref[...]
    both = both + pltpu.roll(both, LANES - 2 * fields, 1)
    lane = lax.broadcasted_iota(jnp.int32, both.shape, 1)
    both = jnp.where(lane < 2 * fields, both, 0.0)
    if lane_shift:
        both = pltpu.roll(both, lane_shift, 1)
    gram_ref[...] = both


def apply_graph(order, keep, lane_shift, fields_in, w, deg, *others, info=None, part="all"):
    depth, cols = deg.shape
    fields = fields_in[0].shape[1]
    parts = len(order)
    chunks = len(fields_in) if info is not None else 0
    out_shape = [room(depth, fields, cols)] * (int(keep) + int(chunks > 0))
    out_shape += [room(parts * fields, LANES)]
    args = ((info,) if chunks else ()) + tuple(fields_in) + (w, deg) + others
    return pl.pallas_call(
        functools.partial(graph_kernel, order, keep, lane_shift, chunks, part),
        out_shape=tuple(out_shape),
        in_specs=[SMEM] * int(chunks > 0) + [VMEM] * (len(args) - int(chunks > 0)),
        out_specs=(VMEM,) * len(out_shape),
        scratch_shapes=[
            pltpu.VMEM((8 if part == "inner" else depth + 4, fields, cols), f32),
            pltpu.VMEM((parts * fields, LANES), f32),
            pltpu.VMEM((5, fields, cols), f32),
        ],
        compiler_params=params(w, deg, *fields_in, *others, *out_shape, room(depth + 9, fields, cols)),
        cost_estimate=cost(50 * fields * depth * cols * 4, 4 * cols * depth * (25 + 3 * fields)),
        name="graph_" + "".join(order) + "_" + part,
    )(*args)


def solve_rayleigh(affinity, mass):
    fields = mass.shape[0]
    row = lax.broadcasted_iota(jnp.int32, (fields, fields), 0)
    for k in range(fields):
        inverse = 1.0 / mass[k : k + 1, k : k + 1]
        column = mass[:, k : k + 1]
        mass_row = mass[k : k + 1, :] * inverse
        affinity_row = affinity[k : k + 1, :] * inverse
        affinity = jnp.where(row == k, affinity_row, affinity - column * affinity_row)
        mass = jnp.where(row == k, mass_row, mass - column * mass_row)
    return affinity


def residual_kernel(gram_ref, g_ref, x_ref, deg_ref, eps_ref, last_ref, high_ref, low_ref, f_ref, ends_ref):
    depth, fields, cols = x_ref.shape
    gram = gram_ref[...]
    affinity = pltpu.roll(gram, LANES - 4 * fields, 1)[:, :fields]
    mass = pltpu.roll(gram, LANES - 5 * fields, 1)[:, :fields]
    ray = split3(solve_rayleigh(affinity, mass).T)
    left = jnp.concatenate([ray[i] for i in (0, 0, 0, 1, 1, 2)], 1)
    block = math.gcd(depth, 16)
    dot = functools.partial(jnp.dot, preferred_element_type=f32)

    def one_block(i, _):
        start = pl.multiple_of(i * block, block)
        rows = []
        for r in range(block):
            piece = split3(x_ref[start + r] * deg_ref[pl.ds(start + r, 1), :])
            right = jnp.concatenate([piece[i] for i in (0, 1, 2, 0, 1, 0)], 0)
            rows.append(g_ref[start + r] - dot(left, right))
        high, low = split(jnp.concatenate(rows, 0))
        result = dot(high, high_ref[...]) + dot(high, low_ref[...]) + dot(low, high_ref[...])
        f_ref[pl.ds(start, block)] = result.reshape(block, fields, cols)
        return 0

    lax.fori_loop(0, depth // block, one_block, 0)

    def sweep(i, carry):
        up, down = carry
        keep = eps_ref[pl.ds(jnp.maximum(i - 1, 0), 1), :]
        return f_ref[depth - 1 - i] + (up - keep * up), f_ref[i] + (down - keep * down)

    zero = jnp.zeros((fields, cols), f32)
    up, down = lax.fori_loop(0, depth, sweep, (zero, zero), unroll=UNROLL)
    last = last_ref[...]
    ends_ref[0] = up * last
    ends_ref[1] = down * last


def residual_spectrum(gram, g, x, deg, eps, last, high, low):
    depth, fields, cols = x.shape
    out_shape = (room(depth, fields, cols), room(2, fields, cols))
    return pl.pallas_call(
        residual_kernel,
        out_shape=out_shape,
        in_specs=[VMEM] * 8,
        out_specs=(VMEM,) * 2,
        compiler_params=params(g, x, deg, high, low, *out_shape, extra=12 * 2**20),
        cost_estimate=cost(6 * depth * fields * cols * cols, 12 * depth * fields * cols),
        name="residual_spectrum",
    )(gram, g, x, deg, eps, last, high, low)


def merge_kernel(level, count, last, info_ref, gain_ref, cross_ref, *refs):
    groups, outs = [ref[...] for ref in refs[:count]], refs[count:]
    place = info_ref[0] >> level

    def join(own, other, step, keep):
        right = ((place >> step) & 1) == 1
        lower, upper = jnp.where(right, other, own), jnp.where(right, own, other)
        row = slice(level + step, level + step + 1)
        g = (lower[1] - upper[0]) * gain_ref[row, :]
        moved = g * cross_ref[row, :]
        return g, jnp.stack([lower[0] - moved, upper[1] + moved]) if keep else None

    g, ends = join(groups[0], groups[1], 0, count == 4 or not last)
    outs[0][...] = g
    if count == 4:
        _, others = join(groups[2], groups[3], 0, True)
        g, ends = join(ends, others, 1, not last)
        outs[1][...] = g
    if not last:
        outs[-1][...] = ends


def merge(level, last, info, groups, gain, cross):
    _, fields, cols = groups[0].shape
    count = len(groups)
    out_shape = (room(fields, cols),) * (count // 2) + (() if last else (room(2, fields, cols),))
    return pl.pallas_call(
        functools.partial(merge_kernel, level, count, last),
        out_shape=out_shape,
        in_specs=[SMEM] + [VMEM] * (2 + count),
        out_specs=(VMEM,) * len(out_shape),
        compiler_params=params(*groups, *out_shape),
        cost_estimate=cost(10 * fields * cols, 28 * fields * cols),
        name="merge",
    )(info, gain, cross, *groups)


def inverse_kernel(levels, chunks, info_ref, *refs):
    g_refs = refs[:levels]
    f_ref, flux_ref, eps_ref, last_ref, high_ref, low_ref = refs[levels : levels + 6]
    out_ref, head_ref, tail_ref, *piece_refs, u_ref = refs[levels + 6 :]
    depth, fields, cols = f_ref.shape
    width = cols // chunks
    flux_top = jnp.zeros((fields, cols), f32)
    flux_bot = jnp.zeros((fields, cols), f32)
    for level in range(levels):
        g = g_refs[level][...]
        flux_top = flux_top + g * flux_ref[level : level + 1, :]
        flux_bot = flux_bot - g * flux_ref[levels + level : levels + level + 1, :]

    value = f_ref[0] + flux_top
    u_ref[0] = value
    for r in range(1, depth):
        value = f_ref[r] + (value - eps_ref[r - 1 : r, :] * value)
        u_ref[r] = value
    value = (value + flux_bot) * last_ref[...]
    u_ref[depth - 1] = value
    for r in range(depth - 2, -1, -1):
        value = u_ref[r] + value
        value = value - eps_ref[r : r + 1, :] * value
        u_ref[r] = value
    block = math.gcd(depth, 16)

    def one_block(i, _):
        start = i * block
        high, low = split(u_ref[pl.ds(start, block)].reshape(block * fields, cols))
        result = jnp.dot(high, high_ref[...], preferred_element_type=f32)
        result += jnp.dot(high, low_ref[...], preferred_element_type=f32)
        result += jnp.dot(low, high_ref[...], preferred_element_type=f32)
        out_ref[pl.ds(start, block)] = result.reshape(block, fields, cols)
        for d in range(chunks):
            lane = pl.multiple_of(info_ref[1 + d] * width, width)
            piece_refs[d][pl.ds(start, block)] = out_ref[pl.ds(start, block), :, pl.ds(lane, width)]
        return 0

    lax.fori_loop(0, depth // block, one_block, 0)
    head_ref[...] = out_ref[0:2]
    tail_ref[...] = out_ref[depth - 2 : depth]


def row_inverse(info, gs, f, flux, eps, last, high, low, chunks):
    depth, fields, cols = f.shape
    out_shape = (room(depth, fields, cols),) + (room(2, fields, cols),) * 2
    out_shape += (room(depth, fields, cols // chunks),) * chunks
    return pl.pallas_call(
        functools.partial(inverse_kernel, len(gs), chunks),
        out_shape=out_shape,
        in_specs=[SMEM] + [VMEM] * (len(gs) + 6),
        out_specs=(VMEM,) * len(out_shape),
        scratch_shapes=[pltpu.VMEM((depth, fields, cols), f32)],
        compiler_params=params(*gs, f, high, low, *out_shape, f, extra=12 * 2**20),
        cost_estimate=cost(6 * depth * fields * cols * cols, 4 * cols * (2 * depth * fields + cols)),
        name="row_inverse",
    )(info, *gs, f, flux, eps, last, high, low)


def hdot(a, b, contract):
    return lax.dot_general(
        a, b, ((contract[0], contract[1]), ((), ())), precision=highest, preferred_element_type=f32
    )


def cholesky_apply(matrix, target):
    size = matrix.shape[0]
    step = 8
    mats = [matrix[i : i + step] for i in range(0, size, step)]
    tars = [target[i : i + step] for i in range(0, size, step)]
    local_row = lax.broadcasted_iota(jnp.int32, (step, 1), 0)
    for k in range(size):
        own, inner = divmod(k, step)
        pivot_row = mats[own][inner : inner + 1, :]
        target_row = tars[own][inner : inner + 1, :]
        inverse = 1.0 / pivot_row[:, k : k + 1]
        for i in range(own, size // step):
            factor = mats[i][:, k : k + 1] * inverse
            if i == own:
                factor = jnp.where(local_row > inner, factor, 0.0)
            mats[i] = mats[i] - factor * pivot_row
            tars[i] = tars[i] - factor * target_row
    matrix = jnp.concatenate(mats, 0)
    target = jnp.concatenate(tars, 0)
    row = lax.broadcasted_iota(jnp.int32, matrix.shape, 0)
    col = lax.broadcasted_iota(jnp.int32, matrix.shape, 1)
    pivots = jnp.sum(jnp.where(row == col, matrix, 0.0), 1, keepdims=True)
    return target * (1.0 / jnp.sqrt(pivots))


def ritz_kernel(fields, pixel_total, first_ref, second_ref, ritz_ref, coeff_ref):
    size = 3 * fields
    gram = second_ref[...]
    first = first_ref[...]
    row = lax.broadcasted_iota(jnp.int32, (LANES, size), 0)
    col = lax.broadcasted_iota(jnp.int32, (LANES, size), 1)
    place_a = jnp.zeros((LANES, size), jnp.bool_)
    place_b = jnp.zeros((LANES, size), jnp.bool_)
    for group, target in ((4, 0), (0, 1), (2, 2)):
        inside = (col >= target * fields) & (col < (target + 1) * fields)
        place_a = place_a | (inside & (row - group * fields == col - target * fields))
        place_b = place_b | (inside & (row - (group + 1) * fields == col - target * fields))
    place_a = place_a.astype(f32)
    place_b = place_b.astype(f32)
    srow = lax.broadcasted_iota(jnp.int32, (size, size), 0)
    scol = lax.broadcasted_iota(jnp.int32, (size, size), 1)
    same = srow // fields == scol // fields
    eye = (srow == scol).astype(f32)

    def assemble(place):
        part = hdot(gram, place, ((1,), (0,)))
        top = hdot(first, place, ((1,), (0,)))
        part = jnp.concatenate([part[:fields] + top, part[fields:]], 0)
        both = part + part.T
        return jnp.where(same, 0.5 * both, both)

    big_a = assemble(place_a)
    big_b = assemble(place_b)
    diagonal = big_b * eye
    scale_col = 1.0 / jnp.sqrt(jnp.sum(diagonal, 1, keepdims=True) + 1e-6)
    scale_row = 1.0 / jnp.sqrt(jnp.sum(diagonal, 0, keepdims=True) + 1e-6)
    norm_a = scale_col * big_a * scale_row
    norm_b = scale_col * big_b * scale_row
    inverse = cholesky_apply(norm_b, eye)
    reduced = hdot(hdot(inverse, norm_a, ((1,), (0,))), inverse, ((1,), (1,)))
    reduced = 0.5 * (reduced + reduced.T) + ritz_offset * eye
    power = hdot(reduced, reduced, ((1,), (0,)))
    power = hdot(power, power, ((1,), (0,)))
    images = power[:fields]
    basis = cholesky_apply(hdot(images, images, ((1,), (1,))), images)
    images = hdot(basis, power, ((1,), (0,)))
    basis = cholesky_apply(hdot(images, images, ((1,), (1,))), images)
    images = hdot(basis, reduced, ((1,), (0,)))
    ones = jnp.ones((8, size), f32)
    ritz_ref[...] = hdot(ones, basis * images, ((1,), (1,)))[0:1] - ritz_offset
    coeff_ref[...] = math.sqrt(pixel_total) * scale_col * hdot(inverse, basis, ((0,), (1,)))


def ritz_step(first, second, fields, pixel_total):
    return pl.pallas_call(
        functools.partial(ritz_kernel, fields, pixel_total),
        out_shape=(
            room(1, fields),
            room(3 * fields, fields),
        ),
        in_specs=[pl.BlockSpec(memory_space=pltpu.VMEM)] * 2,
        out_specs=(pl.BlockSpec(memory_space=pltpu.VMEM),) * 2,
        compiler_params=params(),
        cost_estimate=cost(1 << 25, 1 << 16),
        name="ritz",
    )(first, second)


def combine_kernel(count, begun, info_ref, coeff_ref, x_ref, p_ref, *refs):
    pieces, refs = refs[:count], refs[count:]
    if begun:
        _, _, high_ref, low_ref, block_ref, direction_ref, h_ref = refs
    else:
        block_ref, direction_ref, high_ref, low_ref, h_ref = refs
    fields = x_ref.shape[0]
    width = x_ref.shape[2]
    group = 8 * fields

    @pl.when((pl.program_id(0) == 0) & (not begun))
    def _():
        r = lax.broadcasted_iota(jnp.int32, (group, fields), 0)
        c = lax.broadcasted_iota(jnp.int32, (group, fields), 1)
        rows_of = (r // 8 == c).astype(f32)
        f = lax.broadcasted_iota(jnp.int32, (fields, group), 0)
        q = lax.broadcasted_iota(jnp.int32, (fields, group), 1)
        row = lax.broadcasted_iota(jnp.int32, (group, group), 0)
        col = lax.broadcasted_iota(jnp.int32, (group, group), 1)
        coeffs = coeff_ref[...]
        for part in range(3):
            own = coeffs[part * fields : (part + 1) * fields, :].T
            if part == 1:
                cols_of, same = q % fields == f, row % 8 == col // fields
            else:
                cols_of, same = q // 8 == f, row % 8 == col % 8
            wide = hdot(own, cols_of.astype(f32), ((1,), (0,)))
            wide = jnp.where(same, hdot(rows_of, wide, ((1,), (0,))), 0.0)
            lanes = slice(part * group, (part + 1) * group)
            high_ref[:, lanes], low_ref[:, lanes] = split(wide)

    for d in range(count):

        @pl.when(pl.program_id(0) == d)
        def _(d=d):
            h_ref[...] = pieces[d][...]

    dot = functools.partial(jnp.dot, preferred_element_type=f32)
    for t in range(x_ref.shape[1] // 8):
        rows = slice(8 * t, 8 * t + 8)
        x = split(x_ref[:, rows, :].reshape(group, width))
        h = split(h_ref[rows].reshape(group, width))
        p = split(p_ref[:, rows, :].reshape(group, width))
        hp = [jnp.concatenate([h[i], p[i]], 0) for i in range(2)]
        x_high, x_low = high_ref[:, :group], low_ref[:, :group]
        hp_high, hp_low = high_ref[:, group:], low_ref[:, group:]
        direction = dot(hp_high, hp[0]) + dot(hp_low, hp[0]) + dot(hp_high, hp[1])
        x_left = jnp.concatenate([x_high, x_high, x_low], 1)
        block = direction + dot(x_left, jnp.concatenate([x[0], x[1], x[0]], 0))
        block_ref[:, rows, :] = block.reshape(fields, 8, width)
        direction_ref[:, rows, :] = direction.reshape(fields, 8, width)


def combine(info, coeffs, x, p, pieces, chunks, first=0, begun=()):
    fields, rows, width = x.shape
    count = len(pieces)
    depth = rows // chunks
    spec = pl.BlockSpec((fields, depth, width), lambda i, s: (0, s[1 + chunks + first + i], 0))
    whole = pl.BlockSpec((depth, fields, width), lambda i, s: (0, 0, 0))
    left = pl.BlockSpec(memory_space=pl.ANY)
    wide = (8 * fields, 24 * fields)
    same = pl.BlockSpec(wide, lambda i, s: (0, 0))
    again = (jax.ShapeDtypeStruct(wide, bf16),) * 2
    return pl.pallas_call(
        functools.partial(combine_kernel, count, bool(begun)),
        out_shape=(room(fields, rows, width),) * 2 + (() if begun else again),
        grid_spec=pltpu.PrefetchScalarGridSpec(
            num_scalar_prefetch=1,
            grid=(count,),
            in_specs=[pl.BlockSpec(coeffs.shape, lambda i, s: (0, 0)), spec, spec]
            + [whole] * count
            + ([left, left, same, same] if begun else []),
            out_specs=(spec, spec) + (() if begun else (same, same)),
            scratch_shapes=[pltpu.VMEM((depth, fields, width), f32)],
        ),
        input_output_aliases={4 + count + i: i for i in range(2)} if begun else {},
        compiler_params=params(room(16 * depth, fields, width)),
        cost_estimate=cost(50 * count * depth * fields * width, 20 * count * depth * fields * width),
        name="combine",
    )(info, coeffs, x, p, *pieces, *begun)


def ring_order(count):
    half = count // 2
    return [*range(half), *reversed(range(half, count))] if count > 1 else [0]


@functools.lru_cache(None)
def device_table(strips, chunks):
    order = ring_order(chunks)
    place = [order.index(c) for c in range(chunks)]
    table = []
    for device in range(strips):
        row, col = divmod(device, chunks)
        others = [col ^ d for d in range(chunks)]
        table.append([row * chunks + place[col], *others, *[place[c] for c in others]])
    return np.asarray(table, np.int32)


def local(intensity, start_block, old_direction):
    fields, height, width = start_block.shape
    chunks = lax.axis_size("col")
    row_count = lax.axis_size("row")
    strips = row_count * chunks
    depth = height // chunks
    rows, cols = strips * depth, chunks * width
    device = lax.axis_index("row") * chunks + lax.axis_index("col")
    levels = strips.bit_length() - 1
    order = ring_order(chunks)
    owner = [(s // chunks) * chunks + order[s % chunks] for s in range(strips)]

    table = device_table(strips, chunks)
    eps, last, gain, cross, top_all, bot_all = row_tables(strips, depth, cols)
    by_device = np.concatenate([top_all[table[:, 0]], bot_all[table[:, 0]]], 1)
    high, low = (jnp.asarray(t) for t in cosine_tables(cols))
    high_t, low_t = (jnp.asarray(t.T.copy()) for t in cosine_tables(cols))
    eps, last, gain, cross = (jnp.asarray(t) for t in (eps, last, gain, cross))
    info = lax.dynamic_index_in_dim(jnp.asarray(table), device, 0, False)
    flux = lax.dynamic_index_in_dim(jnp.asarray(by_device), device, 0, False)

    first = chunks.bit_length() - 1
    row_groups = [[first]] + [[*range(b, min(b + 2, levels))] for b in range(first + 1, levels, 2)]
    col_groups = [[*range(b, min(b + 2, first))] for b in range(0, first, 2)]

    def add_up(value, groups, late=None):
        for group in groups:
            away = [1 << b for b in group]
            away += [sum(away)] if len(away) == 2 else []
            got = [lax.ppermute(value, BOTH, [(i, i ^ m) for i in range(strips)]) for m in away]
            if late is not None and group is groups[-1]:
                late, got = lax.optimization_barrier((late, got))
            value = value + got[0] + (got[1] + got[2]) if len(got) == 3 else value + got[0]
        return value, late

    def away(piece, d):
        return lax.ppermute(piece, "col", [(c, c ^ d) for c in range(chunks)])

    def exchange(pieces):
        return [pieces[0]] + [away(pieces[d], d) for d in range(1, chunks)]

    head, tail = edges(start_block, old_direction, intensity)
    above = lax.ppermute(tail, "row", [(i, i + 1) for i in range(row_count - 1)])
    below = lax.ppermute(head, "row", [(i + 1, i) for i in range(row_count - 1)])
    x_pieces = pack(info, start_block, intensity, chunks)
    x_pieces = exchange(fill(info, above, below, x_pieces, 0, True))
    p_pieces = pack(info, old_direction, None, chunks)
    p_own, *p_early, p_late = fill(info, above, below, p_pieces, fields, False)
    p_early = [away(piece, d) for d, piece in enumerate(p_early, 1)]
    p_late, x_pieces[1] = lax.optimization_barrier((p_late, x_pieces[1]))
    p_pieces = [p_own, *p_early, away(p_late, chunks - 1)]
    x_pieces, flux = lax.optimization_barrier((x_pieces, flux))
    w, deg = make_weights(info, x_pieces, depth, rows)
    graph_x, x, gram_x = apply_graph(("v",), True, 4 * fields, x_pieces, w, deg, info=info)
    gram_x, _ = add_up(gram_x, row_groups)
    gram_x, p_pieces = lax.optimization_barrier((gram_x, p_pieces))
    gram_x, _ = add_up(gram_x, col_groups)
    f, ends = residual_spectrum(gram_x, graph_x, x, deg, eps, last, high_t, low_t)

    gs = []
    groups = col_groups + row_groups
    for group in groups:
        level = group[0]
        found = {0: ends}
        for d in range(1, 1 << len(group)):
            place = (int(table[d << level, 0]) ^ int(table[0, 0])) >> level
            pairs = [(i, i ^ (d << level)) for i in range(strips)]
            found[place & (1 << len(group)) - 1] = lax.ppermute(ends, BOTH, pairs)
        is_last = group is groups[-1]
        *new, ends = merge(level, is_last, info, [found[e] for e in sorted(found)], gain, cross) + (
            (None,) if is_last else ()
        )
        gs += new
        if group is groups[-2]:
            p_pieces, ends = lax.optimization_barrier((p_pieces, ends))
    p, gram_p = apply_graph(("x", "v"), False, 2 * fields, p_pieces, w, deg, x, info=info)
    gs[-1], gram_p = lax.optimization_barrier((gs[-1], gram_p))

    h, head, tail, *h_pieces = row_inverse(info, gs, f, flux, eps, last, high, low, chunks)
    h_above = lax.ppermute(tail, BOTH, [(owner[s], owner[s + 1]) for s in range(strips - 1)])
    h_below = lax.ppermute(head, BOTH, [(owner[s + 1], owner[s]) for s in range(strips - 1)])
    h_own, *h_early, h_late = h_pieces
    (gram_inner,) = apply_graph(("x", "v", "p"), False, 0, (h,), w, deg, x, p, part="inner")
    h_early, h_above, h_below, gram_inner = lax.optimization_barrier(
        (h_early, h_above, h_below, gram_inner)
    )
    h_early = [away(piece, d) for d, piece in enumerate(h_early, 1)]
    (gram_outer,) = apply_graph(
        ("x", "v", "p"), False, 0, (h, h_above, h_below), w, deg, x, p, part="outer"
    )
    zero = jnp.zeros((fields, LANES), f32)
    gram = gram_inner + gram_outer + jnp.concatenate([gram_p[:fields], zero, gram_p[fields:]], 0)
    gram, _ = add_up(gram, row_groups)
    gram, h_early = lax.optimization_barrier((gram, h_early))
    gram, h_late = add_up(gram, col_groups, h_late)
    h_late = away(h_late, chunks - 1)
    ritz, coeffs = ritz_step(gram_x, gram, fields, rows * cols)
    given = info, coeffs, start_block, old_direction
    begun = combine(*given, [h_own, *h_early], chunks)
    new_block, new_direction = combine(*given, [h_late], chunks, chunks - 1, begun)
    return new_block, new_direction, ritz.reshape(fields)


def solution(mesh):
    return jax.shard_map(
        local,
        mesh=mesh,
        in_specs=(P("row", "col"), P(None, "row", "col"), P(None, "row", "col")),
        out_specs=(P(None, "row", "col"), P(None, "row", "col"), P()),
        check_vma=False,
    )
```

```python
import functools
import math

import jax
import jax.numpy as jnp
import numpy as np
from jax import lax
from jax.experimental import pallas as pl
from jax.experimental.pallas import tpu as pltpu
from jax.sharding import PartitionSpec as P

SWEEPS = 8
beta_value = 4.0
spatial_rate = 0.25
shift_numerator = 16.0
ritz_offset = 1.5
far = 1e4
highest = lax.Precision.HIGHEST
f32 = jnp.float32
bf16 = jnp.bfloat16
BOTH = ("row", "col")
LANES = 128
UNROLL = 4
VMEM = pl.BlockSpec(memory_space=pltpu.VMEM)
SMEM = pl.BlockSpec(memory_space=pltpu.SMEM)
OFFSETS = [(a, b) for a in range(-2, 3) for b in range(-2, 3)]


def params(*arrays, extra=4 * 2**20):
    total = extra
    for a in arrays:
        shape = (1, 1) + tuple(a.shape)
        padded = math.prod(shape[:-2]) * (-(-shape[-2] // 8) * 8) * (-(-shape[-1] // LANES) * LANES)
        total += padded * a.dtype.itemsize
    return pltpu.CompilerParams(vmem_limit_bytes=total)


def room(*shape):
    return jax.ShapeDtypeStruct(shape, f32)


def cost(flops, nbytes):
    return pl.CostEstimate(flops=int(flops), bytes_accessed=int(nbytes), transcendentals=0)


@functools.lru_cache(None)
def cosine_tables(length):
    k = np.arange(length)[:, None]
    n = np.arange(length)[None, :]
    table = np.cos(np.pi * ((2 * n + 1) * k % (4 * length)) / (2 * length)) * np.sqrt(2.0 / length)
    table[0] *= np.sqrt(0.5)
    high = table.astype(jnp.bfloat16)
    low = (table - high.astype(np.float64)).astype(jnp.bfloat16)
    return high, low


def ratio_sinh(a, b):
    return np.exp(a - b) * (1 - np.exp(-2 * a)) / (1 - np.exp(-2 * b))


@functools.lru_cache(None)
def row_tables(strips, depth, cols):
    rows = strips * depth
    lam = 4 * np.sin(np.pi * np.arange(cols) / (2 * cols)) ** 2
    mu = lam + shift_numerator / (rows * cols)
    excess = np.zeros((depth, cols))
    excess[0] = mu
    for r in range(1, depth):
        last = r == depth - 1
        prev = excess[r - 1]
        excess[r] = mu + prev / (1 + prev) - (1.0 if last else 0.0) + (0.0 if last else 0.0)
        if last:
            excess[r] = mu + prev / (1 + prev)
    eps = excess / (1 + excess)
    last_inv = 1.0 / (mu + eps[depth - 2])
    theta = 2 * np.arcsinh(np.sqrt(mu) / 2)
    levels = strips.bit_length() - 1
    gain, cross = [], []
    top = np.zeros((strips, levels, cols))
    bot = np.zeros((strips, levels, cols))
    for level in range(levels):
        m = 1 << level
        n = m * depth
        half = np.sinh(theta / 2)
        b = n * theta
        a = (n - 0.5) * theta
        end_end = np.exp(a - b) * (1 + np.exp(-2 * a)) / (1 - np.exp(-2 * b)) / (2 * half)
        first_last = 2 * np.cosh(theta / 2) * np.exp(-b) / (1 - np.exp(-2 * b)) / (2 * half)
        gain.append(1 / (1 + 2 * end_end))
        cross.append(first_last)
        rho = [ratio_sinh(p * depth * theta, b) for p in range(m + 1)]
        for s in range(strips):
            p = s % m
            if (s >> level) & 1:
                top[s, level], bot[s, level] = rho[m - p], rho[m - 1 - p]
            else:
                top[s, level], bot[s, level] = rho[p], rho[p + 1]
    cast = lambda x: np.asarray(x, np.float32)
    return cast(eps), cast(last_inv[None]), cast(gain), cast(cross), cast(top), cast(bot)


def split(x):
    high = x.astype(bf16)
    return high, (x - high.astype(f32)).astype(bf16)


def split3(x):
    high = x.astype(bf16)
    rest = x - high.astype(f32)
    middle = rest.astype(bf16)
    return high, middle, (rest - middle.astype(f32)).astype(bf16)


def image_rows(count, fields):
    return -(-count // fields)


def spread(info_ref, chunk_refs, target):
    width = chunk_refs[0].shape[-1]
    count = target.shape[0]
    for d, ref in enumerate(chunk_refs):
        start = pl.multiple_of(info_ref[1 + d] * width, width)
        if len(target.shape) == 3:
            target[:, :, pl.ds(start, width)] = ref[0:count]
        else:
            below = ref[ref.shape[0] - image_rows(count, ref.shape[1]) :]
            target[:, pl.ds(start, width)] = below.reshape(-1, width)[:count]


def edges_kernel(x_top, x_bot, p_top, p_bot, i_top, i_bot, head_ref, tail_ref):
    fields, _, _ = x_top.shape
    for out_ref, rows, refs in (
        (head_ref, slice(0, 2), (x_top, p_top, i_top)),
        (tail_ref, slice(6, 8), (x_bot, p_bot, i_bot)),
    ):
        for f in range(fields):
            out_ref[:, f, :] = refs[0][f, rows, :]
            out_ref[:, fields + f, :] = refs[1][f, rows, :]
        out_ref[:, 2 * fields, :] = refs[2][rows, :]


def edges(x, p, image):
    fields, height, width = x.shape
    bottom = height // 8 - 1
    top = pl.BlockSpec((fields, 8, width), lambda i: (0, 0, 0))
    bot = pl.BlockSpec((fields, 8, width), lambda i: (0, bottom, 0))
    image_top = pl.BlockSpec((8, width), lambda i: (0, 0))
    image_bot = pl.BlockSpec((8, width), lambda i: (bottom, 0))
    out = pl.BlockSpec((2, 2 * fields + 1, width), lambda i: (0, 0, 0))
    return pl.pallas_call(
        edges_kernel,
        grid=(1,),
        out_shape=(room(2, 2 * fields + 1, width),) * 2,
        in_specs=[top, bot, top, bot, image_top, image_bot],
        out_specs=(out, out),
        compiler_params=pltpu.CompilerParams(vmem_limit_bytes=56 * 2**20),
        cost_estimate=cost(0, 8 * 4 * fields * width * 4),
        name="edges",
    )(x, x, p, p, image, image)


def pack_kernel(chunks, depth, with_image, info_ref, x_ref, *refs):
    fields, height, width = x_ref.shape
    if with_image:
        image_ref, *pieces = refs
    else:
        pieces = refs
    for d in range(chunks):
        place = info_ref[1 + chunks + d]
        start = pl.multiple_of(place * depth, depth)
        before = pl.multiple_of(jnp.maximum(start - 8, 0), 8)
        after = pl.multiple_of(jnp.minimum(start + depth, height - 8), 8)
        piece = pieces[d]
        for f in range(fields):
            piece[2 : 2 + depth, f, :] = x_ref[f, pl.ds(start, depth), :]
            piece[0:2, f, :] = x_ref[f, pl.ds(before, 8), :][6:8]
            piece[2 + depth : 4 + depth, f, :] = x_ref[f, pl.ds(after, 8), :][0:2]
        if with_image:
            rows = jnp.concatenate(
                [
                    image_ref[pl.ds(before, 8), :][6:8],
                    image_ref[pl.ds(start, depth), :],
                    image_ref[pl.ds(after, 8), :][0:2],
                ],
                0,
            )
            count = depth + 4
            for r in range(0, count, fields):
                size = min(fields, count - r)
                piece[depth + 4 + r // fields, 0:size, :] = rows[r : r + size]
            rest = -count % fields
            if rest:
                piece[depth + 3 + image_rows(count, fields), fields - rest :, :] = jnp.zeros(
                    (rest, width), f32
                )


def pack(info, x, image, chunks):
    fields, height, width = x.shape
    depth = height // chunks
    count = depth + 4 + (image_rows(depth + 4, fields) if image is not None else 0)
    args = (x,) if image is None else (x, image)
    return pl.pallas_call(
        functools.partial(pack_kernel, chunks, depth, image is not None),
        out_shape=(room(count, fields, width),) * chunks,
        in_specs=[SMEM] + [VMEM] * len(args),
        out_specs=(VMEM,) * chunks,
        compiler_params=params(*args, *(room(count, fields, width),) * chunks),
        cost_estimate=cost(0, 8 * fields * height * width),
        name="pack",
    )(info, *args)


def fill_kernel(chunks, depth, first, with_image, info_ref, above_ref, below_ref, *refs):
    pieces = refs[chunks:]
    fields = pieces[0].shape[1]
    for d in range(chunks):
        place = info_ref[1 + chunks + d]
        piece = pieces[d]
        for which, rows_ref, row in ((0, above_ref, 0), (chunks - 1, below_ref, depth + 2)):

            @pl.when(place == which)
            def _(piece=piece, rows_ref=rows_ref, row=row):
                piece[row : row + 2] = rows_ref[:, first : first + fields, :]
                if with_image:
                    for i in range(2):
                        line = depth + 4 + (row + i) // fields
                        at = (row + i) % fields
                        image = rows_ref[i, 2 * fields : 2 * fields + 1, :]
                        piece[line, at : at + 1, :] = image


def fill(info, above, below, pieces, first, with_image):
    chunks = len(pieces)
    count, fields, width = pieces[0].shape
    depth = count - 4
    if with_image:
        depth = next(n for n in range(1, count) if n + 4 + image_rows(n + 4, fields) == count)
    return pl.pallas_call(
        functools.partial(fill_kernel, chunks, depth, first, with_image),
        out_shape=(room(count, fields, width),) * chunks,
        in_specs=[SMEM] + [VMEM] * (2 + chunks),
        out_specs=(VMEM,) * chunks,
        input_output_aliases={3 + d: d for d in range(chunks)},
        compiler_params=params(*pieces),
        cost_estimate=cost(0, 16 * fields * width),
        name="fill",
    )(info, above, below, *pieces)


def weights_kernel(chunks, total_rows, info_ref, *rest):
    chunk_refs, (w_ref, deg_ref, image_ref) = rest[:chunks], rest[chunks:]
    depth, cols = deg_ref.shape
    spread(info_ref, chunk_refs, image_ref)
    row = lax.broadcasted_iota(jnp.int32, (2, cols), 0) + info_ref[0] * depth
    image_ref[0:2, :] = jnp.where(row - 2 >= 0, image_ref[0:2, :], far)
    inside = row + depth < total_rows
    image_ref[2 + depth :, :] = jnp.where(inside, image_ref[2 + depth :, :], far)
    center = image_ref[2 : 2 + depth, :]
    col = lax.broadcasted_iota(jnp.int32, (depth, cols), 1)
    degree = jnp.zeros((depth, cols), f32)
    for b in range(-2, 3):
        moved = center
        if b:
            col_ok = (col - b >= 0) & (col - b < cols)
            moved = jnp.where(col_ok, pltpu.roll(center, b % cols, 1), -far)
        total = None
        for a in range(-2, 3):
            if a == 0 and b == 0:
                weight = jnp.ones((depth, cols), f32)
            else:
                contrast = moved - image_ref[2 + a : 2 + a + depth, :]
                weight = jnp.exp(-beta_value * contrast * contrast - spatial_rate * (a * a + b * b))
            w_ref[:, OFFSETS.index((a, b)), :] = weight
            total = weight if total is None else total + weight
        degree = degree + (pltpu.roll(total, (-b) % cols, 1) if b else total)
    deg_ref[...] = degree


def make_weights(info, pieces, depth, total_rows):
    cols = pieces[0].shape[2] * len(pieces)
    return pl.pallas_call(
        functools.partial(weights_kernel, len(pieces), total_rows),
        out_shape=(room(depth, 25, cols), room(depth, cols)),
        in_specs=[SMEM] + [VMEM] * len(pieces),
        out_specs=(VMEM,) * 2,
        scratch_shapes=[pltpu.VMEM((depth + 4, cols), f32)],
        compiler_params=params(*pieces, room(depth, 25, cols), extra=16 * 2**20),
        cost_estimate=cost(60 * depth * cols * 25, 25 * depth * cols * 4),
        name="weights",
    )(info, *pieces)


def graph_kernel(order, keep, lane_shift, chunks, part, *refs):
    if chunks:
        info_ref, chunk_refs, refs = refs[0], refs[1 : 1 + chunks], refs[1 + chunks :]
    elif part == "inner":
        v_ref, *refs = refs
    else:
        v_ref, top_ref, bot_ref, *refs = refs
    (w_ref, deg_ref), refs = refs[:2], refs[2:]
    others, refs = refs[: len(order) - 1], list(refs[len(order) - 1 :])
    g_ref = refs.pop(0) if keep else None
    own_ref = refs.pop(0) if chunks else None
    gram_ref, pad_ref, acc_ref, sum_ref = refs
    depth, cols = deg_ref.shape
    fields = sum_ref.shape[1]
    if chunks:
        spread(info_ref, chunk_refs, pad_ref)
    elif part == "outer":
        pad_ref[0:2] = top_ref[...]
        pad_ref[2:6] = v_ref[0:4]
        pad_ref[depth - 2 : depth + 2] = v_ref[depth - 4 : depth]
        pad_ref[2 + depth : 4 + depth] = bot_ref[...]
    parts = len(order)
    groups = fields // 8
    width = 256
    source_ref, shift = (v_ref, 2) if part == "inner" else (pad_ref, 0)

    def one_row(r, acc):
        for c in range(cols // width):
            lanes = slice(c * width, (c + 1) * width)
            values = [
                source_ref[r + a - shift, :, lanes].reshape(groups, 8, width) for a in range(5)
            ]
            for b in range(-2, 3):
                total = None
                for a in range(-2, 3):
                    value = values[a + 2]
                    if a or b:
                        o = OFFSETS.index((a, b))
                        value = w_ref[r, o : o + 1, lanes][None] * value
                    total = value if total is None else total + value
                sum_ref[b + 2, :, lanes] = total.reshape(fields, width)
        result = sum_ref[2]
        for b in (-2, -1, 1, 2):
            result = result + pltpu.roll(sum_ref[b + 2], (-b) % cols, 1)
        if keep:
            g_ref[r] = result
        own = source_ref[r + 2 - shift]
        if chunks:
            own_ref[r] = own
        weighted = deg_ref[pl.ds(r, 1), :] * own
        left, position = [], 0
        for which in order:
            if which == "v":
                left.append(split(own))
            else:
                left.append(split(others[position][r]))
                position += 1
        left = jnp.concatenate([p[0] for p in left] + [p[1] for p in left], 0)
        graph_pair, degree_pair = split(result), split(weighted)
        right = jnp.concatenate(
            [graph_pair[0], degree_pair[0], graph_pair[1], degree_pair[1]], 0
        )
        return acc + lax.dot_general(
            left, right, (((1,), (1,)), ((), ())), preferred_element_type=f32
        )

    start = jnp.zeros((2 * parts * fields, 4 * fields), f32)
    if part == "outer":
        acc = start
        for r in (0, 1, depth - 2, depth - 1):
            acc = one_row(r, acc)
    else:
        skip = 2 if part == "inner" else 0
        turns = math.gcd(depth - 2 * skip, 2 * UNROLL)
        acc = lax.fori_loop(skip, depth - skip, one_row, start, unroll=turns)
    half = parts * fields
    acc_ref[...] = jnp.zeros(acc_ref.shape, f32)
    acc_ref[:, 0 : 4 * fields] = acc[:half] + acc[half:]
    both = acc_ref[...]
    both = both + pltpu.roll(both, LANES - 2 * fields, 1)
    lane = lax.broadcasted_iota(jnp.int32, both.shape, 1)
    both = jnp.where(lane < 2 * fields, both, 0.0)
    if lane_shift:
        both = pltpu.roll(both, lane_shift, 1)
    gram_ref[...] = both


def apply_graph(order, keep, lane_shift, fields_in, w, deg, *others, info=None, part="all"):
    depth, cols = deg.shape
    fields = fields_in[0].shape[1]
    parts = len(order)
    chunks = len(fields_in) if info is not None else 0
    out_shape = [room(depth, fields, cols)] * (int(keep) + int(chunks > 0))
    out_shape += [room(parts * fields, LANES)]
    args = ((info,) if chunks else ()) + tuple(fields_in) + (w, deg) + others
    return pl.pallas_call(
        functools.partial(graph_kernel, order, keep, lane_shift, chunks, part),
        out_shape=tuple(out_shape),
        in_specs=[SMEM] * int(chunks > 0) + [VMEM] * (len(args) - int(chunks > 0)),
        out_specs=(VMEM,) * len(out_shape),
        scratch_shapes=[
            pltpu.VMEM((8 if part == "inner" else depth + 4, fields, cols), f32),
            pltpu.VMEM((parts * fields, LANES), f32),
            pltpu.VMEM((5, fields, cols), f32),
        ],
        compiler_params=params(w, deg, *fields_in, *others, *out_shape, room(depth + 9, fields, cols)),
        cost_estimate=cost(50 * fields * depth * cols * 4, 4 * cols * depth * (25 + 3 * fields)),
        name="graph_" + "".join(order) + "_" + part,
    )(*args)


def solve_rayleigh(affinity, mass):
    fields = mass.shape[0]
    row = lax.broadcasted_iota(jnp.int32, (fields, fields), 0)
    for k in range(fields):
        inverse = 1.0 / mass[k : k + 1, k : k + 1]
        column = mass[:, k : k + 1]
        mass_row = mass[k : k + 1, :] * inverse
        affinity_row = affinity[k : k + 1, :] * inverse
        affinity = jnp.where(row == k, affinity_row, affinity - column * affinity_row)
        mass = jnp.where(row == k, mass_row, mass - column * mass_row)
    return affinity


def residual_kernel(gram_ref, g_ref, x_ref, deg_ref, eps_ref, last_ref, high_ref, low_ref, f_ref, ends_ref):
    depth, fields, cols = x_ref.shape
    gram = gram_ref[...]
    affinity = pltpu.roll(gram, LANES - 4 * fields, 1)[:, :fields]
    mass = pltpu.roll(gram, LANES - 5 * fields, 1)[:, :fields]
    ray = split3(solve_rayleigh(affinity, mass).T)
    left = jnp.concatenate([ray[i] for i in (0, 0, 0, 1, 1, 2)], 1)
    block = math.gcd(depth, 16)
    dot = functools.partial(jnp.dot, preferred_element_type=f32)

    def one_block(i, _):
        start = pl.multiple_of(i * block, block)
        rows = []
        for r in range(block):
            piece = split3(x_ref[start + r] * deg_ref[pl.ds(start + r, 1), :])
            right = jnp.concatenate([piece[i] for i in (0, 1, 2, 0, 1, 0)], 0)
            rows.append(g_ref[start + r] - dot(left, right))
        high, low = split(jnp.concatenate(rows, 0))
        result = dot(high, high_ref[...]) + dot(high, low_ref[...]) + dot(low, high_ref[...])
        f_ref[pl.ds(start, block)] = result.reshape(block, fields, cols)
        return 0

    lax.fori_loop(0, depth // block, one_block, 0)

    def sweep(i, carry):
        up, down = carry
        keep = eps_ref[pl.ds(jnp.maximum(i - 1, 0), 1), :]
        return f_ref[depth - 1 - i] + (up - keep * up), f_ref[i] + (down - keep * down)

    zero = jnp.zeros((fields, cols), f32)
    up, down = lax.fori_loop(0, depth, sweep, (zero, zero), unroll=UNROLL)
    last = last_ref[...]
    ends_ref[0] = up * last
    ends_ref[1] = down * last


def residual_spectrum(gram, g, x, deg, eps, last, high, low):
    depth, fields, cols = x.shape
    out_shape = (room(depth, fields, cols), room(2, fields, cols))
    return pl.pallas_call(
        residual_kernel,
        out_shape=out_shape,
        in_specs=[VMEM] * 8,
        out_specs=(VMEM,) * 2,
        compiler_params=params(g, x, deg, high, low, *out_shape, extra=12 * 2**20),
        cost_estimate=cost(6 * depth * fields * cols * cols, 12 * depth * fields * cols),
        name="residual_spectrum",
    )(gram, g, x, deg, eps, last, high, low)


def merge_kernel(level, count, last, info_ref, gain_ref, cross_ref, *refs):
    groups, outs = [ref[...] for ref in refs[:count]], refs[count:]
    place = info_ref[0] >> level

    def join(own, other, step, keep):
        right = ((place >> step) & 1) == 1
        lower, upper = jnp.where(right, other, own), jnp.where(right, own, other)
        row = slice(level + step, level + step + 1)
        g = (lower[1] - upper[0]) * gain_ref[row, :]
        moved = g * cross_ref[row, :]
        return g, jnp.stack([lower[0] - moved, upper[1] + moved]) if keep else None

    g, ends = join(groups[0], groups[1], 0, count == 4 or not last)
    outs[0][...] = g
    if count == 4:
        _, others = join(groups[2], groups[3], 0, True)
        g, ends = join(ends, others, 1, not last)
        outs[1][...] = g
    if not last:
        outs[-1][...] = ends


def merge(level, last, info, groups, gain, cross):
    _, fields, cols = groups[0].shape
    count = len(groups)
    out_shape = (room(fields, cols),) * (count // 2) + (() if last else (room(2, fields, cols),))
    return pl.pallas_call(
        functools.partial(merge_kernel, level, count, last),
        out_shape=out_shape,
        in_specs=[SMEM] + [VMEM] * (2 + count),
        out_specs=(VMEM,) * len(out_shape),
        compiler_params=params(*groups, *out_shape),
        cost_estimate=cost(10 * fields * cols, 28 * fields * cols),
        name="merge",
    )(info, gain, cross, *groups)


def inverse_kernel(levels, chunks, info_ref, *refs):
    g_refs = refs[:levels]
    f_ref, flux_ref, eps_ref, last_ref, high_ref, low_ref = refs[levels : levels + 6]
    out_ref, head_ref, tail_ref, *piece_refs, u_ref = refs[levels + 6 :]
    depth, fields, cols = f_ref.shape
    width = cols // chunks
    flux_top = jnp.zeros((fields, cols), f32)
    flux_bot = jnp.zeros((fields, cols), f32)
    for level in range(levels):
        g = g_refs[level][...]
        flux_top = flux_top + g * flux_ref[level : level + 1, :]
        flux_bot = flux_bot - g * flux_ref[levels + level : levels + level + 1, :]

    value = f_ref[0] + flux_top
    u_ref[0] = value
    for r in range(1, depth):
        value = f_ref[r] + (value - eps_ref[r - 1 : r, :] * value)
        u_ref[r] = value
    value = (value + flux_bot) * last_ref[...]
    u_ref[depth - 1] = value
    for r in range(depth - 2, -1, -1):
        value = u_ref[r] + value
        value = value - eps_ref[r : r + 1, :] * value
        u_ref[r] = value
    block = math.gcd(depth, 16)

    def one_block(i, _):
        start = i * block
        high, low = split(u_ref[pl.ds(start, block)].reshape(block * fields, cols))
        result = jnp.dot(high, high_ref[...], preferred_element_type=f32)
        result += jnp.dot(high, low_ref[...], preferred_element_type=f32)
        result += jnp.dot(low, high_ref[...], preferred_element_type=f32)
        out_ref[pl.ds(start, block)] = result.reshape(block, fields, cols)
        for d in range(chunks):
            lane = pl.multiple_of(info_ref[1 + d] * width, width)
            piece_refs[d][pl.ds(start, block)] = out_ref[pl.ds(start, block), :, pl.ds(lane, width)]
        return 0

    lax.fori_loop(0, depth // block, one_block, 0)
    head_ref[...] = out_ref[0:2]
    tail_ref[...] = out_ref[depth - 2 : depth]


def row_inverse(info, gs, f, flux, eps, last, high, low, chunks):
    depth, fields, cols = f.shape
    out_shape = (room(depth, fields, cols),) + (room(2, fields, cols),) * 2
    out_shape += (room(depth, fields, cols // chunks),) * chunks
    return pl.pallas_call(
        functools.partial(inverse_kernel, len(gs), chunks),
        out_shape=out_shape,
        in_specs=[SMEM] + [VMEM] * (len(gs) + 6),
        out_specs=(VMEM,) * len(out_shape),
        scratch_shapes=[pltpu.VMEM((depth, fields, cols), f32)],
        compiler_params=params(*gs, f, high, low, *out_shape, f, extra=12 * 2**20),
        cost_estimate=cost(6 * depth * fields * cols * cols, 4 * cols * (2 * depth * fields + cols)),
        name="row_inverse",
    )(info, *gs, f, flux, eps, last, high, low)


def hdot(a, b, contract):
    return lax.dot_general(
        a, b, ((contract[0], contract[1]), ((), ())), precision=highest, preferred_element_type=f32
    )


def cholesky_apply(matrix, target):
    size = matrix.shape[0]
    step = 8
    mats = [matrix[i : i + step] for i in range(0, size, step)]
    tars = [target[i : i + step] for i in range(0, size, step)]
    local_row = lax.broadcasted_iota(jnp.int32, (step, 1), 0)
    for k in range(size):
        own, inner = divmod(k, step)
        pivot_row = mats[own][inner : inner + 1, :]
        target_row = tars[own][inner : inner + 1, :]
        inverse = 1.0 / pivot_row[:, k : k + 1]
        for i in range(own, size // step):
            factor = mats[i][:, k : k + 1] * inverse
            if i == own:
                factor = jnp.where(local_row > inner, factor, 0.0)
            mats[i] = mats[i] - factor * pivot_row
            tars[i] = tars[i] - factor * target_row
    matrix = jnp.concatenate(mats, 0)
    target = jnp.concatenate(tars, 0)
    row = lax.broadcasted_iota(jnp.int32, matrix.shape, 0)
    col = lax.broadcasted_iota(jnp.int32, matrix.shape, 1)
    pivots = jnp.sum(jnp.where(row == col, matrix, 0.0), 1, keepdims=True)
    return target * (1.0 / jnp.sqrt(pivots))


def ritz_kernel(fields, pixel_total, first_ref, second_ref, ritz_ref, coeff_ref):
    size = 3 * fields
    gram = second_ref[...]
    first = first_ref[...]
    row = lax.broadcasted_iota(jnp.int32, (LANES, size), 0)
    col = lax.broadcasted_iota(jnp.int32, (LANES, size), 1)
    place_a = jnp.zeros((LANES, size), jnp.bool_)
    place_b = jnp.zeros((LANES, size), jnp.bool_)
    for group, target in ((4, 0), (0, 1), (2, 2)):
        inside = (col >= target * fields) & (col < (target + 1) * fields)
        place_a = place_a | (inside & (row - group * fields == col - target * fields))
        place_b = place_b | (inside & (row - (group + 1) * fields == col - target * fields))
    place_a = place_a.astype(f32)
    place_b = place_b.astype(f32)
    srow = lax.broadcasted_iota(jnp.int32, (size, size), 0)
    scol = lax.broadcasted_iota(jnp.int32, (size, size), 1)
    same = srow // fields == scol // fields
    eye = (srow == scol).astype(f32)

    def assemble(place):
        part = hdot(gram, place, ((1,), (0,)))
        top = hdot(first, place, ((1,), (0,)))
        part = jnp.concatenate([part[:fields] + top, part[fields:]], 0)
        both = part + part.T
        return jnp.where(same, 0.5 * both, both)

    big_a = assemble(place_a)
    big_b = assemble(place_b)
    diagonal = big_b * eye
    scale_col = 1.0 / jnp.sqrt(jnp.sum(diagonal, 1, keepdims=True) + 1e-6)
    scale_row = 1.0 / jnp.sqrt(jnp.sum(diagonal, 0, keepdims=True) + 1e-6)
    norm_a = scale_col * big_a * scale_row
    norm_b = scale_col * big_b * scale_row
    inverse = cholesky_apply(norm_b, eye)
    reduced = hdot(hdot(inverse, norm_a, ((1,), (0,))), inverse, ((1,), (1,)))
    reduced = 0.5 * (reduced + reduced.T) + ritz_offset * eye
    power = hdot(reduced, reduced, ((1,), (0,)))
    power = hdot(power, power, ((1,), (0,)))
    images = power[:fields]
    basis = cholesky_apply(hdot(images, images, ((1,), (1,))), images)
    images = hdot(basis, power, ((1,), (0,)))
    basis = cholesky_apply(hdot(images, images, ((1,), (1,))), images)
    images = hdot(basis, reduced, ((1,), (0,)))
    ones = jnp.ones((8, size), f32)
    ritz_ref[...] = hdot(ones, basis * images, ((1,), (1,)))[0:1] - ritz_offset
    coeff_ref[...] = math.sqrt(pixel_total) * scale_col * hdot(inverse, basis, ((0,), (1,)))


def ritz_step(first, second, fields, pixel_total):
    return pl.pallas_call(
        functools.partial(ritz_kernel, fields, pixel_total),
        out_shape=(
            room(1, fields),
            room(3 * fields, fields),
        ),
        in_specs=[pl.BlockSpec(memory_space=pltpu.VMEM)] * 2,
        out_specs=(pl.BlockSpec(memory_space=pltpu.VMEM),) * 2,
        compiler_params=params(),
        cost_estimate=cost(1 << 25, 1 << 16),
        name="ritz",
    )(first, second)


def combine_kernel(count, begun, info_ref, coeff_ref, x_ref, p_ref, *refs):
    pieces, refs = refs[:count], refs[count:]
    if begun:
        _, _, high_ref, low_ref, block_ref, direction_ref, h_ref = refs
    else:
        block_ref, direction_ref, high_ref, low_ref, h_ref = refs
    fields = x_ref.shape[0]
    width = x_ref.shape[2]
    group = 8 * fields

    @pl.when((pl.program_id(0) == 0) & (not begun))
    def _():
        r = lax.broadcasted_iota(jnp.int32, (group, fields), 0)
        c = lax.broadcasted_iota(jnp.int32, (group, fields), 1)
        rows_of = (r // 8 == c).astype(f32)
        f = lax.broadcasted_iota(jnp.int32, (fields, group), 0)
        q = lax.broadcasted_iota(jnp.int32, (fields, group), 1)
        row = lax.broadcasted_iota(jnp.int32, (group, group), 0)
        col = lax.broadcasted_iota(jnp.int32, (group, group), 1)
        coeffs = coeff_ref[...]
        for part in range(3):
            own = coeffs[part * fields : (part + 1) * fields, :].T
            if part == 1:
                cols_of, same = q % fields == f, row % 8 == col // fields
            else:
                cols_of, same = q // 8 == f, row % 8 == col % 8
            wide = hdot(own, cols_of.astype(f32), ((1,), (0,)))
            wide = jnp.where(same, hdot(rows_of, wide, ((1,), (0,))), 0.0)
            lanes = slice(part * group, (part + 1) * group)
            high_ref[:, lanes], low_ref[:, lanes] = split(wide)

    for d in range(count):

        @pl.when(pl.program_id(0) == d)
        def _(d=d):
            h_ref[...] = pieces[d][...]

    dot = functools.partial(jnp.dot, preferred_element_type=f32)
    for t in range(x_ref.shape[1] // 8):
        rows = slice(8 * t, 8 * t + 8)
        x = split(x_ref[:, rows, :].reshape(group, width))
        h = split(h_ref[rows].reshape(group, width))
        p = split(p_ref[:, rows, :].reshape(group, width))
        hp = [jnp.concatenate([h[i], p[i]], 0) for i in range(2)]
        x_high, x_low = high_ref[:, :group], low_ref[:, :group]
        hp_high, hp_low = high_ref[:, group:], low_ref[:, group:]
        direction = dot(hp_high, hp[0]) + dot(hp_low, hp[0]) + dot(hp_high, hp[1])
        x_left = jnp.concatenate([x_high, x_high, x_low], 1)
        block = direction + dot(x_left, jnp.concatenate([x[0], x[1], x[0]], 0))
        block_ref[:, rows, :] = block.reshape(fields, 8, width)
        direction_ref[:, rows, :] = direction.reshape(fields, 8, width)


def combine(info, coeffs, x, p, pieces, chunks, first=0, begun=()):
    fields, rows, width = x.shape
    count = len(pieces)
    depth = rows // chunks
    spec = pl.BlockSpec((fields, depth, width), lambda i, s: (0, s[1 + chunks + first + i], 0))
    whole = pl.BlockSpec((depth, fields, width), lambda i, s: (0, 0, 0))
    left = pl.BlockSpec(memory_space=pl.ANY)
    wide = (8 * fields, 24 * fields)
    same = pl.BlockSpec(wide, lambda i, s: (0, 0))
    again = (jax.ShapeDtypeStruct(wide, bf16),) * 2
    return pl.pallas_call(
        functools.partial(combine_kernel, count, bool(begun)),
        out_shape=(room(fields, rows, width),) * 2 + (() if begun else again),
        grid_spec=pltpu.PrefetchScalarGridSpec(
            num_scalar_prefetch=1,
            grid=(count,),
            in_specs=[pl.BlockSpec(coeffs.shape, lambda i, s: (0, 0)), spec, spec]
            + [whole] * count
            + ([left, left, same, same] if begun else []),
            out_specs=(spec, spec) + (() if begun else (same, same)),
            scratch_shapes=[pltpu.VMEM((depth, fields, width), f32)],
        ),
        input_output_aliases={4 + count + i: i for i in range(2)} if begun else {},
        compiler_params=params(room(16 * depth, fields, width)),
        cost_estimate=cost(50 * count * depth * fields * width, 20 * count * depth * fields * width),
        name="combine",
    )(info, coeffs, x, p, *pieces, *begun)


def ring_order(count):
    half = count // 2
    return [*range(half), *reversed(range(half, count))] if count > 1 else [0]


@functools.lru_cache(None)
def device_table(strips, chunks):
    order = ring_order(chunks)
    place = [order.index(c) for c in range(chunks)]
    table = []
    for device in range(strips):
        row, col = divmod(device, chunks)
        others = [col ^ d for d in range(chunks)]
        table.append([row * chunks + place[col], *others, *[place[c] for c in others]])
    return np.asarray(table, np.int32)


def local(intensity, start_block, old_direction):
    fields, height, width = start_block.shape
    chunks = lax.axis_size("col")
    row_count = lax.axis_size("row")
    strips = row_count * chunks
    depth = height // chunks
    rows, cols = strips * depth, chunks * width
    device = lax.axis_index("row") * chunks + lax.axis_index("col")
    levels = strips.bit_length() - 1
    order = ring_order(chunks)
    owner = [(s // chunks) * chunks + order[s % chunks] for s in range(strips)]

    table = device_table(strips, chunks)
    eps, last, gain, cross, top_all, bot_all = row_tables(strips, depth, cols)
    by_device = np.concatenate([top_all[table[:, 0]], bot_all[table[:, 0]]], 1)
    high, low = (jnp.asarray(t) for t in cosine_tables(cols))
    high_t, low_t = (jnp.asarray(t.T.copy()) for t in cosine_tables(cols))
    eps, last, gain, cross = (jnp.asarray(t) for t in (eps, last, gain, cross))
    info = lax.dynamic_index_in_dim(jnp.asarray(table), device, 0, False)
    flux = lax.dynamic_index_in_dim(jnp.asarray(by_device), device, 0, False)

    first = chunks.bit_length() - 1
    row_groups = [[first]] + [[*range(b, min(b + 2, levels))] for b in range(first + 1, levels, 2)]
    col_groups = [[*range(b, min(b + 2, first))] for b in range(0, first, 2)]

    def add_up(value, groups, late=None):
        for group in groups:
            away = [1 << b for b in group]
            away += [sum(away)] if len(away) == 2 else []
            got = [lax.ppermute(value, BOTH, [(i, i ^ m) for i in range(strips)]) for m in away]
            if late is not None and group is groups[-1]:
                late, got = lax.optimization_barrier((late, got))
            value = value + got[0] + (got[1] + got[2]) if len(got) == 3 else value + got[0]
        return value, late

    def away(piece, d):
        return lax.ppermute(piece, "col", [(c, c ^ d) for c in range(chunks)])

    def exchange(pieces):
        return [pieces[0]] + [away(pieces[d], d) for d in range(1, chunks)]

    head, tail = edges(start_block, old_direction, intensity)
    above = lax.ppermute(tail, "row", [(i, i + 1) for i in range(row_count - 1)])
    below = lax.ppermute(head, "row", [(i + 1, i) for i in range(row_count - 1)])
    x_pieces = pack(info, start_block, intensity, chunks)
    x_pieces = exchange(fill(info, above, below, x_pieces, 0, True))
    p_pieces = pack(info, old_direction, None, chunks)
    p_own, *p_early, p_late = fill(info, above, below, p_pieces, fields, False)
    p_early = [away(piece, d) for d, piece in enumerate(p_early, 1)]
    p_late, x_pieces[1] = lax.optimization_barrier((p_late, x_pieces[1]))
    p_pieces = [p_own, *p_early, away(p_late, chunks - 1)]
    x_pieces, flux = lax.optimization_barrier((x_pieces, flux))
    w, deg = make_weights(info, x_pieces, depth, rows)
    graph_x, x, gram_x = apply_graph(("v",), True, 4 * fields, x_pieces, w, deg, info=info)
    gram_x, _ = add_up(gram_x, row_groups)
    gram_x, p_pieces = lax.optimization_barrier((gram_x, p_pieces))
    gram_x, _ = add_up(gram_x, col_groups)
    f, ends = residual_spectrum(gram_x, graph_x, x, deg, eps, last, high_t, low_t)

    gs = []
    groups = col_groups + row_groups
    for group in groups:
        level = group[0]
        found = {0: ends}
        for d in range(1, 1 << len(group)):
            place = (int(table[d << level, 0]) ^ int(table[0, 0])) >> level
            pairs = [(i, i ^ (d << level)) for i in range(strips)]
            found[place & (1 << len(group)) - 1] = lax.ppermute(ends, BOTH, pairs)
        is_last = group is groups[-1]
        *new, ends = merge(level, is_last, info, [found[e] for e in sorted(found)], gain, cross) + (
            (None,) if is_last else ()
        )
        gs += new
        if group is groups[-2]:
            p_pieces, ends = lax.optimization_barrier((p_pieces, ends))
    p, gram_p = apply_graph(("x", "v"), False, 2 * fields, p_pieces, w, deg, x, info=info)
    gs[-1], gram_p = lax.optimization_barrier((gs[-1], gram_p))

    h, head, tail, *h_pieces = row_inverse(info, gs, f, flux, eps, last, high, low, chunks)
    h_above = lax.ppermute(tail, BOTH, [(owner[s], owner[s + 1]) for s in range(strips - 1)])
    h_below = lax.ppermute(head, BOTH, [(owner[s + 1], owner[s]) for s in range(strips - 1)])
    h_own, *h_early, h_late = h_pieces
    (gram_inner,) = apply_graph(("x", "v", "p"), False, 0, (h,), w, deg, x, p, part="inner")
    h_early, h_above, h_below, gram_inner = lax.optimization_barrier(
        (h_early, h_above, h_below, gram_inner)
    )
    h_early = [away(piece, d) for d, piece in enumerate(h_early, 1)]
    (gram_outer,) = apply_graph(
        ("x", "v", "p"), False, 0, (h, h_above, h_below), w, deg, x, p, part="outer"
    )
    zero = jnp.zeros((fields, LANES), f32)
    gram = gram_inner + gram_outer + jnp.concatenate([gram_p[:fields], zero, gram_p[fields:]], 0)
    gram, _ = add_up(gram, row_groups)
    gram, h_early = lax.optimization_barrier((gram, h_early))
    gram, h_late = add_up(gram, col_groups, h_late)
    h_late = away(h_late, chunks - 1)
    ritz, coeffs = ritz_step(gram_x, gram, fields, rows * cols)
    given = info, coeffs, start_block, old_direction
    begun = combine(*given, [h_own, *h_early], chunks)
    new_block, new_direction = combine(*given, [h_late], chunks, chunks - 1, begun)
    return new_block, new_direction, ritz.reshape(fields)


def solution(mesh):
    return jax.shard_map(
        local,
        mesh=mesh,
        in_specs=(P("row", "col"), P(None, "row", "col"), P(None, "row", "col")),
        out_specs=(P(None, "row", "col"), P(None, "row", "col"), P()),
        check_vma=False,
    )
```
